32 devices in a mesh: shard: 2 (over x), ctx: 4 (over z), tp: 4 (over y, core).
Axes of the slice: x: 2, y: 2, z: 4, core: 2. Of those that a mesh axis runs over, the one named last changes fastest.
Arguments:
- hidden_in: bfloat16 [4, 2048, 768], P('shard', 'ctx'), may hold values from -6 to 6
- segment_ids: int32 [4, 2048], P('shard'), may hold values from 0 to 7, never falling along the last dimension, each value on 1 to 1024 neighbouring positions
- qkv_weight: float32 [768, 3, 768], P('shard', None, 'tp'), may hold values from -0.21875 to 0.21875
- qv_bias: float32 [2, 768], P(None, 'tp'), may hold values from -3 to 3
- out_weight: float32 [768, 768], P('tp', 'shard'), may hold values from -1.75 to 1.75
- out_bias: float32 [768], P('shard'), may hold values from -3 to 3
- first_gain: float32 [768], P('shard'), may hold values from 0.5 to 1.5
- first_shift: float32 [768], P('shard'), may hold values from -3 to 3
- inner_weight: float32 [768, 3072], P('shard', 'tp'), may hold values from -0.21875 to 0.21875
- inner_bias: float32 [3072], P('tp'), may hold values from -3 to 3
- outer_weight: float32 [3072, 768], P('tp', 'shard'), may hold values from -0.109375 to 0.109375
- outer_bias: float32 [768], P('shard'), may hold values from -3 to 3
- second_gain: float32 [768], P('shard'), may hold values from 0.5 to 1.5
- second_shift: float32 [768], P('shard'), may hold values from -3 to 3
- cotangent: bfloat16 [4, 2048, 768], P('shard', 'ctx'), may hold values from -6 to 6
Outputs:
- output: bfloat16 [4, 2048, 768], P('shard', 'ctx')
- grad_hidden: bfloat16 [4, 2048, 768], P('shard', 'ctx')
- grad_qkv_weight: float32 [768, 3, 768], P('shard', None, 'tp')
- grad_qv_bias: float32 [2, 768], P(None, 'tp')
- grad_out_weight: float32 [768, 768], P('tp', 'shard')
- grad_out_bias: float32 [768], P('shard')
- grad_first_gain: float32 [768], P('shard')
- grad_first_shift: float32 [768], P('shard')
- grad_inner_weight: float32 [768, 3072], P('shard', 'tp')
- grad_inner_bias: float32 [3072], P('tp')
- grad_outer_weight: float32 [3072, 768], P('tp', 'shard')
- grad_outer_bias: float32 [768], P('shard')
- grad_second_gain: float32 [768], P('shard')
- grad_second_shift: float32 [768], P('shard')
The draws below stay inside these ranges and needn't reach their ends.
Inputs may be any that keep to these rules, and one draw needn't show every extreme that they name: `segment_ids`: within a row ids never fall; each document has 1 to 1024 tokens and one has exactly 1024.
All inputs are finite; a program needn't handle non-finite values.
Results may differ from the reference program's by a relative error of at most 0.014.
The reference program's roundings to bfloat16 on the way count: a program that leaves them out, or rounds other values in their place, can miss the bound.
Values may be sent and summed in bfloat16 or wider, within the bound.
No kernel may reach another device: no remote copies, remote signals or barrier semaphores. Data moves between devices by JAX's collectives and lax.ppermute only.
A program may use at most 128 MiB of HBM per device.

```python
import math
import jax
import jax.numpy as jnp
import numpy as np
from jax import lax

D = 768
HEADS = 12
FF = 3072
HEAD_DIM = 64
SEQ = 2048
ROWS = 4


def levels(rng, extent, pieces, smallest, top_value):
    def one(position, blocks):
        heights = jax.random.uniform(jax.random.fold_in(jax.random.fold_in(rng, 6), position), (blocks,), jnp.float32, smallest / len(pieces), top_value / len(pieces))
        return jnp.repeat(jnp.exp(heights), extent[position] // blocks).reshape((-1,) + (1,) * (len(extent) - position - 1))

    level = one(*pieces[0])
    for cut in pieces[1:]:
        level = level * one(*cut)
    return level


def split_up(amount, total, bound, slope):
    weights = [(1 << 20) // math.isqrt(standing ** slope) + 1 for standing in range(2, amount + 1)]
    rest, holding = total - bound - (amount - 1), [1] * (amount - 1)
    while rest > 0:
        candidates = [i for i in range(amount - 1) if holding[i] < bound]
        mass, budget = sum([weights[i] for i in candidates]), rest
        for i in candidates:
            more = min(bound - holding[i], max(1, budget * weights[i] // mass), rest)
            holding[i] = holding[i] + more
            rest = rest - more
    return np.array([bound] + holding)


def uneven_parts(own_key, count, total, most, skew):
    if count == 2:
        one = jax.random.randint(own_key, (), max(1, total - most), min(most, total - 1) + 1)
        return jnp.stack([one, total - one])
    sizes = jnp.asarray(split_up(count, total, most, skew), jnp.int32)
    pairs = (count - 1) // 2
    giver, taker = sizes[1:1 + 2 * pairs:2], sizes[2:2 + 2 * pairs:2]
    margin = jnp.minimum(giver - 1, most - taker)
    moved = jax.random.randint(jax.random.fold_in(own_key, 1), (pairs,), 0, 1 << 20) % (margin + 1)
    sizes = sizes.at[1:1 + 2 * pairs:2].set(giver - moved).at[2:2 + 2 * pairs:2].set(taker + moved)
    return sizes[jax.random.permutation(jax.random.fold_in(own_key, 2), count)]


def bell_draw(key, shape, scale, reach, shards=(), dtype=jnp.bfloat16):
    level = levels(key, shape, shards, -0.22, 0.18) if shards else 1.0
    drawn = jax.random.normal(key, shape, jnp.float32) * scale * level
    return jnp.minimum(jnp.maximum(drawn, -reach), reach).astype(dtype)


def setup_inputs(seed: int = 0) -> dict:
    splits = jax.random.split(jax.random.key(seed), 16)
    hidden_in = bell_draw(splits[0], (ROWS, SEQ, D), 1.0, 6.0, ((0, 2), (1, 4)))
    segment_ids = jax.vmap(lambda own: jnp.searchsorted(jnp.cumsum(uneven_parts(own, 8, SEQ, SEQ // 2, 2)), jnp.arange(SEQ), side="right"))(jax.random.split(splits[1], ROWS)).reshape((ROWS, SEQ)).astype(jnp.int32)
    qkv_weight = bell_draw(splits[2], (D, 3, D), D ** -0.5, 0.21875, ((0, 2), (2, 4)), jnp.float32)
    qv_bias = bell_draw(splits[3], (2, D), 0.5, 3.0, ((1, 4),), jnp.float32)
    out_weight = bell_draw(splits[4], (D, D), (D // 64) ** -0.5, 1.75, ((0, 4), (1, 2)), jnp.float32)
    out_bias = bell_draw(splits[5], (D,), 0.5, 3.0, ((0, 2),), jnp.float32)
    first_gain = jnp.clip(0.5 + 1.0 * jax.random.uniform(splits[6], (D,), jnp.float32) ** levels(splits[6], (D,), ((0, 2),), -0.2, 0.2), 0.5, 1.5)
    first_shift = bell_draw(splits[7], (D,), 0.5, 3.0, ((0, 2),), jnp.float32)
    inner_weight = bell_draw(splits[8], (D, FF), D ** -0.5, 0.21875, ((0, 2), (1, 4)), jnp.float32)
    inner_bias = bell_draw(splits[9], (FF,), 0.5, 3.0, ((0, 4),), jnp.float32)
    outer_weight = bell_draw(splits[10], (FF, D), FF ** -0.5, 0.109375, ((0, 4), (1, 2)), jnp.float32)
    outer_bias = bell_draw(splits[11], (D,), 0.5, 3.0, ((0, 2),), jnp.float32)
    second_gain = jnp.clip(0.5 + 1.0 * jax.random.uniform(splits[12], (D,), jnp.float32) ** levels(splits[12], (D,), ((0, 2),), -0.2, 0.2), 0.5, 1.5)
    second_shift = bell_draw(splits[13], (D,), 0.5, 3.0, ((0, 2),), jnp.float32)
    cotangent = bell_draw(splits[14], (ROWS, SEQ, D), 1.0, 6.0, ((0, 2), (1, 4)))
    return dict(hidden_in=hidden_in, segment_ids=segment_ids, qkv_weight=qkv_weight, qv_bias=qv_bias, out_weight=out_weight, out_bias=out_bias, first_gain=first_gain, first_shift=first_shift, inner_weight=inner_weight, inner_bias=inner_bias, outer_weight=outer_weight, outer_bias=outer_bias, second_gain=second_gain, second_shift=second_shift, cotangent=cotangent)


EPSILON = 1e-12
NEGATIVE = -1e+30
HIGHEST = lax.Precision.HIGHEST

@jax.custom_vjp
def low(v):
    return lax.optimization_barrier(v.astype(jnp.bfloat16)).astype(jnp.float32)

@jax.custom_vjp
def low_back(v):
    return v

def low_keep(v):
    return (low(v), None)

def low_pass(kept, grad):
    return (grad,)

def back_keep(v):
    return (v, None)

def back_low(kept, grad):
    return (low(grad),)
low.defvjp(low_keep, low_pass)
low_back.defvjp(back_keep, back_low)

def layer_norm(summed, gain_vec, shift_vec):
    average = lax.optimization_barrier(jnp.mean(summed, -1, keepdims=True))
    centered = summed - average
    variance = lax.optimization_barrier(jnp.mean(centered * centered, -1, keepdims=True))
    return centered * lax.rsqrt(variance + EPSILON) * gain_vec + shift_vec

def row_forward(masters, tokens_row, seg_row):
    qkv_w, qv_b, out_w, out_b, gain_one, shift_one, inner_w, inner_b, outer_w, outer_b, gain_two, shift_two = masters
    qkv_w = low(qkv_w)
    out_w = low(out_w)
    out_b = low(out_b)
    gain_one = low(gain_one)
    shift_one = low(shift_one)
    inner_w = low(inner_w)
    outer_w = low(outer_w)
    outer_b = low(outer_b)
    gain_two = low(gain_two)
    shift_two = low(shift_two)
    projected = low_back(jnp.dot(tokens_row, qkv_w.reshape(D, 3 * D), precision=HIGHEST)).reshape(SEQ, 3, D)
    queries = low(projected[:, 0] + qv_b[0]).reshape(SEQ, HEADS, HEAD_DIM)
    key_rows = low(projected[:, 1]).reshape(SEQ, HEADS, HEAD_DIM)
    value_rows = low(projected[:, 2] + qv_b[1]).reshape(SEQ, HEADS, HEAD_DIM)
    block_rows = min(512, SEQ)
    blocks = SEQ // block_rows

    def attend_block(sliced):
        query_block, seg_block = sliced
        scores = low_back(jnp.einsum('ihd,jhd->hij', query_block, key_rows, precision=HIGHEST)) * HEAD_DIM ** (-0.5)
        scores = jnp.where(seg_block[None, :, None] == seg_row[None, None, :], scores, NEGATIVE)
        largest = lax.optimization_barrier(jnp.max(scores, -1, keepdims=True))
        weights_exp = jnp.exp(scores - largest)
        probability = low(weights_exp / lax.optimization_barrier(jnp.sum(weights_exp, -1, keepdims=True)))
        return jnp.einsum('hij,jhd->ihd', probability, value_rows, precision=HIGHEST)
    mixed = lax.map(jax.checkpoint(attend_block), (queries.reshape(blocks, block_rows, HEADS, HEAD_DIM), seg_row.reshape(blocks, block_rows)))
    mixed = low(low_back(mixed.reshape(SEQ, D)))
    first_sum = tokens_row + low_back(jnp.dot(mixed, out_w, precision=HIGHEST)) + out_b
    first_norm = layer_norm(first_sum, gain_one, shift_one)
    activation = low_back(jnp.dot(low(first_norm), inner_w, precision=HIGHEST)) + inner_b
    gelu_out = low(jax.nn.gelu(activation, approximate=False))
    second_sum = first_norm + low_back(jnp.dot(gelu_out, outer_w, precision=HIGHEST)) + outer_b
    return layer_norm(second_sum, gain_two, shift_two)

def reference(hidden_in, segment_ids, qkv_weight, qv_bias, out_weight, out_bias, first_gain, first_shift, inner_weight, inner_bias, outer_weight, outer_bias, second_gain, second_shift, cotangent):
    masters = (qkv_weight.astype(jnp.float32), qv_bias.astype(jnp.float32), out_weight.astype(jnp.float32), out_bias.astype(jnp.float32), first_gain.astype(jnp.float32), first_shift.astype(jnp.float32), inner_weight.astype(jnp.float32), inner_bias.astype(jnp.float32), outer_weight.astype(jnp.float32), outer_bias.astype(jnp.float32), second_gain.astype(jnp.float32), second_shift.astype(jnp.float32))

    def row_step(totals, sliced):
        tokens_row, seg_row, cotangent_row = sliced
        result, pullback = jax.vjp(lambda params, inputs: row_forward(params, inputs, seg_row), masters, tokens_row)
        grad_params, grad_row = pullback(cotangent_row)
        totals = jax.tree.map(lambda former, latter: former + latter, totals, grad_params)
        return (totals, (result.astype(jnp.bfloat16), grad_row.astype(jnp.bfloat16)))
    zeros = jax.tree.map(jnp.zeros_like, masters)
    totals, (outputs, grads) = lax.scan(row_step, zeros, (hidden_in.astype(jnp.float32), segment_ids, cotangent.astype(jnp.float32)))
    return (outputs, grads, totals[0], totals[1], totals[2], totals[3], totals[4], totals[5], totals[6], totals[7], totals[8], totals[9], totals[10], totals[11])
```

```python
import functools

import jax
import jax.numpy as jnp
from jax import lax
from jax.experimental import pallas as pl
from jax.experimental.pallas import tpu as pltpu
from jax.sharding import PartitionSpec as P

HEAD_DIM = 64
LONGEST = 1024
EPSILON = 1e-12
NEGATIVE = -1e30
BF = jnp.bfloat16
F32 = jnp.float32


def dot(a, b):
    return jnp.dot(a, b, preferred_element_type=F32)


def dot_tn(a, b):
    return lax.dot_general(a, b, (((0,), (0,)), ((), ())), preferred_element_type=F32)


def dot_nt(a, b):
    return lax.dot_general(a, b, (((1,), (1,)), ((), ())), preferred_element_type=F32)


def head_stack(tile, first, heads):
    row = lax.broadcasted_iota(jnp.int32, tile.shape, 0)
    parts = []
    for h in range(heads):
        start = first + h * HEAD_DIM
        parts.append(jnp.where((row >= start) & (row < start + HEAD_DIM), tile, jnp.zeros_like(tile)))
    return jnp.concatenate(parts, 1)


def head_rows(tile, first, heads):
    col = lax.broadcasted_iota(jnp.int32, tile.shape, 1)
    parts = []
    for h in range(heads):
        start = first + h * HEAD_DIM
        parts.append(jnp.where((col >= start) & (col < start + HEAD_DIM), tile, jnp.zeros_like(tile)))
    return jnp.concatenate(parts, 0)


def load_blocks(kv_refs, kvb, sem, tok):
    copies = [
        pltpu.make_async_copy(ref, kvb.at[pl.ds(i * tok, tok)], sem.at[i])
        for i, ref in enumerate(kv_refs)
    ]
    for copy in copies:
        copy.start()
    for copy in copies:
        copy.wait()


def forward_kernel(slots, heads, tq, tk, rng, q_ref, qseg_ref, kseg_ref, *rest):
    kv_refs = rest[:slots]
    o_ref, lse_ref, kvb, st, acc, sem = rest[slots:]
    tok = q_ref.shape[0]
    wide = q_ref.shape[1]
    load_blocks(kv_refs, kvb, sem, tok)
    vfirst = 2 * heads * HEAD_DIM - wide
    voff = wide - heads * HEAD_DIM
    for t in range(tok // tq):
        lo, hi = rng[3 * t], rng[3 * t + 1]
        qs = pl.multiple_of(rng[3 * t + 2], tq)
        q3t = head_stack(q_ref[pl.ds(qs, tq), :].T, 0, heads)
        qseg = qseg_ref[t]

        def scan_scores(j, top, q3t=q3t, qseg=qseg):
            at = pl.multiple_of(j * tk, tk)
            scores = dot(kvb[pl.ds(at, tk), :wide], q3t)
            scores = jnp.where(kseg_ref[pl.ds(at, tk), :] == qseg, scores, NEGATIVE)
            st[pl.ds(at, tk), :] = scores
            return jnp.maximum(top, jnp.max(scores.reshape(tk // 8, 8, heads * tq), 0))

        top8 = lax.fori_loop(lo, hi, scan_scores, jnp.full((8, heads * tq), NEGATIVE, F32))
        top = jnp.max(top8, 0, keepdims=True)
        acc[...] = jnp.zeros_like(acc)

        def scan_values(j, total, top=top):
            at = pl.multiple_of(j * tk, tk)
            weights = jnp.exp(st[pl.ds(at, tk), :] - top)
            acc[...] += dot_tn(kvb[pl.ds(at, tk), vfirst:], weights.astype(BF))
            return total + jnp.sum(weights.reshape(tk // 8, 8, heads * tq), 0)

        total8 = lax.fori_loop(lo, hi, scan_values, jnp.zeros((8, heads * tq), F32))
        total = jnp.sum(total8, 0, keepdims=True)
        lse_ref[t] = top + jnp.log(total)
        inv = 1.0 / total
        pieces = [jnp.zeros((voff, tq), F32)]
        for h in range(heads):
            rows = slice(voff + h * HEAD_DIM, voff + (h + 1) * HEAD_DIM)
            cols = slice(h * tq, (h + 1) * tq)
            pieces.append(acc[rows, cols] * inv[:, cols])
        o_ref[t * tq : (t + 1) * tq, :] = jnp.concatenate(pieces, 0).T.astype(BF)


def backward_kernel(slots, heads, tq, tk, rng, q_ref, qseg_ref, kseg_ref, o_ref, do_ref, lse_ref, *rest):
    kv_refs = rest[:slots]
    dq_ref, bias_ref = rest[slots : slots + 2]
    dkv_refs = rest[slots + 2 : 2 * slots + 2]
    kvb, dkv, dqt, sem = rest[2 * slots + 2 :]
    tok = q_ref.shape[0]
    wide = q_ref.shape[1]
    load_blocks(kv_refs, kvb, sem, tok)
    vfirst = 2 * heads * HEAD_DIM - wide
    voff = wide - heads * HEAD_DIM
    dkv[...] = jnp.zeros_like(dkv)
    bias = jnp.zeros((1, wide), F32)
    for t in range(tok // tq):
        lo, hi = rng[3 * t], rng[3 * t + 1]
        qs = pl.multiple_of(rng[3 * t + 2], tq)
        q = q_ref[pl.ds(qs, tq), :]
        do = do_ref[t * tq : (t + 1) * tq, :]
        o = o_ref[t * tq : (t + 1) * tq, :]
        q3t = head_stack(q.T, 0, heads)
        q3 = head_rows(q, 0, heads)
        do3t = head_stack(do.T, voff, heads)
        do3 = head_rows(do, voff, heads)
        prod = (do.astype(F32) * o.astype(F32)).T
        delta = jnp.concatenate(
            [
                jnp.sum(prod[voff + h * HEAD_DIM : voff + (h + 1) * HEAD_DIM], 0, keepdims=True)
                for h in range(heads)
            ],
            1,
        )
        qseg = qseg_ref[t]
        lse = lse_ref[t]
        dqt[...] = jnp.zeros_like(dqt)

        def scan_blocks(j, carry, q3t=q3t, q3=q3, do3t=do3t, do3=do3, delta=delta, qseg=qseg, lse=lse):
            at = pl.multiple_of(j * tk, tk)
            k = kvb[pl.ds(at, tk), :wide]
            v = kvb[pl.ds(at, tk), vfirst:]
            scores = dot(k, q3t)
            same = kseg_ref[pl.ds(at, tk), :] == qseg
            probs = jnp.where(same, jnp.exp(scores - lse), 0.0)
            grad = (probs * (dot(v, do3t) - delta)).astype(BF)
            dkv[pl.ds(at, tk), :wide] += dot(grad, q3)
            dkv[pl.ds(at, tk), vfirst:] += dot(probs.astype(BF), do3)
            dqt[...] += dot_tn(k, grad)
            return carry

        lax.fori_loop(lo, hi, scan_blocks, 0)
        pieces = []
        for h in range(heads):
            pieces.append(dqt[h * HEAD_DIM : (h + 1) * HEAD_DIM, h * tq : (h + 1) * tq])
        pieces.append(jnp.zeros((wide - heads * HEAD_DIM, tq), F32))
        dq = jnp.concatenate(pieces, 0).T * HEAD_DIM**-0.5
        bias = bias + jnp.sum(dq, 0, keepdims=True)
        dq_ref[pl.ds(qs, tq), :] = dq.astype(BF)
    bias_ref[...] = bias
    for i, ref in enumerate(dkv_refs):
        ref[...] = dkv[i * tok : (i + 1) * tok, :].astype(BF)


def make_attention(slots, heads, tok, wide, packed):
    tq = tok // 2
    tk = tq
    vmem = pl.BlockSpec(memory_space=pltpu.VMEM)
    smem = pl.BlockSpec(memory_space=pltpu.SMEM)
    hbm = pl.BlockSpec(memory_space=pl.ANY)
    pairs = 3 * heads * tok * slots * tok * wide
    params = pltpu.CompilerParams(vmem_limit_bytes=48 << 20)
    forward = pl.pallas_call(
        functools.partial(forward_kernel, slots, heads, tq, tk),
        out_shape=(
            jax.ShapeDtypeStruct((tok, wide), BF),
            jax.ShapeDtypeStruct((2, 1, heads * tq), F32),
        ),
        in_specs=[smem, vmem, vmem, vmem] + [hbm] * slots,
        out_specs=(vmem, vmem),
        scratch_shapes=[
            pltpu.VMEM((slots * tok, packed), BF),
            pltpu.VMEM((slots * tok, heads * tq), F32),
            pltpu.VMEM((wide, heads * tq), F32),
            pltpu.SemaphoreType.DMA((slots,)),
        ],
        cost_estimate=pl.CostEstimate(
            flops=pairs, transcendentals=heads * tok * slots * tok, bytes_accessed=slots * tok * packed * 2
        ),
        compiler_params=params,
        name="attend_forward",
    )
    backward = pl.pallas_call(
        functools.partial(backward_kernel, slots, heads, tq, tk),
        out_shape=(
            jax.ShapeDtypeStruct((tok, wide), BF),
            jax.ShapeDtypeStruct((1, wide), F32),
        )
        + tuple(jax.ShapeDtypeStruct((tok, packed), BF) for _ in range(slots)),
        in_specs=[smem, vmem, vmem, vmem, vmem, vmem, vmem] + [hbm] * slots,
        out_specs=(vmem,) * (slots + 2),
        scratch_shapes=[
            pltpu.VMEM((slots * tok, packed), BF),
            pltpu.VMEM((slots * tok, packed), F32),
            pltpu.VMEM((wide, heads * tq), F32),
            pltpu.SemaphoreType.DMA((slots,)),
        ],
        cost_estimate=pl.CostEstimate(
            flops=3 * pairs,
            transcendentals=heads * tok * slots * tok,
            bytes_accessed=slots * tok * packed * 4,
        ),
        compiler_params=params,
        name="attend_backward",
    )
    return forward, backward


def make_body(n_shard, n_ctx, n_tp):
    bits = [1 << i for i in range(n_tp.bit_length() - 1)]

    def exchange(value, axis, size, bit):
        return lax.ppermute(value, axis, [(i, i ^ bit) for i in range(size)])

    def shift(value, step):
        pairs = [(i, i + step) for i in range(n_ctx) if 0 <= i + step < n_ctx]
        return lax.ppermute(value, "ctx", pairs)

    def ctx_sum(value):
        if n_ctx & (n_ctx - 1):
            return lax.psum(value, "ctx")
        ci = lax.axis_index("ctx")
        steps = [1 << i for i in range(n_ctx.bit_length() - 1)]
        cur = value
        for bit in steps:
            half = cur.shape[0] // 2
            up = (ci // bit) % 2
            send = lax.dynamic_slice_in_dim(cur, (1 - up) * half, half, 0).astype(BF)
            keep = lax.dynamic_slice_in_dim(cur, up * half, half, 0)
            cur = keep + exchange(send, "ctx", n_ctx, bit).astype(F32)
        cur = cur.astype(BF)
        for bit in reversed(steps):
            other = exchange(cur, "ctx", n_ctx, bit)
            up = (ci // bit) % 2
            cur = jnp.where(
                up == 0, jnp.concatenate([cur, other], 0), jnp.concatenate([other, cur], 0)
            )
        return cur.astype(F32)

    def body(
        hidden_in,
        segment_ids,
        qkv_weight,
        qv_bias,
        out_weight,
        out_bias,
        first_gain,
        first_shift,
        inner_weight,
        inner_bias,
        outer_weight,
        outer_bias,
        second_gain,
        second_shift,
        cotangent,
    ):
        rows, tok, width = hidden_in.shape
        part = width // n_shard
        cols = qkv_weight.shape[2]
        heads = cols // HEAD_DIM
        units = inner_weight.shape[1]
        wide = -(-cols // 128) * 128
        pad = wide - cols
        packed = 2 * cols
        half = tok // 2
        si = lax.axis_index("shard")
        ci = lax.axis_index("ctx")
        core = lax.axis_index("tp") % 2
        reach = min(n_ctx - 1, 1 + (LONGEST - 2) // tok)
        slots = 2 * reach + 1
        attend_fwd, attend_bwd = make_attention(slots, heads, tok, wide, packed)

        def rolled(value, axis):
            if n_shard == 2:
                first = lax.slice_in_dim(value, 0, part, axis=axis)
                second = lax.slice_in_dim(value, part, width, axis=axis)
                return jnp.where(si == 0, value, jnp.concatenate([second, first], axis))
            return jnp.roll(value, -si * part, axis)

        def unrolled(value, axis):
            if n_shard == 2:
                return rolled(value, axis)
            return jnp.roll(value, si * part, axis)

        def gathered(own, axis):
            if n_shard == 2:
                return jnp.concatenate([own, exchange(own, "shard", 2, 1)], axis)
            return rolled(lax.all_gather(own, "shard", axis=axis, tiled=True), axis)

        def shard_sum(make, axis):
            if n_shard == 2:
                send = make(part, width).astype(BF)
                return make(0, part) + exchange(send, "shard", 2, 1).astype(F32)
            whole = unrolled(make(0, width), axis)
            return lax.psum_scatter(whole, "shard", scatter_dimension=axis, tiled=True)

        def own_half(value):
            return lax.dynamic_slice_in_dim(value, core * half, half, 0)

        def other_half(value):
            return lax.dynamic_slice_in_dim(value, (1 - core) * half, half, 0)

        def tp_sum(own, send):
            total = own + exchange(send.astype(BF), "tp", n_tp, 1).astype(F32)
            for bit in bits[1:]:
                total = total.astype(BF)
                total = total.astype(F32) + exchange(total, "tp", n_tp, bit).astype(F32)
            return total

        def both_halves(own):
            return jnp.concatenate([own, exchange(own, "tp", n_tp, 1)], 0)

        def in_order(pair):
            first, second = pair[:half], pair[half:]
            return jnp.where(core == 0, pair, jnp.concatenate([second, first], 0))

        qkv_low = qkv_weight.astype(BF)
        kv_own = qkv_low[:, 1:].reshape(part, packed)
        q_own = jnp.pad(qkv_low[:, 0], ((0, 0), (0, pad)))
        w_kv = gathered(kv_own, 0)
        w_q = gathered(q_own, 0)
        vec_own = jnp.stack(
            [out_bias, first_gain, first_shift, outer_bias, second_gain, second_shift]
        ).astype(BF)
        vec_own = jnp.pad(vec_own, ((0, 10), (0, 0)))
        wo_vec = gathered(jnp.concatenate([out_weight.astype(BF), vec_own], 0), 1)
        w_out = jnp.concatenate([jnp.zeros((pad, width), BF), wo_vec[:cols]], 0)
        vectors = wo_vec[cols : cols + 6].astype(F32)
        w_in = gathered(inner_weight.astype(BF), 0)
        w_outer = gathered(outer_weight.astype(BF), 1)

        x = rolled(hidden_in, 2)
        cot = rolled(cotangent, 2)

        before = jnp.full((rows, reach * tok), -1, jnp.int32)
        after = jnp.full((rows, reach * tok), 1 << 20, jnp.int32)
        padded = jnp.concatenate([before, segment_ids, after], 1)
        key_seg = lax.dynamic_slice_in_dim(padded, ci * tok, slots * tok, 1)
        q_seg = lax.dynamic_slice_in_dim(segment_ids, ci * tok, tok, 1)
        q_seg = q_seg.reshape(rows, 2, half)
        q_seg = jnp.where(core == 0, q_seg, q_seg[:, ::-1])
        low = jnp.sum(key_seg[:, None, :] < q_seg[:, :, :1], -1) // half
        high = (jnp.sum(key_seg[:, None, :] <= q_seg[:, :, -1:], -1) + half - 1) // half
        begin = jnp.broadcast_to(jnp.stack([core * half, (1 - core) * half])[None], (rows, 2))
        ranges = jnp.stack([low, high, begin], -1).reshape(rows, 6).astype(jnp.int32)
        q_seg3 = jnp.tile(q_seg[:, :, None, :], (1, 1, 1, heads))
        key_col = key_seg[:, :, None]

        v_bias = jnp.concatenate([jnp.zeros((cols,), F32), qv_bias[1]])
        q_bias = jnp.pad(qv_bias[0], (0, pad))

        def blocks_of(own):
            left, right = [own], [own]
            for _ in range(reach):
                left.append(shift(left[-1], 1))
                right.append(shift(right[-1], -1))
            return left[:0:-1] + [own] + right[1:]

        kv = [blocks_of((dot(x[r], w_kv) + v_bias).astype(BF)) for r in range(rows)]
        q = [
            ((dot(x[r], w_q) + q_bias).astype(BF) * jnp.asarray(HEAD_DIM**-0.5, BF))
            for r in range(rows)
        ]

        def normed(summed):
            average = jnp.mean(summed, -1, keepdims=True)
            centered = summed - average
            variance = jnp.mean(centered * centered, -1, keepdims=True)
            scale = lax.rsqrt(variance + EPSILON)
            return centered * scale, scale

        def norm_back(grad, gain, hat, scale):
            inner = grad * gain
            return scale * (
                inner
                - jnp.mean(inner, -1, keepdims=True)
                - hat * jnp.mean(inner * hat, -1, keepdims=True)
            )

        bo, g1, s1, bd, g2, s2 = [vectors[i] for i in range(6)]
        saved = []
        for r in range(rows):
            o, lse = attend_fwd(ranges[r], q[r], q_seg3[r], key_col[r], *kv[r])
            total = tp_sum(dot(o[:half], w_out), dot(o[half:], w_out))
            h1 = own_half(x[r]).astype(F32) + total + bo
            hat1, scale1 = normed(h1)
            y1 = hat1 * g1 + s1
            y1b = both_halves(y1.astype(BF))
            a = dot(y1b, w_in) + inner_bias
            cdf = 0.5 * (1.0 + lax.erf(a * (0.5**0.5)))
            u = (a * cdf).astype(BF)
            slope = (cdf + a * jnp.exp(-0.5 * a * a) * 0.3989422804014327).astype(BF)
            total = tp_sum(dot(u[:half], w_outer), dot(u[half:], w_outer))
            h2 = y1 + total + bd
            hat2, scale2 = normed(h2)
            saved.append((o, lse, hat1, scale1, y1b, u, slope, hat2, scale2))

        outputs = []
        d_vec = jnp.zeros((6, width), F32)
        d_bi = jnp.zeros((units,), F32)
        d_bq = jnp.zeros((wide,), F32)
        d_bv = jnp.zeros((cols,), F32)
        d2b, d1b, dab, dqs, dkvs, dh1s = [], [], [], [], [], []
        for r in range(rows):
            o, lse, hat1, scale1, y1b, u, slope, hat2, scale2 = saved[r]
            c = own_half(cot[r]).astype(F32)
            result = (hat2 * g2 + s2).astype(BF)
            outputs.append(in_order(both_halves(unrolled(result, 1))))
            dh2 = norm_back(c, g2, hat2, scale2)
            dh2b = both_halves(dh2.astype(BF))
            du = dot_nt(dh2b, w_outer)
            da = du * slope.astype(F32)
            d_bi = d_bi + jnp.sum(da, 0)
            da_low = da.astype(BF)
            total = tp_sum(dot_nt(da_low[:half], w_in), dot_nt(da_low[half:], w_in))
            dy1 = dh2 + total
            dh1 = norm_back(dy1, g1, hat1, scale1)
            dh1b = both_halves(dh1.astype(BF))
            d_vec = d_vec + jnp.stack(
                [
                    jnp.sum(dh1, 0),
                    jnp.sum(dy1 * hat1, 0),
                    jnp.sum(dy1, 0),
                    jnp.sum(dh2, 0),
                    jnp.sum(c * hat2, 0),
                    jnp.sum(c, 0),
                ]
            )
            do = dot_nt(dh1b, w_out).astype(BF)
            res = attend_bwd(ranges[r], q[r], q_seg3[r], key_col[r], o, do, lse, *kv[r])
            dq, bias = res[:2]
            parts = res[2:]
            d_bq = d_bq + bias[0]
            carry_right = carry_left = None
            for d in range(reach, 0, -1):
                right, left = parts[reach + d], parts[reach - d]
                if carry_right is not None:
                    right = (right.astype(F32) + carry_right.astype(F32)).astype(BF)
                    left = (left.astype(F32) + carry_left.astype(F32)).astype(BF)
                carry_right, carry_left = shift(right, 1), shift(left, -1)
            dkv = parts[reach].astype(F32)
            if carry_right is not None:
                dkv = dkv + carry_right.astype(F32) + carry_left.astype(F32)
            d_bv = d_bv + jnp.sum(dkv[:, cols:], 0)
            d2b.append(dh2b)
            d1b.append(dh1b)
            dab.append(da_low)
            dqs.append(dq)
            dkvs.append(dkv.astype(BF))
            dh1s.append(dh1)

        hidden_grads = []
        for r in range(rows):
            total = tp_sum(
                dot_nt(own_half(dqs[r]), w_q) + dot_nt(own_half(dkvs[r]), w_kv),
                dot_nt(other_half(dqs[r]), w_q) + dot_nt(other_half(dkvs[r]), w_kv),
            )
            grad = unrolled((dh1s[r] + total).astype(BF), 1)
            hidden_grads.append(in_order(both_halves(grad)))

        every = range(rows)

        def total_of(terms):
            return functools.reduce(lambda p, q: p + q, terms)

        g_outer = shard_sum(lambda a, b: total_of(dot_tn(saved[r][5], d2b[r][:, a:b]) for r in every), 1)
        g_in = shard_sum(lambda a, b: total_of(dot_tn(saved[r][4][:, a:b], dab[r]) for r in every), 0)
        g_out = shard_sum(
            lambda a, b: total_of(dot_tn(saved[r][0], d1b[r][:, a:b]) for r in every)[pad:], 1
        )
        g_q = shard_sum(lambda a, b: total_of(dot_tn(x[r][:, a:b], dqs[r]) for r in every)[:, :cols], 0)
        g_kv = shard_sum(lambda a, b: total_of(dot_tn(x[r][:, a:b], dkvs[r]) for r in every), 0)
        g_outer = ctx_sum(g_outer)
        g_in = ctx_sum(g_in)
        g_out = ctx_sum(g_out)
        g_q = ctx_sum(g_q)
        g_kv = ctx_sum(g_kv)
        grad_qkv = jnp.concatenate([g_q[:, None], g_kv.reshape(part, 2, cols)], 1)

        d_vec = d_vec + exchange(d_vec, "tp", n_tp, 1)
        small = jnp.concatenate([d_bi, d_bq[:cols], d_bv])
        if n_shard == 2:
            send = jnp.concatenate([d_vec[:, part:].reshape(-1), small])
            flat = jnp.concatenate([d_vec[:, :part].reshape(-1), small]) + exchange(send, "shard", 2, 1)
        else:
            vec = lax.psum_scatter(unrolled(d_vec, 1), "shard", scatter_dimension=1, tiled=True)
            flat = jnp.concatenate([vec.reshape(-1), lax.psum(small, "shard")])
        if n_ctx & (n_ctx - 1):
            flat = lax.psum(flat, "ctx")
        else:
            for bit in [1 << i for i in range(n_ctx.bit_length() - 1)]:
                flat = flat + exchange(flat, "ctx", n_ctx, bit)
        vec = flat[: 6 * part].reshape(6, part)
        small = flat[6 * part :]
        return (
            jnp.stack(outputs),
            jnp.stack(hidden_grads),
            grad_qkv,
            small[units:].reshape(2, cols),
            g_out,
            vec[0],
            vec[1],
            vec[2],
            g_in,
            small[:units],
            g_outer,
            vec[3],
            vec[4],
            vec[5],
        )

    return body


def solution(mesh):
    body = make_body(mesh.shape["shard"], mesh.shape["ctx"], mesh.shape["tp"])
    in_specs = (
        P("shard", "ctx", None),
        P("shard", None),
        P("shard", None, "tp"),
        P(None, "tp"),
        P("tp", "shard"),
        P("shard"),
        P("shard"),
        P("shard"),
        P("shard", "tp"),
        P("tp"),
        P("tp", "shard"),
        P("shard"),
        P("shard"),
        P("shard"),
        P("shard", "ctx", None),
    )
    out_specs = (
        P("shard", "ctx", None),
        P("shard", "ctx", None),
        P("shard", None, "tp"),
        P(None, "tp"),
        P("tp", "shard"),
        P("shard"),
        P("shard"),
        P("shard"),
        P("shard", "tp"),
        P("tp"),
        P("tp", "shard"),
        P("shard"),
        P("shard"),
        P("shard"),
    )
    return jax.shard_map(body, mesh=mesh, in_specs=in_specs, out_specs=out_specs, check_vma=False)
```

```python
import functools

import jax
import jax.numpy as jnp
from jax import lax
from jax.experimental import pallas as pl
from jax.experimental.pallas import tpu as pltpu
from jax.sharding import PartitionSpec as P

HEAD_DIM = 64
LONGEST = 1024
EPSILON = 1e-12
NEGATIVE = -1e30
BF = jnp.bfloat16
F32 = jnp.float32


def dot(a, b):
    return jnp.dot(a, b, preferred_element_type=F32)


def dot_tn(a, b):
    return lax.dot_general(a, b, (((0,), (0,)), ((), ())), preferred_element_type=F32)


def dot_nt(a, b):
    return lax.dot_general(a, b, (((1,), (1,)), ((), ())), preferred_element_type=F32)


def head_stack(tile, first, heads):
    row = lax.broadcasted_iota(jnp.int32, tile.shape, 0)
    parts = []
    for h in range(heads):
        start = first + h * HEAD_DIM
        parts.append(jnp.where((row >= start) & (row < start + HEAD_DIM), tile, jnp.zeros_like(tile)))
    return jnp.concatenate(parts, 1)


def head_rows(tile, first, heads):
    col = lax.broadcasted_iota(jnp.int32, tile.shape, 1)
    parts = []
    for h in range(heads):
        start = first + h * HEAD_DIM
        parts.append(jnp.where((col >= start) & (col < start + HEAD_DIM), tile, jnp.zeros_like(tile)))
    return jnp.concatenate(parts, 0)


def load_blocks(kv_refs, kvb, sem, tok, slot_of):
    copies = [
        pltpu.make_async_copy(ref, kvb.at[pl.ds(pl.multiple_of(slot_of(i) * tok, tok), tok)], sem.at[i])
        for i, ref in enumerate(kv_refs)
    ]
    for copy in copies:
        copy.start()
    for copy in copies:
        copy.wait()


def forward_kernel(slots, heads, tq, tk, rng, q_ref, qseg_ref, kseg_ref, *rest):
    kv_refs = rest[:slots]
    o_ref, lse_ref, kvb, st, acc, sem = rest[slots:]
    tok = q_ref.shape[0]
    wide = q_ref.shape[1]
    table = 3 * (tok // tq)
    load_blocks(kv_refs, kvb, sem, tok, lambda i: rng[table + i])
    vfirst = 2 * heads * HEAD_DIM - wide
    voff = wide - heads * HEAD_DIM
    for t in range(tok // tq):
        lo, hi = rng[3 * t], rng[3 * t + 1]
        qs = pl.multiple_of(rng[3 * t + 2], tq)
        q3t = head_stack(q_ref[pl.ds(qs, tq), :].T, 0, heads)
        qseg = qseg_ref[t]

        def scan_scores(j, top, q3t=q3t, qseg=qseg):
            at = pl.multiple_of(j * tk, tk)
            scores = dot(kvb[pl.ds(at, tk), :wide], q3t)
            scores = jnp.where(kseg_ref[pl.ds(at, tk), :] == qseg, scores, NEGATIVE)
            st[pl.ds(at, tk), :] = scores
            return jnp.maximum(top, jnp.max(scores.reshape(tk // 8, 8, heads * tq), 0))

        top8 = lax.fori_loop(lo, hi, scan_scores, jnp.full((8, heads * tq), NEGATIVE, F32))
        top = jnp.max(top8, 0, keepdims=True)
        acc[...] = jnp.zeros_like(acc)

        def scan_values(j, total, top=top):
            at = pl.multiple_of(j * tk, tk)
            weights = jnp.exp(st[pl.ds(at, tk), :] - top)
            acc[...] += dot_tn(kvb[pl.ds(at, tk), vfirst:], weights.astype(BF))
            return total + jnp.sum(weights.reshape(tk // 8, 8, heads * tq), 0)

        total8 = lax.fori_loop(lo, hi, scan_values, jnp.zeros((8, heads * tq), F32))
        total = jnp.sum(total8, 0, keepdims=True)
        lse_ref[t] = top + jnp.log(total)
        inv = 1.0 / total
        pieces = [jnp.zeros((voff, tq), F32)]
        for h in range(heads):
            rows = slice(voff + h * HEAD_DIM, voff + (h + 1) * HEAD_DIM)
            cols = slice(h * tq, (h + 1) * tq)
            pieces.append(acc[rows, cols] * inv[:, cols])
        o_ref[t * tq : (t + 1) * tq, :] = jnp.concatenate(pieces, 0).T.astype(BF)


def backward_kernel(slots, heads, tq, tk, rng, q_ref, qseg_ref, kseg_ref, o_ref, do_ref, lse_ref, *rest):
    kv_refs = rest[:slots]
    dq_ref, bias_ref = rest[slots : slots + 2]
    dkv_refs = rest[slots + 2 : 2 * slots + 2]
    kvb, dkv, dqt, sem = rest[2 * slots + 2 :]
    tok = q_ref.shape[0]
    wide = q_ref.shape[1]
    table = 3 * (tok // tq)
    load_blocks(kv_refs, kvb, sem, tok, lambda i: rng[table + i])
    vfirst = 2 * heads * HEAD_DIM - wide
    voff = wide - heads * HEAD_DIM
    dkv[...] = jnp.zeros_like(dkv)
    bias = jnp.zeros((1, wide), F32)
    for t in range(tok // tq):
        lo, hi = rng[3 * t], rng[3 * t + 1]
        qs = pl.multiple_of(rng[3 * t + 2], tq)
        q = q_ref[pl.ds(qs, tq), :]
        do = do_ref[t * tq : (t + 1) * tq, :]
        o = o_ref[t * tq : (t + 1) * tq, :]
        q3t = head_stack(q.T, 0, heads)
        q3 = head_rows(q, 0, heads)
        do3t = head_stack(do.T, voff, heads)
        do3 = head_rows(do, voff, heads)
        prod = (do.astype(F32) * o.astype(F32)).T
        delta = jnp.concatenate(
            [
                jnp.sum(prod[voff + h * HEAD_DIM : voff + (h + 1) * HEAD_DIM], 0, keepdims=True)
                for h in range(heads)
            ],
            1,
        )
        qseg = qseg_ref[t]
        lse = lse_ref[t]
        dqt[...] = jnp.zeros_like(dqt)

        def scan_blocks(j, carry, q3t=q3t, q3=q3, do3t=do3t, do3=do3, delta=delta, qseg=qseg, lse=lse):
            at = pl.multiple_of(j * tk, tk)
            k = kvb[pl.ds(at, tk), :wide]
            v = kvb[pl.ds(at, tk), vfirst:]
            scores = dot(k, q3t)
            same = kseg_ref[pl.ds(at, tk), :] == qseg
            probs = jnp.where(same, jnp.exp(scores - lse), 0.0)
            grad = (probs * (dot(v, do3t) - delta)).astype(BF)
            dkv[pl.ds(at, tk), :wide] += dot(grad, q3)
            dkv[pl.ds(at, tk), vfirst:] += dot(probs.astype(BF), do3)
            dqt[...] += dot_tn(k, grad)
            return carry

        lax.fori_loop(lo, hi, scan_blocks, 0)
        pieces = []
        for h in range(heads):
            pieces.append(dqt[h * HEAD_DIM : (h + 1) * HEAD_DIM, h * tq : (h + 1) * tq])
        pieces.append(jnp.zeros((wide - heads * HEAD_DIM, tq), F32))
        dq = jnp.concatenate(pieces, 0).T * HEAD_DIM**-0.5
        bias = bias + jnp.sum(dq, 0, keepdims=True)
        dq_ref[pl.ds(qs, tq), :] = dq.astype(BF)
    bias_ref[...] = bias
    for i, ref in enumerate(dkv_refs):
        ref[...] = dkv[pl.ds(pl.multiple_of(rng[table + i] * tok, tok), tok), :].astype(BF)


def make_attention(slots, heads, tok, wide, packed):
    tq = tok // 2
    tk = tq
    vmem = pl.BlockSpec(memory_space=pltpu.VMEM)
    smem = pl.BlockSpec(memory_space=pltpu.SMEM)
    hbm = pl.BlockSpec(memory_space=pl.ANY)
    pairs = 3 * heads * tok * slots * tok * wide
    params = pltpu.CompilerParams(vmem_limit_bytes=48 << 20)
    forward = pl.pallas_call(
        functools.partial(forward_kernel, slots, heads, tq, tk),
        out_shape=(
            jax.ShapeDtypeStruct((tok, wide), BF),
            jax.ShapeDtypeStruct((2, 1, heads * tq), F32),
        ),
        in_specs=[smem, vmem, vmem, vmem] + [hbm] * slots,
        out_specs=(vmem, vmem),
        scratch_shapes=[
            pltpu.VMEM((slots * tok, packed), BF),
            pltpu.VMEM((slots * tok, heads * tq), F32),
            pltpu.VMEM((wide, heads * tq), F32),
            pltpu.SemaphoreType.DMA((slots,)),
        ],
        cost_estimate=pl.CostEstimate(
            flops=pairs, transcendentals=heads * tok * slots * tok, bytes_accessed=slots * tok * packed * 2
        ),
        compiler_params=params,
        name="attend_forward",
    )
    backward = pl.pallas_call(
        functools.partial(backward_kernel, slots, heads, tq, tk),
        out_shape=(
            jax.ShapeDtypeStruct((tok, wide), BF),
            jax.ShapeDtypeStruct((1, wide), F32),
        )
        + tuple(jax.ShapeDtypeStruct((tok, packed), BF) for _ in range(slots)),
        in_specs=[smem, vmem, vmem, vmem, vmem, vmem, vmem] + [hbm] * slots,
        out_specs=(vmem,) * (slots + 2),
        scratch_shapes=[
            pltpu.VMEM((slots * tok, packed), BF),
            pltpu.VMEM((slots * tok, packed), F32),
            pltpu.VMEM((wide, heads * tq), F32),
            pltpu.SemaphoreType.DMA((slots,)),
        ],
        cost_estimate=pl.CostEstimate(
            flops=3 * pairs,
            transcendentals=heads * tok * slots * tok,
            bytes_accessed=slots * tok * packed * 4,
        ),
        compiler_params=params,
        name="attend_backward",
    )
    return forward, backward


def after(value, *others):
    return lax.optimization_barrier((value,) + others)[0]


def make_body(n_shard, n_ctx, n_tp):
    bits = [1 << i for i in range(n_tp.bit_length() - 1)]
    ctx_steps = [1 << i for i in range(n_ctx.bit_length() - 1)]
    ctx_whole = not n_ctx & (n_ctx - 1)

    def exchange(value, axis, size, bit):
        return lax.ppermute(value, axis, [(i, i ^ bit) for i in range(size) if i ^ bit < size])

    def even_swap(value):
        return exchange(value, "ctx", n_ctx, 1)

    def odd_swap(value):
        pairs = []
        for i in range(1, n_ctx - 1, 2):
            pairs += [(i, i + 1), (i + 1, i)]
        return lax.ppermute(value, "ctx", pairs)

    def swap(value, kind):
        return odd_swap(value) if kind else even_swap(value)

    def ctx_sum(value):
        if not ctx_whole:
            return lax.psum(value, "ctx")
        ci = lax.axis_index("ctx")
        cur = value
        for bit in ctx_steps:
            half = cur.shape[0] // 2
            up = (ci // bit) % 2
            send = lax.dynamic_slice_in_dim(cur, (1 - up) * half, half, 0).astype(BF)
            keep = lax.dynamic_slice_in_dim(cur, up * half, half, 0)
            cur = keep + exchange(send, "ctx", n_ctx, bit).astype(F32)
        cur = cur.astype(BF)
        for bit in reversed(ctx_steps):
            other = exchange(cur, "ctx", n_ctx, bit)
            up = (ci // bit) % 2
            cur = jnp.where(
                up == 0, jnp.concatenate([cur, other], 0), jnp.concatenate([other, cur], 0)
            )
        return cur.astype(F32)

    def body(
        hidden_in,
        segment_ids,
        qkv_weight,
        qv_bias,
        out_weight,
        out_bias,
        first_gain,
        first_shift,
        inner_weight,
        inner_bias,
        outer_weight,
        outer_bias,
        second_gain,
        second_shift,
        cotangent,
    ):
        rows, tok, width = hidden_in.shape
        part = width // n_shard
        cols = qkv_weight.shape[2]
        heads = cols // HEAD_DIM
        units = inner_weight.shape[1]
        wide = -(-cols // 128) * 128
        pad = wide - cols
        packed = 2 * cols
        half = tok // 2
        every = range(rows)
        si = lax.axis_index("shard")
        ci = lax.axis_index("ctx")
        core = lax.axis_index("tp") % 2
        reach = min(n_ctx - 1, 1 + (LONGEST - 2) // tok)
        slots = 2 * reach + 1
        attend_fwd, attend_bwd = make_attention(slots, heads, tok, wide, packed)

        def rolled(value, axis):
            if n_shard == 2:
                first = lax.slice_in_dim(value, 0, part, axis=axis)
                second = lax.slice_in_dim(value, part, width, axis=axis)
                return jnp.where(si == 0, value, jnp.concatenate([second, first], axis))
            return jnp.roll(value, -si * part, axis)

        def unrolled(value, axis):
            if n_shard == 2:
                return rolled(value, axis)
            return jnp.roll(value, si * part, axis)

        def gathered(own, axis):
            if n_shard == 2:
                return jnp.concatenate([own, exchange(own, "shard", 2, 1)], axis)
            return rolled(lax.all_gather(own, "shard", axis=axis, tiled=True), axis)

        def gathered_in_order(own):
            if n_shard == 2:
                other = exchange(own, "shard", 2, 1)
                return jnp.where(
                    si == 0, jnp.concatenate([own, other], 0), jnp.concatenate([other, own], 0)
                )
            return lax.all_gather(own, "shard", axis=0, tiled=True)

        def shard_sum(own, send, axis):
            if n_shard == 2:
                return own + exchange(send.astype(BF), "shard", 2, 1).astype(F32)
            whole = unrolled(jnp.concatenate([own, send], axis), axis)
            return lax.psum_scatter(whole, "shard", scatter_dimension=axis, tiled=True)

        def own_half(value):
            return lax.dynamic_slice_in_dim(value, core * half, half, 0)

        def other_half(value):
            return lax.dynamic_slice_in_dim(value, (1 - core) * half, half, 0)

        def core_sum(own, send):
            total = own + exchange(send.astype(BF), "tp", n_tp, 1).astype(F32)
            return total.astype(BF) if len(bits) > 1 else total

        def chip_sum(total):
            for bit in bits[1:]:
                total = total.astype(BF)
                total = total.astype(F32) + exchange(total, "tp", n_tp, bit).astype(F32)
            return total

        def both_halves(own):
            return jnp.concatenate([own, exchange(own, "tp", n_tp, 1)], 0)

        def in_order(pair):
            first, second = pair[:half], pair[half:]
            return jnp.where(core == 0, pair, jnp.concatenate([second, first], 0))

        kv_own = qkv_weight[:, 1:].astype(BF).reshape(part, packed)
        w_kv = gathered_in_order(kv_own)
        q_own = jnp.pad(after(qkv_weight, kv_own)[:, 0].astype(BF), ((0, 0), (0, pad)))
        w_q = gathered_in_order(q_own)

        before = jnp.full((rows, reach * tok), -1, jnp.int32)
        behind = jnp.full((rows, reach * tok), 1 << 20, jnp.int32)
        padded = jnp.concatenate([before, segment_ids, behind], 1)
        key_seg = lax.dynamic_slice_in_dim(padded, ci * tok, slots * tok, 1)
        q_seg = lax.dynamic_slice_in_dim(segment_ids, ci * tok, tok, 1)
        q_seg = q_seg.reshape(rows, 2, half)
        q_seg = jnp.where(core == 0, q_seg, q_seg[:, ::-1])
        low = jnp.sum(key_seg[:, None, :] < q_seg[:, :, :1], -1) // half
        high = (jnp.sum(key_seg[:, None, :] <= q_seg[:, :, -1:], -1) + half - 1) // half
        begin = jnp.broadcast_to(jnp.stack([core * half, (1 - core) * half])[None], (rows, 2))
        ranges = jnp.stack([low, high, begin], -1).reshape(rows, 6).astype(jnp.int32)
        side = 1 - 2 * (ci % 2)
        places = [jnp.int32(reach) + 0 * side]
        for d in range(1, reach + 1):
            places += [reach + d * side, reach - d * side]
        places = jnp.broadcast_to(jnp.stack(places)[None], (rows, slots))
        ranges = jnp.concatenate([ranges, places.astype(jnp.int32)], 1)
        q_seg3 = jnp.tile(q_seg[:, :, None, :], (1, 1, 1, heads))
        key_col = key_seg[:, :, None]

        v_bias = jnp.concatenate([jnp.zeros((cols,), F32), qv_bias[1]])
        q_bias = jnp.pad(qv_bias[0], (0, pad))

        kv = []
        for r in every:
            own = (dot(hidden_in[r], w_kv) + v_bias).astype(BF)
            if r:
                own = after(own, *kv[-1][1:3])
            found = [own]
            last = [own, own]
            for d in range(1, reach + 1):
                even, odd = even_swap(last[1]), odd_swap(last[0])
                found += [even, odd]
                last = [even, odd]
            kv.append(found)
        q = [
            ((dot(hidden_in[r], w_q) + q_bias).astype(BF) * jnp.asarray(HEAD_DIM**-0.5, BF))
            for r in every
        ]

        late = kv[0][0]
        vec_own = jnp.concatenate(
            [out_bias, first_gain, first_shift, outer_bias, second_gain, second_shift]
        )
        vec_own = jnp.pad(vec_own.reshape(6, part), ((0, 10), (0, 0)))
        wo_own = jnp.concatenate([after(out_weight, late), vec_own], 0).astype(BF)
        wo_vec = gathered(wo_own, 1)
        w_out = jnp.concatenate([jnp.zeros((pad, width), BF), wo_vec[:cols]], 0)
        vectors = wo_vec[cols : cols + 6].astype(F32)
        w_in = gathered(after(inner_weight, wo_own).astype(BF), 0)
        w_outer = gathered(after(outer_weight, wo_own).astype(BF), 1)
        bo, g1, s1, bd, g2, s2 = [vectors[i] for i in range(6)]

        def normed(summed):
            average = jnp.mean(summed, -1, keepdims=True)
            centered = summed - average
            variance = jnp.mean(centered * centered, -1, keepdims=True)
            scale = lax.rsqrt(variance + EPSILON)
            return centered * scale, scale

        def norm_back(grad, gain, hat, scale):
            inner = grad * gain
            return scale * (
                inner
                - jnp.mean(inner, -1, keepdims=True)
                - hat * jnp.mean(inner * hat, -1, keepdims=True)
            )

        x_res = [rolled(own_half(hidden_in[r]), 1).astype(F32) for r in every]
        cots = [rolled(own_half(cotangent[r]), 1).astype(F32) for r in every]

        def chain(steps, first_gate=None):
            gate = first_gate
            for r in every:
                gate = steps(r, gate)
            return gate

        def gated(value, gate):
            return value if gate is None else after(value, gate)

        o, lse, sent1 = [None] * rows, [None] * rows, [None] * rows

        def stage1(r, gate):
            o[r], lse[r] = attend_fwd(ranges[r], gated(q[r], gate), q_seg3[r], key_col[r], *kv[r])
            send = dot(o[r][half:], w_out)
            sent1[r] = core_sum(dot(o[r][:half], w_out), send)
            return sent1[r]

        gate = chain(stage1)

        hat1, scale1, y1, y1b = [None] * rows, [None] * rows, [None] * rows, [None] * rows
        u, slope, sent2 = [None] * rows, [None] * rows, [None] * rows

        def stage2(r, gate):
            total = gated(chip_sum(sent1[r]), gate)
            hat1[r], scale1[r] = normed(x_res[r] + total + bo)
            y1[r] = hat1[r] * g1 + s1
            y1b[r] = both_halves(y1[r].astype(BF))
            a = dot(y1b[r], w_in) + inner_bias
            cdf = 0.5 * (1.0 + lax.erf(a * (0.5**0.5)))
            u[r] = (a * cdf).astype(BF)
            slope[r] = (cdf + a * jnp.exp(-0.5 * a * a) * 0.3989422804014327).astype(BF)
            send = dot(u[r][half:], w_outer)
            sent2[r] = core_sum(dot(u[r][:half], w_outer), send)
            return sent2[r]

        gate = chain(stage2, gate)

        result, dh2, d2b, dab, sent3 = ([None] * rows for _ in range(5))
        d_vec2, d_bi = [None] * rows, [None] * rows

        def stage3(r, gate):
            total = gated(chip_sum(sent2[r]), gate)
            hat2, scale2 = normed(y1[r] + total + bd)
            c = cots[r]
            result[r] = (hat2 * g2 + s2).astype(BF)
            dh2[r] = norm_back(c, g2, hat2, scale2)
            d2b[r] = both_halves(dh2[r].astype(BF))
            d_vec2[r] = [jnp.sum(dh2[r], 0), jnp.sum(c * hat2, 0), jnp.sum(c, 0)]
            da = dot_nt(d2b[r], w_outer) * slope[r].astype(F32)
            d_bi[r] = jnp.sum(da, 0)
            dab[r] = da.astype(BF)
            send = dot_nt(dab[r][half:], w_in)
            sent3[r] = core_sum(dot_nt(dab[r][:half], w_in), send)
            return sent3[r]

        gate = chain(stage3, gate)

        def over_rows(terms):
            return functools.reduce(lambda p, q: p + q, terms)

        send_outer = over_rows(dot_tn(gated(u[r], gate), d2b[r][:, part:]) for r in every).astype(BF)
        send_in = over_rows(dot_tn(y1b[r][:, part:], gated(dab[r], gate)) for r in every).astype(BF)
        gate = send_in

        dh1, d1b, d_vec1, dqs, biases, parts = ([None] * rows for _ in range(6))

        def stage4(r, gate):
            total = gated(chip_sum(sent3[r]), gate)
            dy1 = dh2[r] + total
            dh1[r] = norm_back(dy1, g1, hat1[r], scale1[r])
            d1b[r] = both_halves(dh1[r].astype(BF))
            d_vec1[r] = [jnp.sum(dh1[r], 0), jnp.sum(dy1 * hat1[r], 0), jnp.sum(dy1, 0)]
            do = dot_nt(d1b[r], w_out).astype(BF)
            res = attend_bwd(ranges[r], q[r], q_seg3[r], key_col[r], o[r], do, lse[r], *kv[r])
            dqs[r], biases[r], parts[r] = res[0], res[1][0], res[2:]
            return res[0]

        gate = chain(stage4, gate)

        own_outer = over_rows(dot_tn(u[r], d2b[r][:, :part]) for r in every)
        own_in = over_rows(dot_tn(y1b[r][:, :part], dab[r]) for r in every)
        g_outer = shard_sum(own_outer, send_outer, 1)
        g_in = shard_sum(own_in, send_in, 0)

        dkvs, d_bv = [None] * rows, [None] * rows
        for r in every:
            carry = [None, None]
            for d in range(reach, 0, -1):
                pair = [parts[r][2 * d - 1], parts[r][2 * d]]
                if carry[0] is not None:
                    pair = [
                        (p.astype(F32) + c.astype(F32)).astype(BF) for p, c in zip(pair, carry)
                    ]
                even, odd = even_swap(pair[0]), odd_swap(pair[1])
                carry = [odd, even]
            total = parts[r][0].astype(F32)
            if carry[0] is not None:
                total = total + carry[0].astype(F32) + carry[1].astype(F32)
            d_bv[r] = jnp.sum(total[:, cols:], 0)
            dkvs[r] = total.astype(BF)

        if n_shard == 2:
            x_own = [jnp.where(si == 0, hidden_in[r][:, :part], hidden_in[r][:, part:]) for r in every]
            x_send = [jnp.where(si == 0, hidden_in[r][:, part:], hidden_in[r][:, :part]) for r in every]
        else:
            x_all = [rolled(hidden_in[r], 1) for r in every]
            x_own = [x_all[r][:, :part] for r in every]
            x_send = [x_all[r][:, part:] for r in every]
        send_mix = jnp.concatenate(
            [
                over_rows(dot_tn(o[r], d1b[r][:, part:]) for r in every)[pad:].astype(BF),
                over_rows(dot_tn(dqs[r], x_send[r]) for r in every)[:cols].astype(BF),
            ],
            0,
        )
        own_mix = jnp.concatenate(
            [
                over_rows(dot_tn(o[r], d1b[r][:, :part]) for r in every)[pad:],
                over_rows(dot_tn(dqs[r], x_own[r]) for r in every)[:cols],
            ],
            0,
        )
        g_mix = shard_sum(own_mix, send_mix, 1)

        d_vec = jnp.concatenate(
            [over_rows(v) for v in zip(*d_vec1)] + [over_rows(v) for v in zip(*d_vec2)]
        ).reshape(6, width)
        d_vec = d_vec + exchange(d_vec, "tp", n_tp, 1)
        small = jnp.concatenate([over_rows(d_bi), over_rows(biases)[:cols], over_rows(d_bv)])
        send_kv = over_rows(dot_tn(x_send[r], dkvs[r]) for r in every)
        own_kv = over_rows(dot_tn(x_own[r], dkvs[r]) for r in every)
        if n_shard == 2 and ctx_whole:
            own_flat = jnp.concatenate([d_vec[:, :part].reshape(-1), small])
            send_flat = jnp.concatenate([d_vec[:, part:].reshape(-1), small])
            unit = 16 * n_ctx
            lines = -(-own_flat.size // packed)
            lines = lines + (-(part + lines)) % unit
            fill = lines * packed - own_flat.size
            own_flat = jnp.pad(own_flat, (0, fill)).reshape(lines, packed)
            send_flat = jnp.pad(send_flat, (0, fill)).reshape(lines, packed)
            own_kv = jnp.concatenate([own_kv, own_flat], 0)
            send_kv = jnp.concatenate([send_kv.astype(BF), send_flat.astype(BF)], 0)
            g_kv = ctx_sum(shard_sum(own_kv, send_kv, 0))
            flat = g_kv[part:].reshape(-1)
            g_kv = g_kv[:part]
        else:
            vec = lax.psum_scatter(unrolled(d_vec, 1), "shard", scatter_dimension=1, tiled=True)
            flat = jnp.concatenate([vec.reshape(-1), lax.psum(small, "shard")])
            flat = lax.psum(flat, "ctx")
            g_kv = ctx_sum(shard_sum(own_kv, send_kv, 0))
        vec = flat[: 6 * part].reshape(6, part)
        small = flat[6 * part :]

        g_outer = ctx_sum(g_outer)
        g_in = ctx_sum(g_in)
        g_mix = ctx_sum(g_mix)
        grad_qkv = jnp.concatenate([g_mix[cols:].T[:, None], g_kv.reshape(part, 2, cols)], 1)

        hidden_grads = []
        for r in every:
            send = dot_nt(other_half(dqs[r]), w_q) + dot_nt(other_half(dkvs[r]), w_kv)
            own = dot_nt(own_half(dqs[r]), w_q) + dot_nt(own_half(dkvs[r]), w_kv)
            total = chip_sum(core_sum(own, send))
            grad = (unrolled(dh1[r], 1) + total).astype(BF)
            hidden_grads.append(in_order(both_halves(grad)))
        outputs = [in_order(both_halves(unrolled(result[r], 1))) for r in every]

        return (
            jnp.stack(outputs),
            jnp.stack(hidden_grads),
            grad_qkv,
            small[units : units + packed].reshape(2, cols),
            g_mix[:cols],
            vec[0],
            vec[1],
            vec[2],
            g_in,
            small[:units],
            g_outer,
            vec[3],
            vec[4],
            vec[5],
        )

    return body


def solution(mesh):
    body = make_body(mesh.shape["shard"], mesh.shape["ctx"], mesh.shape["tp"])
    in_specs = (
        P("shard", "ctx", None),
        P("shard", None),
        P("shard", None, "tp"),
        P(None, "tp"),
        P("tp", "shard"),
        P("shard"),
        P("shard"),
        P("shard"),
        P("shard", "tp"),
        P("tp"),
        P("tp", "shard"),
        P("shard"),
        P("shard"),
        P("shard"),
        P("shard", "ctx", None),
    )
    out_specs = (
        P("shard", "ctx", None),
        P("shard", "ctx", None),
        P("shard", None, "tp"),
        P(None, "tp"),
        P("tp", "shard"),
        P("shard"),
        P("shard"),
        P("shard"),
        P("shard", "tp"),
        P("tp"),
        P("tp", "shard"),
        P("shard"),
        P("shard"),
        P("shard"),
    )
    return jax.shard_map(body, mesh=mesh, in_specs=in_specs, out_specs=out_specs, check_vma=False)
```

```python
import functools

import jax
import jax.numpy as jnp
from jax import lax
from jax.experimental import pallas as pl
from jax.experimental.pallas import tpu as pltpu
from jax.sharding import PartitionSpec as P

HEAD_DIM = 64
LONGEST = 1024
EPSILON = 1e-12
NEGATIVE = -1e30
BF = jnp.bfloat16
F32 = jnp.float32


def dot(a, b):
    return jnp.dot(a, b, preferred_element_type=F32)


def dot_tn(a, b):
    return lax.dot_general(a, b, (((0,), (0,)), ((), ())), preferred_element_type=F32)


def dot_nt(a, b):
    return lax.dot_general(a, b, (((1,), (1,)), ((), ())), preferred_element_type=F32)


def head_stack(tile, first, heads):
    row = lax.broadcasted_iota(jnp.int32, tile.shape, 0)
    parts = []
    for h in range(heads):
        start = first + h * HEAD_DIM
        parts.append(jnp.where((row >= start) & (row < start + HEAD_DIM), tile, jnp.zeros_like(tile)))
    return jnp.concatenate(parts, 1)


def load_blocks(kv_refs, kvb, sem, tok, slot_of):
    copies = [
        pltpu.make_async_copy(ref, kvb.at[pl.ds(pl.multiple_of(slot_of(i) * tok, tok), tok)], sem.at[i])
        for i, ref in enumerate(kv_refs)
    ]
    for copy in copies:
        copy.start()
    for copy in copies:
        copy.wait()


def forward_kernel(slots, heads, tq, tk, rng, q_ref, qseg_ref, kseg_ref, *rest):
    kv_refs = rest[:slots]
    o_ref, lse_ref, aug_ref, kvb, st, acc, sem = rest[slots:]
    tok = q_ref.shape[0]
    wide = q_ref.shape[1]
    table = 3 * (tok // tq)
    load_blocks(kv_refs, kvb, sem, tok, lambda i: rng[table + i])
    vfirst = 2 * heads * HEAD_DIM - wide
    voff = wide - heads * HEAD_DIM
    for t in range(tok // tq):
        lo, hi = rng[3 * t], rng[3 * t + 1]
        qs = pl.multiple_of(rng[3 * t + 2], tq)
        qt = q_ref[pl.ds(qs, tq), :].T
        q3t = head_stack(qt, 0, heads)
        qseg = qseg_ref[t]

        def scan_scores(j, top, q3t=q3t, qseg=qseg):
            at = pl.multiple_of(j * tk, tk)
            scores = dot(kvb[pl.ds(at, tk), :wide], q3t)
            scores = jnp.where(kseg_ref[pl.ds(at, tk), :] == qseg, scores, NEGATIVE)
            st[pl.ds(at, tk), :] = scores
            return jnp.maximum(top, jnp.max(scores.reshape(tk // 8, 8, heads * tq), 0))

        top8 = lax.fori_loop(lo, hi, scan_scores, jnp.full((8, heads * tq), NEGATIVE, F32))
        top = jnp.max(top8, 0, keepdims=True)
        acc[...] = jnp.zeros_like(acc)

        def scan_values(j, total, top=top):
            at = pl.multiple_of(j * tk, tk)
            weights = jnp.exp(st[pl.ds(at, tk), :] - top)
            acc[...] += dot_tn(kvb[pl.ds(at, tk), vfirst:], weights.astype(BF))
            return total + jnp.sum(weights.reshape(tk // 8, 8, heads * tq), 0)

        total8 = lax.fori_loop(lo, hi, scan_values, jnp.zeros((8, heads * tq), F32))
        total = jnp.sum(total8, 0, keepdims=True)
        lse = top + jnp.log(total)
        lse_ref[t] = lse
        full = jnp.concatenate([qt[: wide - voff].astype(F32), spread(-lse, voff, heads, tq)], 0)
        aug_ref[pl.ds(qs, tq), :] = full.T.astype(BF)
        inv = 1.0 / total
        pieces = [jnp.zeros((voff, tq), F32)]
        for h in range(heads):
            rows = slice(voff + h * HEAD_DIM, voff + (h + 1) * HEAD_DIM)
            cols = slice(h * tq, (h + 1) * tq)
            pieces.append(acc[rows, cols] * inv[:, cols])
        o_ref[t * tq : (t + 1) * tq, :] = jnp.concatenate(pieces, 0).T.astype(BF)


def thirds(value):
    high = value.astype(BF).astype(F32)
    rest = value - high
    middle = rest.astype(BF).astype(F32)
    return [high, middle, rest - middle]


def spread(rows, count, heads, tq):
    at = lax.broadcasted_iota(jnp.int32, (count, tq), 0)
    out = jnp.zeros((count, tq), F32)
    for h in range(heads):
        for i, piece in enumerate(thirds(rows[:, h * tq : (h + 1) * tq])):
            out = jnp.where(at == 3 * h + i, piece, out)
    return out


def mix_kernel(heads, tq, rng, d1_ref, w_ref, o_ref, do_ref, delta_ref):
    wide = o_ref.shape[1]
    voff = wide - heads * HEAD_DIM
    for t in range(o_ref.shape[0] // tq):
        qs = pl.multiple_of(rng[3 * t + 2], tq)
        grad = dot_nt(w_ref[...], d1_ref[t * tq : (t + 1) * tq, :]).astype(BF).astype(F32)
        prod = grad * o_ref[t * tq : (t + 1) * tq, :].T.astype(F32)
        delta = jnp.concatenate(
            [
                jnp.sum(prod[voff + h * HEAD_DIM : voff + (h + 1) * HEAD_DIM], 0, keepdims=True)
                for h in range(heads)
            ],
            1,
        )
        delta_ref[t] = delta
        full = jnp.concatenate([spread(-delta, voff, heads, tq), grad[voff:]], 0)
        do_ref[pl.ds(qs, tq), :] = full.T.astype(BF)


def query_kernel(slots, heads, tq, tk, rng, q_ref, qseg_ref, kseg_ref, do_ref, lse_ref, delta_ref, *rest):
    kv_refs = rest[:slots]
    dq_ref, bias_ref, kvb, dqt, sem = rest[slots:]
    tok = q_ref.shape[0]
    wide = q_ref.shape[1]
    table = 3 * (tok // tq)
    load_blocks(kv_refs, kvb, sem, tok, lambda i: rng[table + i])
    vfirst = 2 * heads * HEAD_DIM - wide
    voff = wide - heads * HEAD_DIM
    bias = jnp.zeros((1, wide), F32)
    for t in range(tok // tq):
        lo, hi = rng[3 * t], rng[3 * t + 1]
        qs = pl.multiple_of(rng[3 * t + 2], tq)
        q3t = head_stack(q_ref[pl.ds(qs, tq), :].T, 0, heads)
        do3t = head_stack(do_ref[pl.ds(qs, tq), :].T, voff, heads)
        delta = delta_ref[t]
        qseg = qseg_ref[t]
        lse = lse_ref[t]
        dqt[...] = jnp.zeros_like(dqt)

        def scan_keys(j, carry, q3t=q3t, do3t=do3t, delta=delta, qseg=qseg, lse=lse):
            at = pl.multiple_of(j * tk, tk)
            k = kvb[pl.ds(at, tk), :wide]
            same = kseg_ref[pl.ds(at, tk), :] == qseg
            probs = jnp.where(same, jnp.exp(dot(k, q3t) - lse), 0.0)
            grad = (probs * (dot(kvb[pl.ds(at, tk), vfirst:], do3t) - delta)).astype(BF)
            dqt[...] += dot_tn(k, grad)
            return carry

        lax.fori_loop(lo, hi, scan_keys, 0)
        pieces = []
        for h in range(heads):
            pieces.append(dqt[h * HEAD_DIM : (h + 1) * HEAD_DIM, h * tq : (h + 1) * tq])
        pieces.append(jnp.zeros((wide - heads * HEAD_DIM, tq), F32))
        dq = jnp.concatenate(pieces, 0).T * HEAD_DIM**-0.5
        bias = bias + jnp.sum(dq, 0, keepdims=True)
        dq_ref[pl.ds(qs, tq), :] = dq.astype(BF)
    bias_ref[...] = bias


def key_kernel(slots, row, heads, tq, tk, rng, kv_ref, kseg_ref, qseg_ref, *rest):
    q_refs, do_refs = rest[:slots], rest[slots : 2 * slots]
    dkv_ref, bias_ref, qb, dob, dkt, dvt, qsem, dosem = rest[2 * slots :]
    tok, packed = kv_ref.shape
    wide = qb.shape[1]
    table = 3 * (tok // tq)
    copies = []
    for i in range(slots):
        place = pl.ds(pl.multiple_of(rng[table + i] * tok, tok), tok)
        q_part = q_refs[i].at[pl.ds(row * tok, tok)]
        copies.append(pltpu.make_async_copy(q_part, qb.at[place], qsem.at[i]))
        copies.append(pltpu.make_async_copy(do_refs[i], dob.at[place], dosem.at[i]))
    for copy in copies:
        copy.start()
    for copy in copies:
        copy.wait()
    cols = heads * HEAD_DIM
    vfirst = packed - wide
    voff = wide - cols
    at_row = lax.broadcasted_iota(jnp.int32, (wide, tq), 0)
    bias = jnp.zeros((1, packed), F32)
    for t in range(tok // tq):
        lo, hi = rng[3 * t], rng[3 * t + 1]
        qs = pl.multiple_of(rng[3 * t + 2], tq)

        def stack(tile, first, ones):
            parts = []
            for h in range(heads):
                head = (at_row >= first + h * HEAD_DIM) & (at_row < first + (h + 1) * HEAD_DIM)
                one = (at_row >= ones + 3 * h) & (at_row < ones + 3 * h + 3)
                kept = jnp.where(head, tile, jnp.zeros_like(tile))
                parts.append(jnp.where(one, jnp.ones_like(tile), kept))
            return jnp.concatenate(parts, 1)

        k3t = stack(kv_ref[pl.ds(qs, tq), :wide].T, 0, cols)
        v3t = stack(kv_ref[pl.ds(qs, tq), vfirst:].T, voff, 0)
        kseg = kseg_ref[t]
        dkt[...] = jnp.zeros_like(dkt)
        dvt[...] = jnp.zeros_like(dvt)

        def scan_queries(j, carry, k3t=k3t, v3t=v3t, kseg=kseg):
            at = pl.multiple_of(j * tk, tk)
            q = qb[pl.ds(at, tk), :]
            do = dob[pl.ds(at, tk), :]
            same = qseg_ref[pl.ds(at, tk), :] == kseg
            probs = jnp.where(same, jnp.exp(dot(q, k3t)), 0.0)
            grad = (probs * dot(do, v3t)).astype(BF)
            dkt[...] += dot_tn(q, grad)
            dvt[...] += dot_tn(do, probs.astype(BF))
            return carry

        lax.fori_loop(lo, hi, scan_queries, 0)
        pieces = []
        for ref, first in ((dkt, 0), (dvt, voff)):
            for h in range(heads):
                start = first + h * HEAD_DIM
                pieces.append(ref[start : start + HEAD_DIM, h * tq : (h + 1) * tq])
        grads = jnp.concatenate(pieces, 0).T
        bias = bias + jnp.sum(grads, 0, keepdims=True)
        dkv_ref[pl.ds(qs, tq), :] = grads.astype(BF)
    bias_ref[...] = bias


def input_kernel(rng, dq_ref, dkv_ref, wq_ref, wkv_ref, own_ref, send_ref):
    half = own_ref.shape[0]
    for t, ref in enumerate((own_ref, send_ref)):
        at = pl.ds(pl.multiple_of(rng[3 * t + 2], half), half)
        total = dot_nt(dq_ref[at, :], wq_ref[...]) + dot_nt(dkv_ref[at, :], wkv_ref[...])
        ref[...] = total.astype(ref.dtype)


def weight_kernel(part, axis, rows, keep, *refs):
    own_ref, send_ref = refs[-2:]
    at = 0
    for first, last in keep:
        lefts, rights = refs[:rows], refs[rows : 2 * rows]
        refs = refs[2 * rows :]
        for ref, span in ((own_ref, slice(0, part)), (send_ref, slice(part, None))):
            total = None
            for a, b in zip(lefts, rights):
                term = dot_tn(a[...], b[:, span]) if axis else dot_tn(a[:, span], b[...])
                total = term if total is None else total + term
            if axis:
                ref[at : at + last - first, :] = total[first:last].astype(ref.dtype)
            else:
                ref[...] = total.astype(ref.dtype)
        at += last - first


def weight_grads(pairs, part, axis, keep):
    width = pairs[0][1 if axis else 0][0].shape[1]
    if part % 128 or (width - part) % 128:
        total = jnp.concatenate(
            [
                functools.reduce(lambda p, q: p + q, [dot_tn(a, b) for a, b in zip(*pair)])[
                    (slice(*span) if axis else slice(None))
                ]
                for pair, span in zip(pairs, keep)
            ],
            0,
        )
        if axis:
            return total[:, :part], total[:, part:].astype(BF)
        return total[:part], total[part:].astype(BF)
    kept = sum(last - first for first, last in keep)
    shapes = [(kept, n) if axis else (n, pairs[0][1][0].shape[1]) for n in (part, width - part)]
    operands = [x for lefts, rights in pairs for x in list(lefts) + list(rights)]
    work = sum(2 * a.shape[0] * a.shape[1] * b.shape[1] for lefts, rights in pairs for a, b in zip(lefts, rights))
    vmem = pl.BlockSpec(memory_space=pltpu.VMEM)
    return pl.pallas_call(
        functools.partial(weight_kernel, part, axis, len(pairs[0][0]), keep),
        out_shape=(jax.ShapeDtypeStruct(shapes[0], F32), jax.ShapeDtypeStruct(shapes[1], BF)),
        in_specs=[vmem] * len(operands),
        out_specs=(vmem, vmem),
        cost_estimate=pl.CostEstimate(
            flops=work, transcendentals=0, bytes_accessed=sum(x.size * 2 for x in operands)
        ),
        compiler_params=pltpu.CompilerParams(vmem_limit_bytes=24 << 20),
        name="weight_grads",
    )(*operands)


def last_kernel(rows, part, units, refs_in, own_ref, send_ref):
    dkv_refs, x_refs = refs_in[:rows], refs_in[rows : 2 * rows]
    vec_ref = refs_in[2 * rows]
    unit_refs, q_refs, v_refs = (refs_in[2 * rows + 1 + i * rows :][:rows] for i in range(3))
    packed = dkv_refs[0].shape[1]
    cols = packed // 2
    shape = (own_ref.shape[0] - packed, part)
    at = lax.broadcasted_iota(jnp.int32, shape, 0)
    lane = lax.broadcasted_iota(jnp.int32, (1, part), 1)

    def over(refs):
        return functools.reduce(lambda a, b: a + b, [ref[...] for ref in refs])

    unit_row = over(unit_refs)
    q_row = jnp.concatenate([over(q_refs), jnp.zeros((1, packed - q_refs[0].shape[1]), F32)], 1)
    pieces = [unit_row[:, i : i + packed] for i in range(0, units, packed)]
    pieces.append(jnp.where(lane < cols, q_row, over(v_refs)))
    for ref, span in ((own_ref, slice(0, part)), (send_ref, slice(part, None))):
        total = None
        for a, b in zip(dkv_refs, x_refs):
            term = dot_tn(a[...], b[:, span])
            total = term if total is None else total + term
        ref[:packed, :] = total.astype(ref.dtype)
        block = jnp.concatenate([vec_ref[:, span], jnp.zeros((shape[0] - 8, part), F32)], 0)
        for i, piece in enumerate(pieces):
            block = jnp.where(at == 8 + i, piece, block)
        ref[packed:, :] = block.astype(ref.dtype)


def last_grads(dkvs, xs, d_vec, d_units, d_q, d_v, part, lines):
    rows = len(dkvs)
    packed = dkvs[0].shape[1]
    units = d_units[0].shape[1]
    operands = list(dkvs) + list(xs) + [d_vec] + list(d_units) + list(d_q) + list(d_v)
    vmem = pl.BlockSpec(memory_space=pltpu.VMEM)
    shape = (packed + lines, part)

    def kernel(*refs):
        last_kernel(rows, part, units, refs[:-2], *refs[-2:])

    return pl.pallas_call(
        kernel,
        out_shape=(jax.ShapeDtypeStruct(shape, F32), jax.ShapeDtypeStruct(shape, BF)),
        in_specs=[vmem] * len(operands),
        out_specs=(vmem, vmem),
        cost_estimate=pl.CostEstimate(
            flops=4 * rows * packed * part * xs[0].shape[0],
            transcendentals=0,
            bytes_accessed=sum(x.size * 2 for x in operands),
        ),
        compiler_params=pltpu.CompilerParams(vmem_limit_bytes=24 << 20),
        name="last_grads",
    )(*operands)


def make_attention(slots, heads, tok, wide, packed, width, n_rows):
    tq = tok // 2
    tk = tq
    vmem = pl.BlockSpec(memory_space=pltpu.VMEM)
    smem = pl.BlockSpec(memory_space=pltpu.SMEM)
    hbm = pl.BlockSpec(memory_space=pl.ANY)
    pairs = 2 * heads * tok * 1024 * wide
    params = pltpu.CompilerParams(vmem_limit_bytes=32 << 20)
    rowed = jax.ShapeDtypeStruct((2, 1, heads * tq), F32)
    tokens = jax.ShapeDtypeStruct((tok, wide), BF)

    def cost(products, exps):
        return pl.CostEstimate(
            flops=products * pairs,
            transcendentals=exps * heads * tok * 1024,
            bytes_accessed=slots * tok * packed * 2,
        )

    forward = pl.pallas_call(
        functools.partial(forward_kernel, slots, heads, tq, tk),
        out_shape=(tokens, rowed, tokens),
        in_specs=[smem, vmem, vmem, vmem] + [hbm] * slots,
        out_specs=(vmem, vmem, vmem),
        scratch_shapes=[
            pltpu.VMEM((slots * tok, packed), BF),
            pltpu.VMEM((slots * tok, heads * tq), F32),
            pltpu.VMEM((wide, heads * tq), F32),
            pltpu.SemaphoreType.DMA((slots,)),
        ],
        cost_estimate=cost(2, 1),
        compiler_params=params,
        name="attend_forward",
    )
    mix_back = pl.pallas_call(
        functools.partial(mix_kernel, heads, tq),
        out_shape=(tokens, rowed),
        in_specs=[smem, vmem, vmem, vmem],
        out_specs=(vmem, vmem),
        cost_estimate=pl.CostEstimate(
            flops=2 * tok * wide * width, transcendentals=0, bytes_accessed=tok * (2 * wide + width) * 2
        ),
        compiler_params=params,
        name="mix_back",
    )
    query_back = pl.pallas_call(
        functools.partial(query_kernel, slots, heads, tq, tk),
        out_shape=(tokens, jax.ShapeDtypeStruct((1, wide), F32)),
        in_specs=[smem] + [vmem] * 6 + [hbm] * slots,
        out_specs=(vmem, vmem),
        scratch_shapes=[
            pltpu.VMEM((slots * tok, packed), BF),
            pltpu.VMEM((wide, heads * tq), F32),
            pltpu.SemaphoreType.DMA((slots,)),
        ],
        cost_estimate=cost(3, 1),
        compiler_params=params,
        name="query_back",
    )
    key_back = [
        pl.pallas_call(
            functools.partial(key_kernel, slots, row, heads, tq, tk),
            out_shape=(
                jax.ShapeDtypeStruct((tok, packed), BF),
                jax.ShapeDtypeStruct((1, packed), F32),
            ),
            in_specs=[smem] + [vmem] * 3 + [hbm] * (2 * slots),
            out_specs=(vmem, vmem),
            scratch_shapes=[
                pltpu.VMEM((slots * tok, wide), BF),
                pltpu.VMEM((slots * tok, wide), BF),
                pltpu.VMEM((wide, heads * tq), F32),
                pltpu.VMEM((wide, heads * tq), F32),
                pltpu.SemaphoreType.DMA((slots,)),
                pltpu.SemaphoreType.DMA((slots,)),
            ],
            cost_estimate=cost(4, 1),
            compiler_params=params,
            name="key_back",
        )
        for row in range(n_rows)
    ]
    input_back = pl.pallas_call(
        input_kernel,
        out_shape=(
            jax.ShapeDtypeStruct((tq, width), F32),
            jax.ShapeDtypeStruct((tq, width), BF),
        ),
        in_specs=[smem] + [vmem] * 4,
        out_specs=(vmem, vmem),
        cost_estimate=pl.CostEstimate(
            flops=2 * tok * (wide + packed) * width,
            transcendentals=0,
            bytes_accessed=tok * (wide + packed + width) * 4,
        ),
        compiler_params=params,
        name="input_back",
    )
    return forward, mix_back, query_back, key_back, input_back


def after(value, *others):
    return lax.optimization_barrier((value,) + others)[0]


def make_body(n_shard, n_ctx, n_tp):
    bits = [1 << i for i in range(n_tp.bit_length() - 1)]
    ctx_steps = [1 << i for i in range(n_ctx.bit_length() - 1)]
    ctx_whole = not n_ctx & (n_ctx - 1)

    def exchange(value, axis, size, bit):
        return lax.ppermute(value, axis, [(i, i ^ bit) for i in range(size) if i ^ bit < size])

    def even_swap(value):
        return exchange(value, "ctx", n_ctx, 1)

    def odd_swap(value):
        pairs = []
        for i in range(1, n_ctx - 1, 2):
            pairs += [(i, i + 1), (i + 1, i)]
        return lax.ppermute(value, "ctx", pairs)

    def swap(value, kind):
        return odd_swap(value) if kind else even_swap(value)

    ctx_count = max(2 * len(ctx_steps) - 1, 1)

    def ctx_step(cur, step):
        ci = lax.axis_index("ctx")
        count = len(ctx_steps)
        bit = ctx_steps[step] if step < count else ctx_steps[2 * count - 2 - step]
        up = (ci // bit) % 2
        if step == count - 1:
            cur = cur.astype(BF)
            return (cur.astype(F32) + exchange(cur, "ctx", n_ctx, bit).astype(F32)).astype(BF)
        if step < count:
            half = cur.shape[0] // 2
            send = lax.dynamic_slice_in_dim(cur, (1 - up) * half, half, 0).astype(BF)
            keep = lax.dynamic_slice_in_dim(cur, up * half, half, 0)
            return keep + exchange(send, "ctx", n_ctx, bit).astype(F32)
        other = exchange(cur, "ctx", n_ctx, bit)
        return jnp.where(up == 0, jnp.concatenate([cur, other], 0), jnp.concatenate([other, cur], 0))

    def body(
        hidden_in,
        segment_ids,
        qkv_weight,
        qv_bias,
        out_weight,
        out_bias,
        first_gain,
        first_shift,
        inner_weight,
        inner_bias,
        outer_weight,
        outer_bias,
        second_gain,
        second_shift,
        cotangent,
    ):
        rows, tok, width = hidden_in.shape
        part = width // n_shard
        cols = qkv_weight.shape[2]
        heads = cols // HEAD_DIM
        units = inner_weight.shape[1]
        wide = -(-cols // 128) * 128
        pad = wide - cols
        packed = 2 * cols
        half = tok // 2
        every = list(range(rows))
        si = lax.axis_index("shard")
        ci = lax.axis_index("ctx")
        core = lax.axis_index("tp") % 2
        reach = min(n_ctx - 1, 1 + (LONGEST - 2) // tok)
        slots = 2 * reach + 1
        attend_fwd, mix_back, query_back, key_back, input_back = make_attention(
            slots, heads, tok, wide, packed, width, rows
        )

        def rolled(value, axis):
            if n_shard == 2:
                first = lax.slice_in_dim(value, 0, part, axis=axis)
                second = lax.slice_in_dim(value, part, width, axis=axis)
                return jnp.where(si == 0, value, jnp.concatenate([second, first], axis))
            return jnp.roll(value, -si * part, axis)

        def unrolled(value, axis):
            if n_shard == 2:
                return rolled(value, axis)
            return jnp.roll(value, si * part, axis)

        def others(own, axis):
            if n_shard == 2:
                return exchange(own, "shard", 2, 1)
            whole = rolled(lax.all_gather(own, "shard", axis=axis, tiled=True), axis)
            return lax.slice_in_dim(whole, part, width, axis=axis)

        def gathered(own, axis):
            if n_shard == 2:
                return jnp.concatenate([own, exchange(own, "shard", 2, 1)], axis)
            return rolled(lax.all_gather(own, "shard", axis=axis, tiled=True), axis)

        def gathered_in_order(own):
            if n_shard == 2:
                other = exchange(own, "shard", 2, 1)
                return jnp.where(
                    si == 0, jnp.concatenate([own, other], 0), jnp.concatenate([other, own], 0)
                )
            return lax.all_gather(own, "shard", axis=0, tiled=True)

        def own_half(value):
            return lax.dynamic_slice_in_dim(value, core * half, half, 0)

        def core_sum(own, send):
            total = own + exchange(send.astype(BF), "tp", n_tp, 1).astype(F32)
            return total.astype(BF) if len(bits) > 1 else total

        def chip_sum(total):
            for bit in bits[1:]:
                total = total.astype(BF)
                total = total.astype(F32) + exchange(total, "tp", n_tp, bit).astype(F32)
            return total

        def both_halves(own):
            return jnp.concatenate([own, exchange(own, "tp", n_tp, 1)], 0)

        def in_order(pair):
            first, second = pair[:half], pair[half:]
            return jnp.where(core == 0, pair, jnp.concatenate([second, first], 0))

        box = {}

        def hold(value, *names):
            value, *kept = lax.optimization_barrier((value,) + tuple(box[n] for n in names))
            box.update(zip(names, kept))
            return value

        box["kv_own"] = qkv_weight[:, 1:].astype(BF).reshape(part, packed)
        box["w_kv"] = gathered_in_order(box["kv_own"])
        q_own = jnp.pad(qkv_weight[:, 0].astype(BF), ((0, 0), (0, pad)))
        q_own = hold(q_own, "w_kv")
        w_kv = box["w_kv"]
        w_q = gathered_in_order(q_own)

        before = jnp.full((rows, reach * tok), -1, jnp.int32)
        behind = jnp.full((rows, reach * tok), 1 << 20, jnp.int32)
        padded = jnp.concatenate([before, segment_ids, behind], 1)
        key_seg = lax.dynamic_slice_in_dim(padded, ci * tok, slots * tok, 1)
        q_seg = lax.dynamic_slice_in_dim(segment_ids, ci * tok, tok, 1)
        q_seg = q_seg.reshape(rows, 2, half)
        q_seg = jnp.where(core == 0, q_seg, q_seg[:, ::-1])
        low = jnp.sum(key_seg[:, None, :] < q_seg[:, :, :1], -1) // half
        high = (jnp.sum(key_seg[:, None, :] <= q_seg[:, :, -1:], -1) + half - 1) // half
        begin = jnp.broadcast_to(jnp.stack([core * half, (1 - core) * half])[None], (rows, 2))
        ranges = jnp.stack([low, high, begin], -1).reshape(rows, 6).astype(jnp.int32)
        side = 1 - 2 * (ci % 2)
        places = [jnp.int32(reach) + 0 * side]
        for d in range(1, reach + 1):
            places += [reach + d * side, reach - d * side]
        places = jnp.broadcast_to(jnp.stack(places)[None], (rows, slots))
        ranges = jnp.concatenate([ranges, places.astype(jnp.int32)], 1)
        q_seg3 = jnp.tile(q_seg[:, :, None, :], (1, 1, 1, heads))
        key_col = key_seg[:, :, None]

        v_bias = jnp.concatenate([jnp.zeros((cols,), F32), qv_bias[1]])
        q_bias = jnp.pad(qv_bias[0], (0, pad))

        def halo(own):
            found = [own]
            last = [own, own]
            for d in range(1, reach + 1):
                even, odd = even_swap(last[1]), odd_swap(last[0])
                found += [even, odd]
                last = [even, odd]
            return found

        kv = []
        for r in every:
            box[f"kv{r}"] = (dot(hidden_in[r], w_kv) + v_bias).astype(BF)
            if r:
                box[f"kv{r}"] = after(box[f"kv{r}"], *kv[-1][1:3])
            kv.append(halo(box[f"kv{r}"]))
        q = [
            ((dot(hidden_in[r], w_q) + q_bias).astype(BF) * jnp.asarray(HEAD_DIM**-0.5, BF))
            for r in every
        ]

        vec_own = [out_bias, first_gain, first_shift, outer_bias, second_gain, second_shift]
        vec_own = jnp.concatenate([v[None] for v in vec_own] + [jnp.zeros((10, part), F32)], 0)
        wo_own = hold(jnp.concatenate([out_weight, vec_own], 0).astype(BF), "kv0")
        wo_vec = gathered(wo_own, 1)
        w_out = jnp.concatenate([jnp.zeros((pad, width), BF), wo_vec[:cols]], 0)
        vectors = wo_vec[cols : cols + 6].astype(F32)
        in_own = hold(inner_weight, "kv0").astype(BF)
        box["w_in"] = others(in_own, 0)
        outer_own = hold(outer_weight, "w_in").astype(BF)
        box["w_outer"] = others(outer_own, 1)
        bo, g1, s1, bd, g2, s2 = [vectors[i] for i in range(6)]

        def normed(summed):
            average = jnp.mean(summed, -1, keepdims=True)
            centered = summed - average
            variance = jnp.mean(centered * centered, -1, keepdims=True)
            scale = lax.rsqrt(variance + EPSILON)
            return centered * scale, scale

        def norm_back(grad, gain, hat, scale):
            inner = grad * gain
            return scale * (
                inner
                - jnp.mean(inner, -1, keepdims=True)
                - hat * jnp.mean(inner * hat, -1, keepdims=True)
            )

        x_roll = [rolled(hidden_in[r], 1) for r in every]
        x_res = [own_half(x_roll[r]).astype(F32) for r in every]
        cots = [rolled(own_half(cotangent[r]), 1).astype(F32) for r in every]

        ready = {0: ["w_in"], rows - 1: ["w_outer"]}

        def before(r, this, last):
            return [f"{this}{r - 1}"] if r else ([f"{last}{rows - 1}"] if last else [])

        o, lse, aug = [None] * rows, [None] * rows, [None] * rows
        for r in every:
            query = hold(q[r], *before(r, "a", None), *ready.get(r, []))
            o[r], lse[r], aug[r] = attend_fwd(ranges[r], query, q_seg3[r], key_col[r], *kv[r])
            send = dot(o[r][half:], w_out)
            box[f"a{r}"] = core_sum(dot(o[r][:half], w_out), send)
        q_halo = halo(jnp.concatenate(aug, 0))
        for i, block in enumerate(q_halo[1:]):
            box[f"q{i}"] = block

        hat1, scale1, y1, y1b = [None] * rows, [None] * rows, [None] * rows, [None] * rows
        u, slope = [None] * rows, [None] * rows
        for r in every:
            total = hold(chip_sum(box[f"a{r}"]), *before(r, "b", "a"))
            hat1[r], scale1[r] = normed(x_res[r] + total + bo)
            y1[r] = hat1[r] * g1 + s1
            y1b[r] = both_halves(y1[r].astype(BF))
            if not r:
                w_in = jnp.concatenate([in_own, box["w_in"]], 0)
                w_outer = jnp.concatenate([outer_own, box["w_outer"]], 1)
            a = dot(y1b[r], w_in) + inner_bias
            cdf = 0.5 * (1.0 + lax.erf(a * (0.5**0.5)))
            u[r] = (a * cdf).astype(BF)
            slope[r] = (cdf + a * jnp.exp(-0.5 * a * a) * 0.3989422804014327).astype(BF)
            send = dot(u[r][half:], w_outer)
            box[f"b{r}"] = core_sum(dot(u[r][:half], w_outer), send)

        result, dh2, d2b, dab = ([None] * rows for _ in range(4))
        d_vec2, d_bi = [None] * rows, [None] * rows
        for r in every:
            arrived = [f"q{i}" for i in (0, 1)] if not r else []
            total = hold(chip_sum(box[f"b{r}"]), *before(r, "c", "b"), *arrived)
            hat2, scale2 = normed(y1[r] + total + bd)
            c = cots[r]
            result[r] = (hat2 * g2 + s2).astype(BF)
            dh2[r] = norm_back(c, g2, hat2, scale2)
            d2b[r] = both_halves(dh2[r].astype(BF))
            d_vec2[r] = [jnp.sum(v, 0, keepdims=True) for v in (dh2[r], c * hat2, c)]
            da = dot_nt(d2b[r], w_outer) * slope[r].astype(F32)
            d_bi[r] = jnp.sum(da, 0, keepdims=True)
            dab[r] = da.astype(BF)
            send = dot_nt(dab[r][half:], w_in)
            box[f"c{r}"] = core_sum(dot_nt(dab[r][:half], w_in), send)

        def over_rows(terms):
            return functools.reduce(lambda p, q: p + q, terms)

        def shard_send(name, send):
            box[name] = exchange(send, "shard", 2, 1) if n_shard == 2 else send

        def shard_total(name, own, axis):
            if n_shard == 2:
                return own + box[name].astype(F32)
            whole = unrolled(jnp.concatenate([own, box[name].astype(F32)], axis), axis)
            return lax.psum_scatter(whole, "shard", scatter_dimension=axis, tiled=True)

        def advance(name):
            value, step = box[name], at_step.get(name, 0)
            if ctx_whole and step < ctx_count:
                box[name] = ctx_step(value, step)
            elif not step:
                box[name] = lax.psum(value, "ctx")
            at_step[name] = step + 1

        def finish(name):
            while at_step.get(name, 0) < ctx_count:
                advance(name)
            return box[name].astype(F32)

        at_step = {}

        dh1, d1b, d_vec1, dos, deltas = ([None] * rows for _ in range(5))

        def stage4(r, *names):
            total = hold(chip_sum(box[f"c{r}"]), *names)
            dy1 = dh2[r] + total
            dh1[r] = norm_back(dy1, g1, hat1[r], scale1[r])
            d1b[r] = both_halves(dh1[r].astype(BF))
            d_vec1[r] = [jnp.sum(v, 0, keepdims=True) for v in (dh1[r], dy1 * hat1[r], dy1)]
            box[f"do{r}"], deltas[r] = mix_back(ranges[r], d1b[r], w_out, o[r])

        def send_do(r, d):
            last = [box[f"do{r}"]] * 2 if d == 1 else [box[f"do{r}_{2 * d - 4}"], box[f"do{r}_{2 * d - 3}"]]
            box[f"do{r}_{2 * d - 2}"] = even_swap(last[1])
            box[f"do{r}_{2 * d - 1}"] = odd_swap(last[0])

        gate = [f"c{rows - 1}", "q2", "q3"]
        for r in every:
            stage4(r, *gate)
            send_do(r, 1)
            gate = [f"do{r}"]
            if not r:
                lefts = [hold(u[0], "do0")] + u[1:]
                own_first, box["send_first"] = weight_grads(
                    [(lefts, d2b), (dab, y1b)], part, 1, [(0, units), (0, units)]
                )
                gate = ["send_first"]
        shard_send("x_first", box["send_first"])
        for d in range(2, reach + 1):
            for r in every:
                send_do(r, d)

        dqs, biases, dkvs, d_bv = ([None] * rows for _ in range(4))
        for r in every:
            names = [f"do{rows - 1}", "do0_0", "do0_1"] if not r else [f"dq{r - 1}", f"do{r}_0", f"do{r}_1"]
            if r:
                box["first"] = shard_total("x_first", own_first, 1)
                names.append("first")
            query = hold(aug[r], *names)
            dqs[r], biases[r] = query_back(
                ranges[r], query, q_seg3[r], key_col[r], box[f"do{r}"], lse[r], deltas[r], *kv[r]
            )
            box[f"dq{r}"] = dqs[r]
        dqs = [box[f"dq{r}"] for r in every]
        advance("first")
        own_mix, box["send_mix"] = weight_grads(
            [(o, d1b), (dqs, x_roll)], part, 1, [(pad, wide), (0, cols)]
        )
        shard_send("x_mix", box["send_mix"])
        for r in every:
            names = [f"dq{rows - 1}", "send_mix"] if not r else [f"dkv{r - 1}", "first", "mix"]
            own = hold(kv[r][0], *names)
            blocks = [box[f"do{r}"]] + [box[f"do{r}_{i}"] for i in range(2 * reach)]
            q_blocks = q_halo[:1] + [box[f"q{i}"] for i in range(2 * reach)]
            dkvs[r], bias = key_back[r](ranges[r], own, q_seg3[r], key_col[r], *q_blocks, *blocks)
            d_bv[r] = bias
            box[f"dkv{r}"] = dkvs[r]
            if not r:
                advance("first")
                box["mix"] = shard_total("x_mix", own_mix, 1)
        dkvs = [box[f"dkv{r}"] for r in every]

        d_vec = jnp.concatenate(
            [over_rows(v) for v in zip(*d_vec1)]
            + [over_rows(v) for v in zip(*d_vec2)]
            + [jnp.zeros((2, width), F32)],
            0,
        )
        d_vec = d_vec + exchange(d_vec, "tp", n_tp, 1)
        if n_shard == 2 and ctx_whole and part == packed and units % packed == 0:
            lines = 8 + units // packed + 1
            lines += (-(packed + lines)) % (16 * n_ctx)
            own_last, send_last = last_grads(dkvs, x_roll, d_vec, d_bi, biases, d_bv, part, lines)
            shard_send("x_last", send_last)
            box["last"] = shard_total("x_last", own_last, 1)
            g_last = finish("last")
            vec = g_last[packed : packed + 6]
            d_units = g_last[packed + 8 : packed + 8 + units // packed].reshape(units)
            d_qv = g_last[packed + 8 + units // packed].reshape(2, cols)
        else:
            own_last, send_last = weight_grads([(dkvs, x_roll)], part, 1, [(0, packed)])
            d_qv = jnp.concatenate([over_rows(biases)[:, :cols], over_rows(d_bv)[:, cols:]], 1)
            vec = lax.psum_scatter(unrolled(d_vec, 1), "shard", scatter_dimension=1, tiled=True)
            vec = lax.psum(vec, "ctx")
            d_units = lax.psum(over_rows(d_bi)[0], ("shard", "ctx"))
            d_qv = lax.psum(d_qv[0], ("shard", "ctx")).reshape(2, cols)
            shard_send("x_last", send_last)
            box["last"] = shard_total("x_last", own_last, 1)
            g_last = finish("last")
        g_first = finish("first")
        g_mix = finish("mix")
        grad_qkv = jnp.concatenate([g_mix[cols:], g_last[:packed]], 0).T.reshape(part, 3, cols)

        hidden_grads = []
        for r in every:
            own, send = input_back(ranges[r], dqs[r], dkvs[r], w_q, w_kv)
            total = chip_sum(core_sum(own, send))
            grad = (unrolled(dh1[r], 1) + total).astype(BF)
            hidden_grads.append(in_order(both_halves(grad)))
        mine = jnp.stack([unrolled(result[r], 1) for r in every])
        theirs = exchange(mine, "tp", n_tp, 1)
        outputs = jnp.where(
            core == 0, jnp.concatenate([mine, theirs], 1), jnp.concatenate([theirs, mine], 1)
        )

        return (
            outputs,
            jnp.stack(hidden_grads),
            grad_qkv,
            d_qv,
            g_mix[:cols],
            vec[0],
            vec[1],
            vec[2],
            g_first[units : 2 * units].T,
            d_units,
            g_first[:units],
            vec[3],
            vec[4],
            vec[5],
        )

    return body


def solution(mesh):
    body = make_body(mesh.shape["shard"], mesh.shape["ctx"], mesh.shape["tp"])
    in_specs = (
        P("shard", "ctx", None),
        P("shard", None),
        P("shard", None, "tp"),
        P(None, "tp"),
        P("tp", "shard"),
        P("shard"),
        P("shard"),
        P("shard"),
        P("shard", "tp"),
        P("tp"),
        P("tp", "shard"),
        P("shard"),
        P("shard"),
        P("shard"),
        P("shard", "ctx", None),
    )
    out_specs = (
        P("shard", "ctx", None),
        P("shard", "ctx", None),
        P("shard", None, "tp"),
        P(None, "tp"),
        P("tp", "shard"),
        P("shard"),
        P("shard"),
        P("shard"),
        P("shard", "tp"),
        P("tp"),
        P("tp", "shard"),
        P("shard"),
        P("shard"),
        P("shard"),
    )
    return jax.shard_map(body, mesh=mesh, in_specs=in_specs, out_specs=out_specs, check_vma=False)
```

```python
import functools

import jax
import jax.numpy as jnp
from jax import lax
from jax.experimental import pallas as pl
from jax.experimental.pallas import tpu as pltpu
from jax.sharding import PartitionSpec as P

HEAD_DIM = 64
LONGEST = 1024
EPSILON = 1e-12
NEGATIVE = -1e30
HBM_SPACE = pl.ANY
FWD, BWD = 24, 14
BF = jnp.bfloat16
F32 = jnp.float32


def dot(a, b):
    return jnp.dot(a, b, preferred_element_type=F32)


def dot_tn(a, b):
    return lax.dot_general(a, b, (((0,), (0,)), ((), ())), preferred_element_type=F32)


def dot_nt(a, b):
    return lax.dot_general(a, b, (((1,), (1,)), ((), ())), preferred_element_type=F32)


def head_stack(tile, first, heads):
    row = lax.broadcasted_iota(jnp.int32, tile.shape, 0)
    parts = []
    for h in range(heads):
        start = first + h * HEAD_DIM
        parts.append(jnp.where((row >= start) & (row < start + HEAD_DIM), tile, jnp.zeros_like(tile)))
    return jnp.concatenate(parts, 1)


def load_blocks(kv_refs, kvb, sem, tok, slot_of):
    copies = [
        pltpu.make_async_copy(ref, kvb.at[pl.ds(pl.multiple_of(slot_of(i) * tok, tok), tok)], sem.at[i])
        for i, ref in enumerate(kv_refs)
    ]
    for copy in copies:
        copy.start()
    for copy in copies:
        copy.wait()


def forward_kernel(slots, heads, tq, tk, rng, q_ref, qseg_ref, kseg_ref, *rest):
    kv_refs = rest[:slots]
    o_ref, lse_ref, aug_ref, all_ref, kvb, st, acc, sem, out_sem = rest[slots:]
    tok = q_ref.shape[0]
    wide = q_ref.shape[1]
    table = 3 * (tok // tq)
    load_blocks(kv_refs, kvb, sem, tok, lambda i: rng[table + i])
    keep = pltpu.make_async_copy(kvb, all_ref, out_sem)
    keep.start()
    vfirst = 2 * heads * HEAD_DIM - wide
    voff = wide - heads * HEAD_DIM
    for t in range(tok // tq):
        lo, hi = rng[3 * t], rng[3 * t + 1]
        qs = pl.multiple_of(rng[3 * t + 2], tq)
        qt = q_ref[pl.ds(qs, tq), :].T
        q3t = head_stack(qt, 0, heads)
        qseg = qseg_ref[t]

        def scan_scores(j, top, q3t=q3t, qseg=qseg):
            at = pl.multiple_of(j * tk, tk)
            scores = dot(kvb[pl.ds(at, tk), :wide], q3t)
            scores = jnp.where(kseg_ref[pl.ds(at, tk), :] == qseg, scores, NEGATIVE)
            st[pl.ds(at, tk), :] = scores
            return jnp.maximum(top, jnp.max(scores.reshape(tk // 8, 8, heads * tq), 0))

        top8 = lax.fori_loop(lo, hi, scan_scores, jnp.full((8, heads * tq), NEGATIVE, F32))
        top = jnp.max(top8, 0, keepdims=True)
        acc[...] = jnp.zeros_like(acc)

        def scan_values(j, total, top=top):
            at = pl.multiple_of(j * tk, tk)
            weights = jnp.exp(st[pl.ds(at, tk), :] - top)
            acc[...] += dot_tn(kvb[pl.ds(at, tk), vfirst:], weights.astype(BF))
            return total + jnp.sum(weights.reshape(tk // 8, 8, heads * tq), 0)

        total8 = lax.fori_loop(lo, hi, scan_values, jnp.zeros((8, heads * tq), F32))
        total = jnp.sum(total8, 0, keepdims=True)
        lse = top + jnp.log(total)
        lse_ref[t] = lse
        full = jnp.concatenate([qt[: wide - voff].astype(F32), spread(-lse, voff, heads, tq)], 0)
        aug_ref[pl.ds(qs, tq), :] = full.T.astype(BF)
        inv = 1.0 / total
        pieces = [jnp.zeros((voff, tq), F32)]
        for h in range(heads):
            rows = slice(voff + h * HEAD_DIM, voff + (h + 1) * HEAD_DIM)
            cols = slice(h * tq, (h + 1) * tq)
            pieces.append(acc[rows, cols] * inv[:, cols])
        o_ref[t * tq : (t + 1) * tq, :] = jnp.concatenate(pieces, 0).T.astype(BF)
    keep.wait()


def thirds(value):
    high = value.astype(BF).astype(F32)
    rest = value - high
    middle = rest.astype(BF).astype(F32)
    return [high, middle, rest - middle]


def spread(rows, count, heads, tq):
    at = lax.broadcasted_iota(jnp.int32, (count, tq), 0)
    out = jnp.zeros((count, tq), F32)
    for h in range(heads):
        for i, piece in enumerate(thirds(rows[:, h * tq : (h + 1) * tq])):
            out = jnp.where(at == 3 * h + i, piece, out)
    return out


def mix_kernel(heads, tq, rng, d1_ref, w_ref, o_ref, do_ref, delta_ref):
    wide = o_ref.shape[1]
    voff = wide - heads * HEAD_DIM
    for t in range(o_ref.shape[0] // tq):
        qs = pl.multiple_of(rng[3 * t + 2], tq)
        grad = dot_nt(w_ref[...], d1_ref[t * tq : (t + 1) * tq, :]).astype(BF).astype(F32)
        prod = grad * o_ref[t * tq : (t + 1) * tq, :].T.astype(F32)
        delta = jnp.concatenate(
            [
                jnp.sum(prod[voff + h * HEAD_DIM : voff + (h + 1) * HEAD_DIM], 0, keepdims=True)
                for h in range(heads)
            ],
            1,
        )
        delta_ref[t] = delta
        full = jnp.concatenate([spread(-delta, voff, heads, tq), grad[voff:]], 0)
        do_ref[pl.ds(qs, tq), :] = full.T.astype(BF)


def query_kernel(heads, tq, tk, rng, q_ref, qseg_ref, kseg_ref, do_ref, lse_ref, delta_ref, *rest):
    kv_ref, dq_ref, bias_ref, kvb, dqt, sem = rest
    tok = q_ref.shape[0]
    wide = q_ref.shape[1]
    load = pltpu.make_async_copy(kv_ref, kvb, sem)
    load.start()
    load.wait()
    vfirst = 2 * heads * HEAD_DIM - wide
    voff = wide - heads * HEAD_DIM
    bias = jnp.zeros((1, wide), F32)
    for t in range(tok // tq):
        lo, hi = rng[3 * t], rng[3 * t + 1]
        qs = pl.multiple_of(rng[3 * t + 2], tq)
        q3t = head_stack(q_ref[pl.ds(qs, tq), :].T, 0, heads)
        do3t = head_stack(do_ref[pl.ds(qs, tq), :].T, voff, heads)
        delta = delta_ref[t]
        qseg = qseg_ref[t]
        lse = lse_ref[t]
        dqt[...] = jnp.zeros_like(dqt)

        def scan_keys(j, carry, q3t=q3t, do3t=do3t, delta=delta, qseg=qseg, lse=lse):
            at = pl.multiple_of(j * tk, tk)
            k = kvb[pl.ds(at, tk), :wide]
            same = kseg_ref[pl.ds(at, tk), :] == qseg
            probs = jnp.where(same, jnp.exp(dot(k, q3t) - lse), 0.0)
            grad = (probs * (dot(kvb[pl.ds(at, tk), vfirst:], do3t) - delta)).astype(BF)
            dqt[...] += dot_tn(k, grad)
            return carry

        lax.fori_loop(lo, hi, scan_keys, 0)
        pieces = []
        for h in range(heads):
            pieces.append(dqt[h * HEAD_DIM : (h + 1) * HEAD_DIM, h * tq : (h + 1) * tq])
        pieces.append(jnp.zeros((wide - heads * HEAD_DIM, tq), F32))
        dq = jnp.concatenate(pieces, 0).T * HEAD_DIM**-0.5
        bias = bias + jnp.sum(dq, 0, keepdims=True)
        dq_ref[pl.ds(qs, tq), :] = dq.astype(BF)
    bias_ref[...] = bias


def key_kernel(slots, row, heads, tq, tk, rng, kv_ref, kseg_ref, qseg_ref, *rest):
    q_refs, do_refs = rest[:slots], rest[slots : 2 * slots]
    dkv_ref, bias_ref, qb, dob, dkt, dvt, qsem, dosem = rest[2 * slots :]
    tok, packed = kv_ref.shape
    wide = qb.shape[1]
    table = 3 * (tok // tq)
    copies = []
    for i in range(slots):
        place = pl.ds(pl.multiple_of(rng[table + i] * tok, tok), tok)
        q_part = q_refs[i].at[pl.ds(row * tok, tok)]
        copies.append(pltpu.make_async_copy(q_part, qb.at[place], qsem.at[i]))
        copies.append(pltpu.make_async_copy(do_refs[i], dob.at[place], dosem.at[i]))
    for copy in copies:
        copy.start()
    for copy in copies:
        copy.wait()
    cols = heads * HEAD_DIM
    vfirst = packed - wide
    voff = wide - cols
    at_row = lax.broadcasted_iota(jnp.int32, (wide, tq), 0)
    bias = jnp.zeros((1, packed), F32)
    for t in range(tok // tq):
        lo, hi = rng[3 * t], rng[3 * t + 1]
        qs = pl.multiple_of(rng[3 * t + 2], tq)

        def stack(tile, first, ones):
            parts = []
            for h in range(heads):
                head = (at_row >= first + h * HEAD_DIM) & (at_row < first + (h + 1) * HEAD_DIM)
                one = (at_row >= ones + 3 * h) & (at_row < ones + 3 * h + 3)
                kept = jnp.where(head, tile, jnp.zeros_like(tile))
                parts.append(jnp.where(one, jnp.ones_like(tile), kept))
            return jnp.concatenate(parts, 1)

        k3t = stack(kv_ref[pl.ds(qs, tq), :wide].T, 0, cols)
        v3t = stack(kv_ref[pl.ds(qs, tq), vfirst:].T, voff, 0)
        kseg = kseg_ref[t]
        dkt[...] = jnp.zeros_like(dkt)
        dvt[...] = jnp.zeros_like(dvt)

        def scan_queries(j, carry, k3t=k3t, v3t=v3t, kseg=kseg):
            at = pl.multiple_of(j * tk, tk)
            q = qb[pl.ds(at, tk), :]
            do = dob[pl.ds(at, tk), :]
            same = qseg_ref[pl.ds(at, tk), :] == kseg
            probs = jnp.where(same, jnp.exp(dot(q, k3t)), 0.0)
            grad = (probs * dot(do, v3t)).astype(BF)
            dkt[...] += dot_tn(q, grad)
            dvt[...] += dot_tn(do, probs.astype(BF))
            return carry

        lax.fori_loop(lo, hi, scan_queries, 0)
        pieces = []
        for ref, first in ((dkt, 0), (dvt, voff)):
            for h in range(heads):
                start = first + h * HEAD_DIM
                pieces.append(ref[start : start + HEAD_DIM, h * tq : (h + 1) * tq])
        grads = jnp.concatenate(pieces, 0).T
        bias = bias + jnp.sum(grads, 0, keepdims=True)
        dkv_ref[pl.ds(qs, tq), :] = grads.astype(BF)
    bias_ref[...] = bias


def input_kernel(rng, dq_ref, dkv_ref, wq_ref, wkv_ref, own_ref, send_ref):
    half = own_ref.shape[0]
    for t, ref in enumerate((own_ref, send_ref)):
        at = pl.ds(pl.multiple_of(rng[3 * t + 2], half), half)
        total = dot_nt(dq_ref[at, :], wq_ref[...]) + dot_nt(dkv_ref[at, :], wkv_ref[...])
        ref[...] = total.astype(ref.dtype)


def weight_kernel(part, axis, rows, keep, *refs):
    own_ref, send_ref = refs[-2:]
    at = 0
    for first, last in keep:
        lefts, rights = refs[:rows], refs[rows : 2 * rows]
        refs = refs[2 * rows :]
        for ref, span in ((own_ref, slice(0, part)), (send_ref, slice(part, None))):
            total = None
            for a, b in zip(lefts, rights):
                term = dot_tn(a[...], b[:, span]) if axis else dot_tn(a[:, span], b[...])
                total = term if total is None else total + term
            if axis:
                ref[at : at + last - first, :] = total[first:last].astype(ref.dtype)
            else:
                ref[...] = total.astype(ref.dtype)
        at += last - first


def weight_grads(pairs, part, axis, keep):
    width = pairs[0][1 if axis else 0][0].shape[1]
    if part % 128 or (width - part) % 128:
        total = jnp.concatenate(
            [
                functools.reduce(lambda p, q: p + q, [dot_tn(a, b) for a, b in zip(*pair)])[
                    (slice(*span) if axis else slice(None))
                ]
                for pair, span in zip(pairs, keep)
            ],
            0,
        )
        if axis:
            return total[:, :part], total[:, part:].astype(BF)
        return total[:part], total[part:].astype(BF)
    kept = sum(last - first for first, last in keep)
    shapes = [(kept, n) if axis else (n, pairs[0][1][0].shape[1]) for n in (part, width - part)]
    operands = [x for lefts, rights in pairs for x in list(lefts) + list(rights)]
    work = sum(2 * a.shape[0] * a.shape[1] * b.shape[1] for lefts, rights in pairs for a, b in zip(lefts, rights))
    vmem = pl.BlockSpec(memory_space=pltpu.VMEM)
    return pl.pallas_call(
        functools.partial(weight_kernel, part, axis, len(pairs[0][0]), keep),
        out_shape=(jax.ShapeDtypeStruct(shapes[0], F32), jax.ShapeDtypeStruct(shapes[1], BF)),
        in_specs=[vmem] * len(operands),
        out_specs=(vmem, vmem),
        cost_estimate=pl.CostEstimate(
            flops=work, transcendentals=0, bytes_accessed=sum(x.size * 2 for x in operands)
        ),
        compiler_params=pltpu.CompilerParams(vmem_limit_bytes=16 << 20),
        name="weight_grads",
    )(*operands)


def last_kernel(rows, part, units, refs_in, own_ref, send_ref):
    dkv_refs, x_refs = refs_in[:rows], refs_in[rows : 2 * rows]
    vec_ref = refs_in[2 * rows]
    unit_refs, q_refs, v_refs = (refs_in[2 * rows + 1 + i * rows :][:rows] for i in range(3))
    packed = dkv_refs[0].shape[1]
    cols = packed // 2
    shape = (own_ref.shape[0] - packed, part)
    at = lax.broadcasted_iota(jnp.int32, shape, 0)
    lane = lax.broadcasted_iota(jnp.int32, (1, part), 1)

    def over(refs):
        return functools.reduce(lambda a, b: a + b, [ref[...] for ref in refs])

    unit_row = over(unit_refs)
    q_row = jnp.concatenate([over(q_refs), jnp.zeros((1, packed - q_refs[0].shape[1]), F32)], 1)
    pieces = [unit_row[:, i : i + packed] for i in range(0, units, packed)]
    pieces.append(jnp.where(lane < cols, q_row, over(v_refs)))
    for ref, span in ((own_ref, slice(0, part)), (send_ref, slice(part, None))):
        total = None
        for a, b in zip(dkv_refs, x_refs):
            term = dot_tn(a[...], b[:, span])
            total = term if total is None else total + term
        ref[:packed, :] = total.astype(ref.dtype)
        block = jnp.concatenate([vec_ref[:, span], jnp.zeros((shape[0] - 8, part), F32)], 0)
        for i, piece in enumerate(pieces):
            block = jnp.where(at == 8 + i, piece, block)
        ref[packed:, :] = block.astype(ref.dtype)


def last_grads(dkvs, xs, d_vec, d_units, d_q, d_v, part, lines):
    rows = len(dkvs)
    packed = dkvs[0].shape[1]
    units = d_units[0].shape[1]
    operands = list(dkvs) + list(xs) + [d_vec] + list(d_units) + list(d_q) + list(d_v)
    vmem = pl.BlockSpec(memory_space=pltpu.VMEM)
    shape = (packed + lines, part)

    def kernel(*refs):
        last_kernel(rows, part, units, refs[:-2], *refs[-2:])

    return pl.pallas_call(
        kernel,
        out_shape=(jax.ShapeDtypeStruct(shape, F32), jax.ShapeDtypeStruct(shape, BF)),
        in_specs=[vmem] * len(operands),
        out_specs=(vmem, vmem),
        cost_estimate=pl.CostEstimate(
            flops=4 * rows * packed * part * xs[0].shape[0],
            transcendentals=0,
            bytes_accessed=sum(x.size * 2 for x in operands),
        ),
        compiler_params=pltpu.CompilerParams(vmem_limit_bytes=16 << 20),
        name="last_grads",
    )(*operands)


def make_attention(slots, heads, tok, wide, packed, width, n_rows):
    tq = tok // 2
    tk = tq
    vmem = pl.BlockSpec(memory_space=pltpu.VMEM)
    smem = pl.BlockSpec(memory_space=pltpu.SMEM)
    hbm = pl.BlockSpec(memory_space=HBM_SPACE)
    pairs = 2 * heads * tok * 1024 * wide
    def grant(size):
        return pltpu.CompilerParams(vmem_limit_bytes=size << 20)

    params = grant(BWD)
    rowed = jax.ShapeDtypeStruct((2, 1, heads * tq), F32)
    tokens = jax.ShapeDtypeStruct((tok, wide), BF)

    def cost(products, exps):
        return pl.CostEstimate(
            flops=products * pairs,
            transcendentals=exps * heads * tok * 1024,
            bytes_accessed=slots * tok * packed * 2,
        )

    forward = pl.pallas_call(
        functools.partial(forward_kernel, slots, heads, tq, tk),
        out_shape=(tokens, rowed, tokens, jax.ShapeDtypeStruct((slots * tok, packed), BF)),
        in_specs=[smem, vmem, vmem, vmem] + [hbm] * slots,
        out_specs=(vmem, vmem, vmem, pl.BlockSpec(memory_space=pltpu.HBM)),
        scratch_shapes=[
            pltpu.VMEM((slots * tok, packed), BF),
            pltpu.VMEM((slots * tok, heads * tq), F32),
            pltpu.VMEM((wide, heads * tq), F32),
            pltpu.SemaphoreType.DMA((slots,)),
            pltpu.SemaphoreType.DMA,
        ],
        cost_estimate=cost(2, 1),
        compiler_params=grant(FWD),
        name="attend_forward",
    )
    mix_back = pl.pallas_call(
        functools.partial(mix_kernel, heads, tq),
        out_shape=(tokens, rowed),
        in_specs=[smem, vmem, vmem, vmem],
        out_specs=(vmem, vmem),
        cost_estimate=pl.CostEstimate(
            flops=2 * tok * wide * width, transcendentals=0, bytes_accessed=tok * (2 * wide + width) * 2
        ),
        compiler_params=params,
        name="mix_back",
    )
    query_back = pl.pallas_call(
        functools.partial(query_kernel, heads, tq, tk),
        out_shape=(tokens, jax.ShapeDtypeStruct((1, wide), F32)),
        in_specs=[smem] + [vmem] * 6 + [pl.BlockSpec(memory_space=pltpu.HBM)],
        out_specs=(vmem, vmem),
        scratch_shapes=[
            pltpu.VMEM((slots * tok, packed), BF),
            pltpu.VMEM((wide, heads * tq), F32),
            pltpu.SemaphoreType.DMA,
        ],
        cost_estimate=cost(3, 1),
        compiler_params=params,
        name="query_back",
    )
    key_back = [
        pl.pallas_call(
            functools.partial(key_kernel, slots, row, heads, tq, tk),
            out_shape=(
                jax.ShapeDtypeStruct((tok, packed), BF),
                jax.ShapeDtypeStruct((1, packed), F32),
            ),
            in_specs=[smem] + [vmem] * 3 + [hbm] * (2 * slots),
            out_specs=(vmem, vmem),
            scratch_shapes=[
                pltpu.VMEM((slots * tok, wide), BF),
                pltpu.VMEM((slots * tok, wide), BF),
                pltpu.VMEM((wide, heads * tq), F32),
                pltpu.VMEM((wide, heads * tq), F32),
                pltpu.SemaphoreType.DMA((slots,)),
                pltpu.SemaphoreType.DMA((slots,)),
            ],
            cost_estimate=cost(4, 1),
            compiler_params=params,
            name="key_back",
        )
        for row in range(n_rows)
    ]
    input_back = pl.pallas_call(
        input_kernel,
        out_shape=(
            jax.ShapeDtypeStruct((tq, width), F32),
            jax.ShapeDtypeStruct((tq, width), BF),
        ),
        in_specs=[smem] + [vmem] * 4,
        out_specs=(vmem, vmem),
        cost_estimate=pl.CostEstimate(
            flops=2 * tok * (wide + packed) * width,
            transcendentals=0,
            bytes_accessed=tok * (wide + packed + width) * 4,
        ),
        compiler_params=params,
        name="input_back",
    )
    return forward, mix_back, query_back, key_back, input_back


def after(value, *others):
    return lax.optimization_barrier((value,) + others)[0]


def make_body(n_shard, n_ctx, n_tp):
    bits = [1 << i for i in range(n_tp.bit_length() - 1)]
    ctx_steps = [1 << i for i in range(n_ctx.bit_length() - 1)]
    ctx_whole = not n_ctx & (n_ctx - 1)

    def exchange(value, axis, size, bit):
        return lax.ppermute(value, axis, [(i, i ^ bit) for i in range(size) if i ^ bit < size])

    def even_swap(value):
        return exchange(value, "ctx", n_ctx, 1)

    def odd_swap(value):
        pairs = []
        for i in range(1, n_ctx - 1, 2):
            pairs += [(i, i + 1), (i + 1, i)]
        return lax.ppermute(value, "ctx", pairs)

    def swap(value, kind):
        return odd_swap(value) if kind else even_swap(value)

    ctx_count = max(2 * len(ctx_steps) - 1, 1)

    def ctx_step(cur, step):
        ci = lax.axis_index("ctx")
        count = len(ctx_steps)
        bit = ctx_steps[step] if step < count else ctx_steps[2 * count - 2 - step]
        up = (ci // bit) % 2
        if step == count - 1:
            cur = cur.astype(BF)
            return (cur.astype(F32) + exchange(cur, "ctx", n_ctx, bit).astype(F32)).astype(BF)
        if step < count:
            half = cur.shape[0] // 2
            send = lax.dynamic_slice_in_dim(cur, (1 - up) * half, half, 0).astype(BF)
            keep = lax.dynamic_slice_in_dim(cur, up * half, half, 0)
            return keep + exchange(send, "ctx", n_ctx, bit).astype(F32)
        other = exchange(cur, "ctx", n_ctx, bit)
        return jnp.where(up == 0, jnp.concatenate([cur, other], 0), jnp.concatenate([other, cur], 0))

    def body(
        hidden_in,
        segment_ids,
        qkv_weight,
        qv_bias,
        out_weight,
        out_bias,
        first_gain,
        first_shift,
        inner_weight,
        inner_bias,
        outer_weight,
        outer_bias,
        second_gain,
        second_shift,
        cotangent,
    ):
        rows, tok, width = hidden_in.shape
        part = width // n_shard
        cols = qkv_weight.shape[2]
        heads = cols // HEAD_DIM
        units = inner_weight.shape[1]
        wide = -(-cols // 128) * 128
        pad = wide - cols
        packed = 2 * cols
        half = tok // 2
        every = list(range(rows))
        si = lax.axis_index("shard")
        ci = lax.axis_index("ctx")
        core = lax.axis_index("tp") % 2
        reach = min(n_ctx - 1, 1 + (LONGEST - 2) // tok)
        slots = 2 * reach + 1
        attend_fwd, mix_back, query_back, key_back, input_back = make_attention(
            slots, heads, tok, wide, packed, width, rows
        )

        def rolled(value, axis):
            if n_shard == 2:
                first = lax.slice_in_dim(value, 0, part, axis=axis)
                second = lax.slice_in_dim(value, part, width, axis=axis)
                return jnp.where(si == 0, value, jnp.concatenate([second, first], axis))
            return jnp.roll(value, -si * part, axis)

        def unrolled(value, axis):
            if n_shard == 2:
                return rolled(value, axis)
            return jnp.roll(value, si * part, axis)

        def others(own, axis):
            if n_shard == 2:
                return exchange(own, "shard", 2, 1)
            whole = rolled(lax.all_gather(own, "shard", axis=axis, tiled=True), axis)
            return lax.slice_in_dim(whole, part, width, axis=axis)

        def gathered(own, axis):
            if n_shard == 2:
                return jnp.concatenate([own, exchange(own, "shard", 2, 1)], axis)
            return rolled(lax.all_gather(own, "shard", axis=axis, tiled=True), axis)

        def gathered_in_order(own):
            if n_shard == 2:
                other = exchange(own, "shard", 2, 1)
                return jnp.where(
                    si == 0, jnp.concatenate([own, other], 0), jnp.concatenate([other, own], 0)
                )
            return lax.all_gather(own, "shard", axis=0, tiled=True)

        def own_half(value):
            return lax.dynamic_slice_in_dim(value, core * half, half, 0)

        def core_sum(own, send):
            total = own + exchange(send.astype(BF), "tp", n_tp, 1).astype(F32)
            return total.astype(BF) if len(bits) > 1 else total

        def chip_send(name):
            if len(bits) == 2:
                box["y" + name] = exchange(box[name], "tp", n_tp, bits[1])

        def chip_total(name):
            total = box[name].astype(F32)
            if len(bits) == 2:
                return total + box["y" + name].astype(F32)
            for bit in bits[1:]:
                total = total.astype(BF)
                total = total.astype(F32) + exchange(total, "tp", n_tp, bit).astype(F32)
            return total

        def stage_sum(name, own, send, beside, *names):
            if beside and len(bits) == 2:
                names += ("y" + beside,)
            if names:
                own, send = hold_all([own, send], *names)
            box[name] = core_sum(own, send)
            chip_send(name)

        def both_halves(own):
            return jnp.concatenate([own, exchange(own, "tp", n_tp, 1)], 0)

        def in_order(pair):
            first, second = pair[:half], pair[half:]
            return jnp.where(core == 0, pair, jnp.concatenate([second, first], 0))

        box = {}

        def hold_all(values, *names):
            kept = lax.optimization_barrier(tuple(values) + tuple(box[n] for n in names))
            box.update(zip(names, kept[len(values) :]))
            return kept[: len(values)]

        def hold(value, *names):
            return hold_all([value], *names)[0]

        box["kv_own"] = qkv_weight[:, 1:].astype(BF).reshape(part, packed)
        box["w_kv"] = gathered_in_order(box["kv_own"])
        q_own = jnp.pad(qkv_weight[:, 0].astype(BF), ((0, 0), (0, pad)))
        q_own = hold(q_own, "w_kv")
        w_kv = box["w_kv"]
        w_q = gathered_in_order(q_own)

        before = jnp.full((rows, reach * tok), -1, jnp.int32)
        behind = jnp.full((rows, reach * tok), 1 << 20, jnp.int32)
        padded = jnp.concatenate([before, segment_ids, behind], 1)
        key_seg = lax.dynamic_slice_in_dim(padded, ci * tok, slots * tok, 1)
        q_seg = lax.dynamic_slice_in_dim(segment_ids, ci * tok, tok, 1)
        q_seg = q_seg.reshape(rows, 2, half)
        q_seg = jnp.where(core == 0, q_seg, q_seg[:, ::-1])
        low = jnp.sum(key_seg[:, None, :] < q_seg[:, :, :1], -1) // half
        high = (jnp.sum(key_seg[:, None, :] <= q_seg[:, :, -1:], -1) + half - 1) // half
        begin = jnp.broadcast_to(jnp.stack([core * half, (1 - core) * half])[None], (rows, 2))
        ranges = jnp.stack([low, high, begin], -1).reshape(rows, 6).astype(jnp.int32)
        side = 1 - 2 * (ci % 2)
        places = [jnp.int32(reach) + 0 * side]
        for d in range(1, reach + 1):
            places += [reach + d * side, reach - d * side]
        places = jnp.broadcast_to(jnp.stack(places)[None], (rows, slots))
        ranges = jnp.concatenate([ranges, places.astype(jnp.int32)], 1)
        q_seg3 = jnp.tile(q_seg[:, :, None, :], (1, 1, 1, heads))
        key_col = key_seg[:, :, None]

        v_bias = jnp.concatenate([jnp.zeros((cols,), F32), qv_bias[1]])
        q_bias = jnp.pad(qv_bias[0], (0, pad))

        def halo(own):
            found = [own]
            last = [own, own]
            for d in range(1, reach + 1):
                even, odd = even_swap(last[1]), odd_swap(last[0])
                found += [even, odd]
                last = [even, odd]
            return found

        def send_blocks(name, d):
            last = [box[name]] * 2 if d == 1 else [box[f"{name}_{2 * d - 4}"], box[f"{name}_{2 * d - 3}"]]
            box[f"{name}_{2 * d - 2}"] = even_swap(last[1])
            box[f"{name}_{2 * d - 1}"] = odd_swap(last[0])

        def send_kv(r, first):
            for d in range(first, reach + 1):
                send_blocks(f"kv{r}", d)

        for r in every:
            box[f"kv{r}"] = (dot(hidden_in[r], w_kv) + v_bias).astype(BF)
            if r:
                box[f"kv{r}"] = hold(box[f"kv{r}"], f"kv{r - 1}_0", f"kv{r - 1}_1")
            else:
                send_kv(0, 1)
                continue
            send_blocks(f"kv{r}", 1)
        q = [
            ((dot(hidden_in[r], w_q) + q_bias).astype(BF) * jnp.asarray(HEAD_DIM**-0.5, BF))
            for r in every
        ]

        vec_own = [out_bias, first_gain, first_shift, outer_bias, second_gain, second_shift]
        vec_own = jnp.concatenate([v[None] for v in vec_own] + [jnp.zeros((10, part), F32)], 0)
        wo_own = hold(jnp.concatenate([out_weight, vec_own], 0).astype(BF), "kv0")
        wo_vec = gathered(wo_own, 1)
        w_out = jnp.concatenate([jnp.zeros((pad, width), BF), wo_vec[:cols]], 0)
        vectors = wo_vec[cols : cols + 6].astype(F32)
        in_own = hold(inner_weight, "kv0").astype(BF)
        box["w_in"] = others(in_own, 0)
        outer_own = hold(outer_weight, "w_in").astype(BF)
        box["w_outer"] = others(outer_own, 1)
        bo, g1, s1, bd, g2, s2 = [vectors[i] for i in range(6)]

        def normed(summed):
            average = jnp.mean(summed, -1, keepdims=True)
            centered = summed - average
            variance = jnp.mean(centered * centered, -1, keepdims=True)
            scale = lax.rsqrt(variance + EPSILON)
            return centered * scale, scale

        def norm_back(grad, gain, hat, scale):
            inner = grad * gain
            return scale * (
                inner
                - jnp.mean(inner, -1, keepdims=True)
                - hat * jnp.mean(inner * hat, -1, keepdims=True)
            )

        x_roll = [rolled(hidden_in[r], 1) for r in every]
        x_res = [own_half(x_roll[r]).astype(F32) for r in every]
        cots = [rolled(own_half(cotangent[r]), 1).astype(F32) for r in every]

        ready = {0: ["w_in"], rows - 1: ["w_outer"]}

        def before(r, this, last):
            return [f"{this}{r - 1}"] if r else ([f"{last}{rows - 1}"] if last else [])

        o, lse, aug, kv_all = ([None] * rows for _ in range(4))
        for r in every:
            query = hold(q[r], *before(r, "a", None), *ready.get(r, []))
            blocks = [box[f"kv{r}"]] + [box[f"kv{r}_{i}"] for i in range(2 * reach)]
            out = attend_fwd(ranges[r], query, q_seg3[r], key_col[r], *blocks)
            if r < rows - 1:
                out = hold_all(out, f"kv{r + 1}_0", f"kv{r + 1}_1")
                send_kv(r + 1, 2)
            o[r], lse[r], aug[r], kv_all[r] = out
            send = dot(o[r][half:], w_out)
            stage_sum(f"a{r}", dot(o[r][:half], w_out), send, f"a{r - 1}" if r else None)
        q_halo = halo(jnp.concatenate(aug, 0))
        for i, block in enumerate(q_halo[1:]):
            box[f"q{i}"] = block

        hat1, scale1, y1, y1b = [None] * rows, [None] * rows, [None] * rows, [None] * rows
        u, slope = [None] * rows, [None] * rows
        for r in every:
            total = hold(chip_total(f"a{r}"), *before(r, "b", "a"))
            hat1[r], scale1[r] = normed(x_res[r] + total + bo)
            y1[r] = hat1[r] * g1 + s1
            y1b[r] = both_halves(y1[r].astype(BF))
            if not r:
                w_in = jnp.concatenate([in_own, box["w_in"]], 0)
                w_outer = jnp.concatenate([outer_own, box["w_outer"]], 1)
            a = dot(y1b[r], w_in) + inner_bias
            cdf = 0.5 * (1.0 + lax.erf(a * (0.5**0.5)))
            u[r] = (a * cdf).astype(BF)
            slope[r] = (cdf + a * jnp.exp(-0.5 * a * a) * 0.3989422804014327).astype(BF)
            send = dot(u[r][half:], w_outer)
            arrived = ["q0", "q1"] if r == rows - 1 else []
            stage_sum(f"b{r}", dot(u[r][:half], w_outer), send, f"b{r - 1}" if r else f"a{rows - 1}", *arrived)

        result, dh2, d2b, dab = ([None] * rows for _ in range(4))
        d_vec2, d_bi = [None] * rows, [None] * rows
        for r in every:
            total = hold(chip_total(f"b{r}"), *before(r, "c", "b"))
            hat2, scale2 = normed(y1[r] + total + bd)
            c = cots[r]
            result[r] = (hat2 * g2 + s2).astype(BF)
            dh2[r] = norm_back(c, g2, hat2, scale2)
            d2b[r] = both_halves(dh2[r].astype(BF))
            d_vec2[r] = [jnp.sum(v, 0, keepdims=True) for v in (dh2[r], c * hat2, c)]
            da = dot_nt(d2b[r], w_outer) * slope[r].astype(F32)
            d_bi[r] = jnp.sum(da, 0, keepdims=True)
            dab[r] = da.astype(BF)
            send = dot_nt(dab[r][half:], w_in)
            arrived = [f"q{i}" for i in range(2, 2 * reach)] if r == rows - 1 else []
            stage_sum(f"c{r}", dot_nt(dab[r][:half], w_in), send, f"c{r - 1}" if r else f"b{rows - 1}", *arrived)

        def over_rows(terms):
            return functools.reduce(lambda p, q: p + q, terms)

        def shard_send(name, send):
            box[name] = exchange(send, "shard", 2, 1) if n_shard == 2 else send

        def shard_total(name, own, axis):
            if n_shard == 2:
                return own + box[name].astype(F32)
            whole = unrolled(jnp.concatenate([own, box[name].astype(F32)], axis), axis)
            return lax.psum_scatter(whole, "shard", scatter_dimension=axis, tiled=True)

        def advance(name):
            value, step = box[name], at_step.get(name, 0)
            if ctx_whole and step < ctx_count:
                box[name] = ctx_step(value, step)
            elif not step:
                box[name] = lax.psum(value, "ctx")
            at_step[name] = step + 1

        def finish(name):
            while at_step.get(name, 0) < ctx_count:
                advance(name)
            return box[name].astype(F32)

        at_step = {}

        dh1, d1b, d_vec1, dos, deltas = ([None] * rows for _ in range(5))

        def stage4(r, *names):
            total = hold(chip_total(f"c{r}"), *names)
            dy1 = dh2[r] + total
            dh1[r] = norm_back(dy1, g1, hat1[r], scale1[r])
            d1b[r] = both_halves(dh1[r].astype(BF))
            d_vec1[r] = [jnp.sum(v, 0, keepdims=True) for v in (dh1[r], dy1 * hat1[r], dy1)]
            box[f"do{r}"], deltas[r] = mix_back(ranges[r], d1b[r], w_out, o[r])

        gate = [f"c{rows - 1}"]
        for r in every:
            stage4(r, *gate)
            if r:
                box[f"do{r}"] = hold(box[f"do{r}"], *[f"do{r - 1}_{i}" for i in range(2, 2 * reach)])
            send_blocks(f"do{r}", 1)
            gate = [f"do{r}"]
            if not r:
                lefts = [hold(u[0], "do0")] + u[1:]
                own_first, send_first = weight_grads(
                    [(lefts, d2b), (dab, y1b)], part, 1, [(0, units), (0, units)]
                )
                box["send_first"] = send_first
                names = ["do0_0", "do0_1"] + ([f"yc{rows - 1}"] if len(bits) == 2 else [])
                own_first, box["send_first"] = hold_all([own_first, send_first], *names)
                shard_send("x_first", box["send_first"])
                gate = ["send_first"]
            elif r < rows - 1:
                box[f"do{r}"] = hold(box[f"do{r}"], f"do{r}_0", f"do{r}_1")
            if r < rows - 1:
                for d in range(2, reach + 1):
                    send_blocks(f"do{r}", d)

        dqs, biases, dkvs, d_bv = ([None] * rows for _ in range(4))
        for r in every:
            query = hold(aug[r], f"dq{r - 1}" if r else f"do{rows - 1}")
            dq, biases[r] = query_back(
                ranges[r], query, q_seg3[r], key_col[r], box[f"do{r}"], lse[r], deltas[r], kv_all[r]
            )
            if not r:
                names = [f"do{rows - 1}_0", f"do{rows - 1}_1", "x_first"]
            else:
                names = [f"do{rows - 1}_{j}" for j in range(2, 2 * reach)] + ["first"] if r == rows - 1 else []
            box[f"dq{r}"] = hold(dq, *names)
            if not r:
                for d in range(2, reach + 1):
                    send_blocks(f"do{rows - 1}", d)
                box["first"] = shard_total("x_first", own_first, 1)
                advance("first")
        dqs = [box[f"dq{r}"] for r in every]
        own_mix, box["send_mix"] = weight_grads(
            [(o, d1b), (dqs, x_roll)], part, 1, [(pad, wide), (0, cols)]
        )
        shard_send("x_mix", box["send_mix"])
        advance("first")
        for r in every:
            own = hold(box[f"kv{r}"], *(["send_mix"] if not r else [f"dkv{r - 1}"]))
            blocks = [box[f"do{r}"]] + [box[f"do{r}_{i}"] for i in range(2 * reach)]
            q_blocks = q_halo[:1] + [box[f"q{i}"] for i in range(2 * reach)]
            dkv, d_bv[r] = key_back[r](ranges[r], own, q_seg3[r], key_col[r], *q_blocks, *blocks)
            box[f"dkv{r}"] = hold(dkv, *(["x_mix"] if not r else ["mix"] if r == 1 else []))
            if not r:
                box["mix"] = shard_total("x_mix", own_mix, 1)
                advance("mix")
        dkvs = [box[f"dkv{r}"] for r in every]
        for r in every:
            own, send = input_back(ranges[r], dqs[r], dkvs[r], w_q, w_kv)
            if r == rows - 1:
                own, send = hold_all([own, send], "first")
            box[f"h{r}"] = core_sum(own, send)
            chip_send(f"h{r}")

        d_vec = jnp.concatenate(
            [over_rows(v) for v in zip(*d_vec1)]
            + [over_rows(v) for v in zip(*d_vec2)]
            + [jnp.zeros((2, width), F32)],
            0,
        )
        d_vec = d_vec + exchange(d_vec, "tp", n_tp, 1)
        if n_shard == 2 and ctx_whole and part == packed and units % packed == 0:
            lines = 8 + units // packed + 1
            lines += (-(packed + lines)) % (16 * n_ctx)
            own_last, send_last = last_grads(dkvs, x_roll, d_vec, d_bi, biases, d_bv, part, lines)
            shard_send("x_last", send_last)
            box["last"] = shard_total("x_last", own_last, 1)
            advance("last")
            if at_step["mix"] < ctx_count:
                advance("mix")
                box["mix"] = hold(box["mix"], "last")
            g_last = finish("last")
            vec = g_last[packed : packed + 6]
            d_units = g_last[packed + 8 : packed + 8 + units // packed].reshape(units)
            d_qv = g_last[packed + 8 + units // packed].reshape(2, cols)
        else:
            own_last, send_last = weight_grads([(dkvs, x_roll)], part, 1, [(0, packed)])
            d_qv = jnp.concatenate([over_rows(biases)[:, :cols], over_rows(d_bv)[:, cols:]], 1)
            vec = lax.psum_scatter(unrolled(d_vec, 1), "shard", scatter_dimension=1, tiled=True)
            vec = lax.psum(vec, "ctx")
            d_units = lax.psum(over_rows(d_bi)[0], ("shard", "ctx"))
            d_qv = lax.psum(d_qv[0], ("shard", "ctx")).reshape(2, cols)
            shard_send("x_last", send_last)
            box["last"] = shard_total("x_last", own_last, 1)
            g_last = finish("last")
        g_first = finish("first")
        g_mix = finish("mix")
        grad_qkv = jnp.concatenate([g_mix[cols:], g_last[:packed]], 0).T.reshape(part, 3, cols)

        hidden_grads = []
        for r in every:
            total = chip_total(f"h{r}")
            grad = (unrolled(dh1[r], 1) + total).astype(BF)
            hidden_grads.append(in_order(both_halves(grad)))
        mine = hold(jnp.stack([unrolled(result[r], 1) for r in every]), "h0")
        theirs = exchange(mine, "tp", n_tp, 1)
        outputs = jnp.where(
            core == 0, jnp.concatenate([mine, theirs], 1), jnp.concatenate([theirs, mine], 1)
        )

        return (
            outputs,
            jnp.stack(hidden_grads),
            grad_qkv,
            d_qv,
            g_mix[:cols],
            vec[0],
            vec[1],
            vec[2],
            g_first[units : 2 * units].T,
            d_units,
            g_first[:units],
            vec[3],
            vec[4],
            vec[5],
        )

    return body


def solution(mesh):
    body = make_body(mesh.shape["shard"], mesh.shape["ctx"], mesh.shape["tp"])
    in_specs = (
        P("shard", "ctx", None),
        P("shard", None),
        P("shard", None, "tp"),
        P(None, "tp"),
        P("tp", "shard"),
        P("shard"),
        P("shard"),
        P("shard"),
        P("shard", "tp"),
        P("tp"),
        P("tp", "shard"),
        P("shard"),
        P("shard"),
        P("shard"),
        P("shard", "ctx", None),
    )
    out_specs = (
        P("shard", "ctx", None),
        P("shard", "ctx", None),
        P("shard", None, "tp"),
        P(None, "tp"),
        P("tp", "shard"),
        P("shard"),
        P("shard"),
        P("shard"),
        P("shard", "tp"),
        P("tp"),
        P("tp", "shard"),
        P("shard"),
        P("shard"),
        P("shard"),
    )
    return jax.shard_map(body, mesh=mesh, in_specs=in_specs, out_specs=out_specs, check_vma=False)
```

```python
import functools

import jax
import jax.numpy as jnp
from jax import lax
from jax.experimental import pallas as pl
from jax.experimental.pallas import tpu as pltpu
from jax.sharding import PartitionSpec as P

HEAD_DIM = 64
LONGEST = 1024
EPSILON = 1e-12
NEGATIVE = -1e30
HBM_SPACE = pl.ANY
FWD, BWD = 24, 14
BF = jnp.bfloat16
F32 = jnp.float32


def dot(a, b):
    return jnp.dot(a, b, preferred_element_type=F32)


def dot_tn(a, b):
    return lax.dot_general(a, b, (((0,), (0,)), ((), ())), preferred_element_type=F32)


def dot_nt(a, b):
    return lax.dot_general(a, b, (((1,), (1,)), ((), ())), preferred_element_type=F32)


def head_stack(tile, first, heads):
    row = lax.broadcasted_iota(jnp.int32, tile.shape, 0)
    parts = []
    for h in range(heads):
        start = first + h * HEAD_DIM
        parts.append(jnp.where((row >= start) & (row < start + HEAD_DIM), tile, jnp.zeros_like(tile)))
    return jnp.concatenate(parts, 1)


def load_blocks(kv_refs, kvb, sem, tok, slot_of):
    copies = [
        pltpu.make_async_copy(ref, kvb.at[pl.ds(pl.multiple_of(slot_of(i) * tok, tok), tok)], sem.at[i])
        for i, ref in enumerate(kv_refs)
    ]
    for copy in copies:
        copy.start()
    for copy in copies:
        copy.wait()


def forward_kernel(slots, heads, tq, tk, rng, q_ref, qseg_ref, kseg_ref, *rest):
    kv_refs = rest[:slots]
    o_ref, lse_ref, aug_ref, all_ref, kvb, st, acc, sem, out_sem = rest[slots:]
    tok = q_ref.shape[0]
    wide = q_ref.shape[1]
    table = 3 * (tok // tq)
    load_blocks(kv_refs, kvb, sem, tok, lambda i: rng[table + i])
    keep = pltpu.make_async_copy(kvb, all_ref, out_sem)
    keep.start()
    vfirst = 2 * heads * HEAD_DIM - wide
    voff = wide - heads * HEAD_DIM

    def one_tile(t, carry):
        lo, hi = rng[3 * t], rng[3 * t + 1]
        qs = pl.multiple_of(rng[3 * t + 2], tq)
        qt = q_ref[pl.ds(qs, tq), :].T
        q3t = head_stack(qt, 0, heads)
        qseg = qseg_ref[t]

        def scan_scores(j, top):
            at = pl.multiple_of(j * tk, tk)
            scores = dot(kvb[pl.ds(at, tk), :wide], q3t)
            scores = jnp.where(kseg_ref[pl.ds(at, tk), :] == qseg, scores, NEGATIVE)
            st[pl.ds(at, tk), :] = scores
            return jnp.maximum(top, jnp.max(scores.reshape(tk // 8, 8, heads * tq), 0))

        top8 = lax.fori_loop(lo, hi, scan_scores, jnp.full((8, heads * tq), NEGATIVE, F32))
        top = jnp.max(top8, 0, keepdims=True)
        acc[...] = jnp.zeros_like(acc)

        def scan_values(j, total):
            at = pl.multiple_of(j * tk, tk)
            weights = jnp.exp(st[pl.ds(at, tk), :] - top)
            acc[...] += dot_tn(kvb[pl.ds(at, tk), vfirst:], weights.astype(BF))
            return total + jnp.sum(weights.reshape(tk // 8, 8, heads * tq), 0)

        total8 = lax.fori_loop(lo, hi, scan_values, jnp.zeros((8, heads * tq), F32))
        total = jnp.sum(total8, 0, keepdims=True)
        lse = top + jnp.log(total)
        lse_ref[t] = lse
        full = jnp.concatenate([qt[: wide - voff].astype(F32), spread(-lse, voff, heads, tq)], 0)
        aug_ref[pl.ds(qs, tq), :] = full.T.astype(BF)
        inv = 1.0 / total
        pieces = [jnp.zeros((voff, tq), F32)]
        for h in range(heads):
            rows = slice(voff + h * HEAD_DIM, voff + (h + 1) * HEAD_DIM)
            cols = slice(h * tq, (h + 1) * tq)
            pieces.append(acc[rows, cols] * inv[:, cols])
        o_ref[pl.ds(pl.multiple_of(t * tq, tq), tq), :] = jnp.concatenate(pieces, 0).T.astype(BF)
        return carry

    lax.fori_loop(0, tok // tq, one_tile, 0)
    keep.wait()


def thirds(value):
    high = value.astype(BF).astype(F32)
    rest = value - high
    middle = rest.astype(BF).astype(F32)
    return [high, middle, rest - middle]


def spread(rows, count, heads, tq):
    at = lax.broadcasted_iota(jnp.int32, (count, tq), 0)
    out = jnp.zeros((count, tq), F32)
    for h in range(heads):
        for i, piece in enumerate(thirds(rows[:, h * tq : (h + 1) * tq])):
            out = jnp.where(at == 3 * h + i, piece, out)
    return out


def mix_kernel(heads, tq, rng, d1_ref, w_ref, o_ref, do_ref, delta_ref):
    wide = o_ref.shape[1]
    voff = wide - heads * HEAD_DIM

    def one_tile(t, carry):
        qs = pl.multiple_of(rng[3 * t + 2], tq)
        at = pl.ds(pl.multiple_of(t * tq, tq), tq)
        grad = dot_nt(w_ref[...], d1_ref[at, :]).astype(BF).astype(F32)
        prod = grad * o_ref[at, :].T.astype(F32)
        delta = jnp.concatenate(
            [
                jnp.sum(prod[voff + h * HEAD_DIM : voff + (h + 1) * HEAD_DIM], 0, keepdims=True)
                for h in range(heads)
            ],
            1,
        )
        delta_ref[t] = delta
        full = jnp.concatenate([spread(-delta, voff, heads, tq), grad[voff:]], 0)
        do_ref[pl.ds(qs, tq), :] = full.T.astype(BF)
        return carry

    lax.fori_loop(0, o_ref.shape[0] // tq, one_tile, 0)


def query_kernel(heads, tq, tk, rng, q_ref, qseg_ref, kseg_ref, do_ref, lse_ref, delta_ref, *rest):
    kv_ref, dq_ref, bias_ref, kvb, dqt, sem = rest
    tok = q_ref.shape[0]
    wide = q_ref.shape[1]
    load = pltpu.make_async_copy(kv_ref, kvb, sem)
    load.start()
    load.wait()
    vfirst = 2 * heads * HEAD_DIM - wide
    voff = wide - heads * HEAD_DIM

    def one_tile(t, bias):
        lo, hi = rng[3 * t], rng[3 * t + 1]
        qs = pl.multiple_of(rng[3 * t + 2], tq)
        q3t = head_stack(q_ref[pl.ds(qs, tq), :].T, 0, heads)
        do3t = head_stack(do_ref[pl.ds(qs, tq), :].T, voff, heads)
        delta = delta_ref[t]
        qseg = qseg_ref[t]
        lse = lse_ref[t]
        dqt[...] = jnp.zeros_like(dqt)

        def scan_keys(j, carry):
            at = pl.multiple_of(j * tk, tk)
            k = kvb[pl.ds(at, tk), :wide]
            same = kseg_ref[pl.ds(at, tk), :] == qseg
            probs = jnp.where(same, jnp.exp(dot(k, q3t) - lse), 0.0)
            grad = (probs * (dot(kvb[pl.ds(at, tk), vfirst:], do3t) - delta)).astype(BF)
            dqt[...] += dot_tn(k, grad)
            return carry

        lax.fori_loop(lo, hi, scan_keys, 0)
        pieces = []
        for h in range(heads):
            pieces.append(dqt[h * HEAD_DIM : (h + 1) * HEAD_DIM, h * tq : (h + 1) * tq])
        pieces.append(jnp.zeros((wide - heads * HEAD_DIM, tq), F32))
        dq = jnp.concatenate(pieces, 0).T * HEAD_DIM**-0.5
        added = jnp.sum(dq, 0, keepdims=True)
        dq_ref[pl.ds(qs, tq), :] = dq.astype(BF)
        return bias + added

    bias_ref[...] = lax.fori_loop(0, tok // tq, one_tile, jnp.zeros((1, wide), F32))


def key_kernel(slots, heads, tq, tk, rng, kv_ref, kseg_ref, qseg_ref, *rest):
    q_refs, do_refs = rest[:slots], rest[slots : 2 * slots]
    dkv_ref, bias_ref, qb, dob, dkt, dvt, qsem, dosem = rest[2 * slots :]
    tok, packed = kv_ref.shape
    wide = qb.shape[1]
    table = 3 * (tok // tq)
    copies = []
    for i in range(slots):
        place = pl.ds(pl.multiple_of(rng[table + i] * tok, tok), tok)
        q_part = q_refs[i].at[pl.ds(pl.multiple_of(rng[table + slots] * tok, tok), tok)]
        copies.append(pltpu.make_async_copy(q_part, qb.at[place], qsem.at[i]))
        copies.append(pltpu.make_async_copy(do_refs[i], dob.at[place], dosem.at[i]))
    for copy in copies:
        copy.start()
    for copy in copies:
        copy.wait()
    cols = heads * HEAD_DIM
    vfirst = packed - wide
    voff = wide - cols
    at_row = lax.broadcasted_iota(jnp.int32, (wide, tq), 0)

    def one_tile(t, bias):
        lo, hi = rng[3 * t], rng[3 * t + 1]
        qs = pl.multiple_of(rng[3 * t + 2], tq)

        def stack(tile, first, ones):
            parts = []
            for h in range(heads):
                head = (at_row >= first + h * HEAD_DIM) & (at_row < first + (h + 1) * HEAD_DIM)
                one = (at_row >= ones + 3 * h) & (at_row < ones + 3 * h + 3)
                kept = jnp.where(head, tile, jnp.zeros_like(tile))
                parts.append(jnp.where(one, jnp.ones_like(tile), kept))
            return jnp.concatenate(parts, 1)

        k3t = stack(kv_ref[pl.ds(qs, tq), :wide].T, 0, cols)
        v3t = stack(kv_ref[pl.ds(qs, tq), vfirst:].T, voff, 0)
        kseg = kseg_ref[t]
        dkt[...] = jnp.zeros_like(dkt)
        dvt[...] = jnp.zeros_like(dvt)

        def scan_queries(j, carry):
            at = pl.multiple_of(j * tk, tk)
            q = qb[pl.ds(at, tk), :]
            do = dob[pl.ds(at, tk), :]
            same = qseg_ref[pl.ds(at, tk), :] == kseg
            probs = jnp.where(same, jnp.exp(dot(q, k3t)), 0.0)
            grad = (probs * dot(do, v3t)).astype(BF)
            dkt[...] += dot_tn(q, grad)
            dvt[...] += dot_tn(do, probs.astype(BF))
            return carry

        lax.fori_loop(lo, hi, scan_queries, 0)
        pieces = []
        for ref, first in ((dkt, 0), (dvt, voff)):
            for h in range(heads):
                start = first + h * HEAD_DIM
                pieces.append(ref[start : start + HEAD_DIM, h * tq : (h + 1) * tq])
        grads = jnp.concatenate(pieces, 0).T
        added = jnp.sum(grads, 0, keepdims=True)
        dkv_ref[pl.ds(qs, tq), :] = grads.astype(BF)
        return bias + added

    bias_ref[...] = lax.fori_loop(0, tok // tq, one_tile, jnp.zeros((1, packed), F32))


def input_kernel(rng, dq_ref, dkv_ref, wq_ref, wkv_ref, own_ref, send_ref):
    half = own_ref.shape[0]
    for t, ref in enumerate((own_ref, send_ref)):
        at = pl.ds(pl.multiple_of(rng[3 * t + 2], half), half)
        total = dot_nt(dq_ref[at, :], wq_ref[...]) + dot_nt(dkv_ref[at, :], wkv_ref[...])
        ref[...] = total.astype(ref.dtype)


def add_products(lefts, rights, cut, span, dtype):
    total = None
    for a, b in zip(lefts, rights):
        term = dot_tn(a[:, cut], b[:, span])
        total = term if total is None else total + term
    return total.astype(dtype)


def weight_kernel(part, rows, keep, *refs):
    own_ref, send_ref = refs[-2:]
    spans = ((own_ref, slice(0, part)), (send_ref, slice(part, None)))
    at = 0
    for first, last in keep:
        lefts, rights = refs[:rows], refs[rows : 2 * rows]
        refs = refs[2 * rows :]
        if first or last % 256:
            for ref, span in spans:
                total = add_products(lefts, rights, slice(None), span, ref.dtype)
                ref[at : at + last - first, :] = total[first:last]
        else:

            def one_tile(i, carry, lefts=lefts, rights=rights, at=at):
                cut = pl.ds(pl.multiple_of(i * 256, 256), 256)
                for ref, span in spans:
                    total = add_products(lefts, rights, cut, span, ref.dtype)
                    ref[pl.ds(pl.multiple_of(at + i * 256, 64), 256), :] = total
                return carry

            lax.fori_loop(0, last // 256, one_tile, 0)
        at += last - first


def weight_grads(pairs, part, keep):
    width = pairs[0][1][0].shape[1]
    if part % 128 or (width - part) % 128:
        total = jnp.concatenate(
            [
                functools.reduce(lambda p, q: p + q, [dot_tn(a, b) for a, b in zip(*pair)])[slice(*span)]
                for pair, span in zip(pairs, keep)
            ],
            0,
        )
        return total[:, :part], total[:, part:].astype(BF)
    kept = sum(last - first for first, last in keep)
    operands = [x for lefts, rights in pairs for x in list(lefts) + list(rights)]
    work = sum(2 * a.shape[0] * a.shape[1] * b.shape[1] for lefts, rights in pairs for a, b in zip(lefts, rights))
    vmem = pl.BlockSpec(memory_space=pltpu.VMEM)
    return pl.pallas_call(
        functools.partial(weight_kernel, part, len(pairs[0][0]), keep),
        out_shape=(
            jax.ShapeDtypeStruct((kept, part), F32),
            jax.ShapeDtypeStruct((kept, width - part), BF),
        ),
        in_specs=[vmem] * len(operands),
        out_specs=(vmem, vmem),
        cost_estimate=pl.CostEstimate(
            flops=work, transcendentals=0, bytes_accessed=sum(x.size * 2 for x in operands)
        ),
        compiler_params=pltpu.CompilerParams(vmem_limit_bytes=16 << 20),
        name="weight_grads",
    )(*operands)


def last_kernel(rows, part, units, refs_in, own_ref, send_ref):
    dkv_refs, x_refs = refs_in[:rows], refs_in[rows : 2 * rows]
    vec_ref = refs_in[2 * rows]
    unit_refs, q_refs, v_refs = (refs_in[2 * rows + 1 + i * rows :][:rows] for i in range(3))
    packed = dkv_refs[0].shape[1]
    cols = packed // 2
    shape = (own_ref.shape[0] - packed, part)
    at = lax.broadcasted_iota(jnp.int32, shape, 0)
    lane = lax.broadcasted_iota(jnp.int32, (1, part), 1)

    def over(refs):
        return functools.reduce(lambda a, b: a + b, [ref[...] for ref in refs])

    unit_row = over(unit_refs)
    q_row = jnp.concatenate([over(q_refs), jnp.zeros((1, packed - q_refs[0].shape[1]), F32)], 1)
    pieces = [unit_row[:, i : i + packed] for i in range(0, units, packed)]
    pieces.append(jnp.where(lane < cols, q_row, over(v_refs)))
    for ref, span in ((own_ref, slice(0, part)), (send_ref, slice(part, None))):

        def one_tile(i, carry, ref=ref, span=span):
            cut = pl.ds(pl.multiple_of(i * 128, 128), 128)
            ref[cut, :] = add_products(dkv_refs, x_refs, cut, span, ref.dtype)
            return carry

        lax.fori_loop(0, packed // 128, one_tile, 0)
        block = jnp.concatenate([vec_ref[:, span], jnp.zeros((shape[0] - 8, part), F32)], 0)
        for i, piece in enumerate(pieces):
            block = jnp.where(at == 8 + i, piece, block)
        ref[packed:, :] = block.astype(ref.dtype)


def last_grads(dkvs, xs, d_vec, d_units, d_q, d_v, part, lines):
    rows = len(dkvs)
    packed = dkvs[0].shape[1]
    units = d_units[0].shape[1]
    operands = list(dkvs) + list(xs) + [d_vec] + list(d_units) + list(d_q) + list(d_v)
    vmem = pl.BlockSpec(memory_space=pltpu.VMEM)
    shape = (packed + lines, part)

    def kernel(*refs):
        last_kernel(rows, part, units, refs[:-2], *refs[-2:])

    return pl.pallas_call(
        kernel,
        out_shape=(jax.ShapeDtypeStruct(shape, F32), jax.ShapeDtypeStruct(shape, BF)),
        in_specs=[vmem] * len(operands),
        out_specs=(vmem, vmem),
        cost_estimate=pl.CostEstimate(
            flops=4 * rows * packed * part * xs[0].shape[0],
            transcendentals=0,
            bytes_accessed=sum(x.size * 2 for x in operands),
        ),
        compiler_params=pltpu.CompilerParams(vmem_limit_bytes=16 << 20),
        name="last_grads",
    )(*operands)


def make_attention(slots, heads, tok, wide, packed, width):
    tq = tok // 2
    tk = tq
    vmem = pl.BlockSpec(memory_space=pltpu.VMEM)
    smem = pl.BlockSpec(memory_space=pltpu.SMEM)
    hbm = pl.BlockSpec(memory_space=HBM_SPACE)
    pairs = 2 * heads * tok * 1024 * wide
    def grant(size):
        return pltpu.CompilerParams(vmem_limit_bytes=size << 20)

    params = grant(BWD)
    rowed = jax.ShapeDtypeStruct((2, 1, heads * tq), F32)
    tokens = jax.ShapeDtypeStruct((tok, wide), BF)

    def cost(products, exps):
        return pl.CostEstimate(
            flops=products * pairs,
            transcendentals=exps * heads * tok * 1024,
            bytes_accessed=slots * tok * packed * 2,
        )

    forward = pl.pallas_call(
        functools.partial(forward_kernel, slots, heads, tq, tk),
        out_shape=(tokens, rowed, tokens, jax.ShapeDtypeStruct((slots * tok, packed), BF)),
        in_specs=[smem, vmem, vmem, vmem] + [hbm] * slots,
        out_specs=(vmem, vmem, vmem, pl.BlockSpec(memory_space=pltpu.HBM)),
        scratch_shapes=[
            pltpu.VMEM((slots * tok, packed), BF),
            pltpu.VMEM((slots * tok, heads * tq), F32),
            pltpu.VMEM((wide, heads * tq), F32),
            pltpu.SemaphoreType.DMA((slots,)),
            pltpu.SemaphoreType.DMA,
        ],
        cost_estimate=cost(2, 1),
        compiler_params=grant(FWD),
        name="attend_forward",
    )
    mix_back = pl.pallas_call(
        functools.partial(mix_kernel, heads, tq),
        out_shape=(tokens, rowed),
        in_specs=[smem, vmem, vmem, vmem],
        out_specs=(vmem, vmem),
        cost_estimate=pl.CostEstimate(
            flops=2 * tok * wide * width, transcendentals=0, bytes_accessed=tok * (2 * wide + width) * 2
        ),
        compiler_params=params,
        name="mix_back",
    )
    query_back = pl.pallas_call(
        functools.partial(query_kernel, heads, tq, tk),
        out_shape=(tokens, jax.ShapeDtypeStruct((1, wide), F32)),
        in_specs=[smem] + [vmem] * 6 + [pl.BlockSpec(memory_space=pltpu.HBM)],
        out_specs=(vmem, vmem),
        scratch_shapes=[
            pltpu.VMEM((slots * tok, packed), BF),
            pltpu.VMEM((wide, heads * tq), F32),
            pltpu.SemaphoreType.DMA,
        ],
        cost_estimate=cost(3, 1),
        compiler_params=params,
        name="query_back",
    )
    key_back = pl.pallas_call(
        functools.partial(key_kernel, slots, heads, tq, tk),
        out_shape=(
            jax.ShapeDtypeStruct((tok, packed), BF),
            jax.ShapeDtypeStruct((1, packed), F32),
        ),
        in_specs=[smem] + [vmem] * 3 + [hbm] * (2 * slots),
        out_specs=(vmem, vmem),
        scratch_shapes=[
            pltpu.VMEM((slots * tok, wide), BF),
            pltpu.VMEM((slots * tok, wide), BF),
            pltpu.VMEM((wide, heads * tq), F32),
            pltpu.VMEM((wide, heads * tq), F32),
            pltpu.SemaphoreType.DMA((slots,)),
            pltpu.SemaphoreType.DMA((slots,)),
        ],
        cost_estimate=cost(4, 1),
        compiler_params=params,
        name="key_back",
    )
    input_back = pl.pallas_call(
        input_kernel,
        out_shape=(
            jax.ShapeDtypeStruct((tq, width), F32),
            jax.ShapeDtypeStruct((tq, width), BF),
        ),
        in_specs=[smem] + [vmem] * 4,
        out_specs=(vmem, vmem),
        cost_estimate=pl.CostEstimate(
            flops=2 * tok * (wide + packed) * width,
            transcendentals=0,
            bytes_accessed=tok * (wide + packed + width) * 4,
        ),
        compiler_params=params,
        name="input_back",
    )
    return forward, mix_back, query_back, key_back, input_back


def after(value, *others):
    return lax.optimization_barrier((value,) + others)[0]


def make_body(n_shard, n_ctx, n_tp):
    bits = [1 << i for i in range(n_tp.bit_length() - 1)]
    ctx_steps = [1 << i for i in range(n_ctx.bit_length() - 1)]
    ctx_whole = not n_ctx & (n_ctx - 1)

    def exchange(value, axis, size, bit):
        return lax.ppermute(value, axis, [(i, i ^ bit) for i in range(size) if i ^ bit < size])

    def even_swap(value):
        return exchange(value, "ctx", n_ctx, 1)

    def odd_swap(value):
        pairs = []
        for i in range(1, n_ctx - 1, 2):
            pairs += [(i, i + 1), (i + 1, i)]
        return lax.ppermute(value, "ctx", pairs)

    def swap(value, kind):
        return odd_swap(value) if kind else even_swap(value)

    ctx_count = max(2 * len(ctx_steps) - 1, 1)

    def ctx_step(cur, step, late):
        ci = lax.axis_index("ctx")
        count = len(ctx_steps)
        bit = ctx_steps[step] if step < count else ctx_steps[2 * count - 2 - step]
        up = (ci // bit) % 2
        if step == count - 1:
            cur = cur.astype(BF)
            return (cur.astype(F32) + late(exchange(cur, "ctx", n_ctx, bit)).astype(F32)).astype(BF)
        if step < count:
            half = cur.shape[0] // 2
            send = lax.dynamic_slice_in_dim(cur, (1 - up) * half, half, 0).astype(BF)
            keep = lax.dynamic_slice_in_dim(cur, up * half, half, 0)
            return keep + late(exchange(send, "ctx", n_ctx, bit)).astype(F32)
        other = late(exchange(cur, "ctx", n_ctx, bit))
        return jnp.where(up == 0, jnp.concatenate([cur, other], 0), jnp.concatenate([other, cur], 0))

    def body(
        hidden_in,
        segment_ids,
        qkv_weight,
        qv_bias,
        out_weight,
        out_bias,
        first_gain,
        first_shift,
        inner_weight,
        inner_bias,
        outer_weight,
        outer_bias,
        second_gain,
        second_shift,
        cotangent,
    ):
        rows, tok, width = hidden_in.shape
        part = width // n_shard
        cols = qkv_weight.shape[2]
        heads = cols // HEAD_DIM
        units = inner_weight.shape[1]
        wide = -(-cols // 128) * 128
        pad = wide - cols
        packed = 2 * cols
        half = tok // 2
        every = list(range(rows))
        si = lax.axis_index("shard")
        ci = lax.axis_index("ctx")
        core = lax.axis_index("tp") % 2
        reach = min(n_ctx - 1, 1 + (LONGEST - 2) // tok)
        slots = 2 * reach + 1
        attend_fwd, mix_back, query_back, key_back, input_back = make_attention(
            slots, heads, tok, wide, packed, width
        )

        def rolled(value, axis):
            if n_shard == 2:
                first = lax.slice_in_dim(value, 0, part, axis=axis)
                second = lax.slice_in_dim(value, part, width, axis=axis)
                return jnp.where(si == 0, value, jnp.concatenate([second, first], axis))
            return jnp.roll(value, -si * part, axis)

        def unrolled(value, axis):
            if n_shard == 2:
                return rolled(value, axis)
            return jnp.roll(value, si * part, axis)

        def others(own, axis):
            if n_shard == 2:
                return exchange(own, "shard", 2, 1)
            whole = rolled(lax.all_gather(own, "shard", axis=axis, tiled=True), axis)
            return lax.slice_in_dim(whole, part, width, axis=axis)

        def gathered(own, axis):
            if n_shard == 2:
                return jnp.concatenate([own, exchange(own, "shard", 2, 1)], axis)
            return rolled(lax.all_gather(own, "shard", axis=axis, tiled=True), axis)

        def gathered_in_order(own):
            if n_shard == 2:
                other = exchange(own, "shard", 2, 1)
                return jnp.where(
                    si == 0, jnp.concatenate([own, other], 0), jnp.concatenate([other, own], 0)
                )
            return lax.all_gather(own, "shard", axis=0, tiled=True)

        def own_half(value):
            return lax.dynamic_slice_in_dim(value, core * half, half, 0)

        def core_sum(own, send):
            total = own + exchange(send.astype(BF), "tp", n_tp, 1).astype(F32)
            return total.astype(BF) if len(bits) > 1 else total

        def chip_send(name):
            if len(bits) == 2:
                box["y" + name] = exchange(box[name], "tp", n_tp, bits[1])

        def chip_total(name):
            total = box[name].astype(F32)
            if len(bits) == 2:
                return total + box["y" + name].astype(F32)
            for bit in bits[1:]:
                total = total.astype(BF)
                total = total.astype(F32) + exchange(total, "tp", n_tp, bit).astype(F32)
            return total

        def stage_sum(name, own, send, beside, *names):
            if beside and len(bits) == 2:
                names += ("y" + beside,)
            if names:
                own, send = hold_all([own, send], *names)
            box[name] = core_sum(own, send)
            chip_send(name)

        def both_halves(own):
            return jnp.concatenate([own, exchange(own, "tp", n_tp, 1)], 0)

        def in_order(pair):
            first, second = pair[:half], pair[half:]
            return jnp.where(core == 0, pair, jnp.concatenate([second, first], 0))

        box = {}

        def hold_all(values, *names):
            kept = lax.optimization_barrier(tuple(values) + tuple(box[n] for n in names))
            box.update(zip(names, kept[len(values) :]))
            return kept[: len(values)]

        def hold(value, *names):
            return hold_all([value], *names)[0]

        box["kv_own"] = qkv_weight[:, 1:].astype(BF).reshape(part, packed)
        box["w_kv"] = gathered_in_order(box["kv_own"])
        q_own = jnp.pad(qkv_weight[:, 0].astype(BF), ((0, 0), (0, pad)))
        q_own = hold(q_own, "w_kv")
        w_kv = box["w_kv"]
        w_q = gathered_in_order(q_own)

        before = jnp.full((rows, reach * tok), -1, jnp.int32)
        behind = jnp.full((rows, reach * tok), 1 << 20, jnp.int32)
        padded = jnp.concatenate([before, segment_ids, behind], 1)
        key_seg = lax.dynamic_slice_in_dim(padded, ci * tok, slots * tok, 1)
        q_seg = lax.dynamic_slice_in_dim(segment_ids, ci * tok, tok, 1)
        q_seg = q_seg.reshape(rows, 2, half)
        q_seg = jnp.where(core == 0, q_seg, q_seg[:, ::-1])
        low = jnp.sum(key_seg[:, None, :] < q_seg[:, :, :1], -1) // half
        high = (jnp.sum(key_seg[:, None, :] <= q_seg[:, :, -1:], -1) + half - 1) // half
        begin = jnp.broadcast_to(jnp.stack([core * half, (1 - core) * half])[None], (rows, 2))
        ranges = jnp.stack([low, high, begin], -1).reshape(rows, 6).astype(jnp.int32)
        side = 1 - 2 * (ci % 2)
        places = [jnp.int32(reach) + 0 * side]
        for d in range(1, reach + 1):
            places += [reach + d * side, reach - d * side]
        places = jnp.broadcast_to(jnp.stack(places)[None], (rows, slots))
        numbers = jnp.arange(rows, dtype=jnp.int32)[:, None]
        ranges = jnp.concatenate([ranges, places.astype(jnp.int32), numbers], 1)
        q_seg3 = jnp.tile(q_seg[:, :, None, :], (1, 1, 1, heads))
        key_col = key_seg[:, :, None]

        v_bias = jnp.concatenate([jnp.zeros((cols,), F32), qv_bias[1]])
        q_bias = jnp.pad(qv_bias[0], (0, pad))

        def halo(own):
            found = [own]
            last = [own, own]
            for d in range(1, reach + 1):
                even, odd = even_swap(last[1]), odd_swap(last[0])
                found += [even, odd]
                last = [even, odd]
            return found

        def send_blocks(name, d):
            last = [box[name]] * 2 if d == 1 else [box[f"{name}_{2 * d - 4}"], box[f"{name}_{2 * d - 3}"]]
            box[f"{name}_{2 * d - 2}"] = even_swap(last[1])
            box[f"{name}_{2 * d - 1}"] = odd_swap(last[0])

        def send_kv(r, first):
            for d in range(first, reach + 1):
                send_blocks(f"kv{r}", d)

        for r in every:
            box[f"kv{r}"] = (dot(hidden_in[r], w_kv) + v_bias).astype(BF)
            if r:
                box[f"kv{r}"] = hold(box[f"kv{r}"], f"kv{r - 1}_0", f"kv{r - 1}_1")
            else:
                send_kv(0, 1)
                continue
            send_blocks(f"kv{r}", 1)
        q = [
            ((dot(hidden_in[r], w_q) + q_bias).astype(BF) * jnp.asarray(HEAD_DIM**-0.5, BF))
            for r in every
        ]

        vec_own = [out_bias, first_gain, first_shift, outer_bias, second_gain, second_shift]
        vec_own = jnp.concatenate([v[None] for v in vec_own] + [jnp.zeros((10, part), F32)], 0)
        wo_own = hold(jnp.concatenate([out_weight, vec_own], 0).astype(BF), "kv0")
        wo_vec = gathered(wo_own, 1)
        w_out = jnp.concatenate([jnp.zeros((pad, width), BF), wo_vec[:cols]], 0)
        vectors = wo_vec[cols : cols + 6].astype(F32)
        in_own = hold(inner_weight, "kv0").astype(BF)
        box["w_in"] = others(in_own, 0)
        outer_own = hold(outer_weight, "w_in").astype(BF)
        box["w_outer"] = others(outer_own, 1)
        bo, g1, s1, bd, g2, s2 = [vectors[i] for i in range(6)]

        def normed(summed):
            average = jnp.mean(summed, -1, keepdims=True)
            centered = summed - average
            variance = jnp.mean(centered * centered, -1, keepdims=True)
            scale = lax.rsqrt(variance + EPSILON)
            return centered * scale, scale

        def norm_back(grad, gain, hat, scale):
            inner = grad * gain
            return scale * (
                inner
                - jnp.mean(inner, -1, keepdims=True)
                - hat * jnp.mean(inner * hat, -1, keepdims=True)
            )

        x_roll = [rolled(hidden_in[r], 1) for r in every]
        x_res = [own_half(x_roll[r]).astype(F32) for r in every]
        cots = [rolled(own_half(cotangent[r]), 1).astype(F32) for r in every]

        ready = {0: ["w_in"], rows - 1: ["w_outer"]}

        def before(r, this, last):
            return [f"{this}{r - 1}"] if r else ([f"{last}{rows - 1}"] if last else [])

        o, lse, aug, kv_all = ([None] * rows for _ in range(4))
        for r in every:
            query = hold(q[r], *before(r, "a", None), *ready.get(r, []))
            blocks = [box[f"kv{r}"]] + [box[f"kv{r}_{i}"] for i in range(2 * reach)]
            out = attend_fwd(ranges[r], query, q_seg3[r], key_col[r], *blocks)
            if r < rows - 1:
                out = hold_all(out, f"kv{r + 1}_0", f"kv{r + 1}_1")
                send_kv(r + 1, 2)
            o[r], lse[r], aug[r], kv_all[r] = out
            send = dot(o[r][half:], w_out)
            stage_sum(f"a{r}", dot(o[r][:half], w_out), send, f"a{r - 1}" if r else None)
        q_halo = halo(jnp.concatenate(aug, 0))
        for i, block in enumerate(q_halo[1:]):
            box[f"q{i}"] = block

        hat1, scale1, y1, y1b = [None] * rows, [None] * rows, [None] * rows, [None] * rows
        u, slope = [None] * rows, [None] * rows
        for r in every:
            total = hold(chip_total(f"a{r}"), *before(r, "b", "a"))
            hat1[r], scale1[r] = normed(x_res[r] + total + bo)
            y1[r] = hat1[r] * g1 + s1
            y1b[r] = both_halves(y1[r].astype(BF))
            if not r:
                w_in = jnp.concatenate([in_own, box["w_in"]], 0)
                w_outer = jnp.concatenate([outer_own, box["w_outer"]], 1)
            a = dot(y1b[r], w_in) + inner_bias
            cdf = 0.5 * (1.0 + lax.erf(a * (0.5**0.5)))
            u[r] = (a * cdf).astype(BF)
            slope[r] = (cdf + a * jnp.exp(-0.5 * a * a) * 0.3989422804014327).astype(BF)
            send = dot(u[r][half:], w_outer)
            arrived = ["q0", "q1"] if r == rows - 1 else []
            stage_sum(f"b{r}", dot(u[r][:half], w_outer), send, f"b{r - 1}" if r else f"a{rows - 1}", *arrived)

        result, dh2, d2b, dab = ([None] * rows for _ in range(4))
        d_vec2, d_bi = [None] * rows, [None] * rows
        for r in every:
            total = hold(chip_total(f"b{r}"), *before(r, "c", "b"))
            hat2, scale2 = normed(y1[r] + total + bd)
            c = cots[r]
            result[r] = (hat2 * g2 + s2).astype(BF)
            dh2[r] = norm_back(c, g2, hat2, scale2)
            d2b[r] = both_halves(dh2[r].astype(BF))
            d_vec2[r] = [jnp.sum(v, 0, keepdims=True) for v in (dh2[r], c * hat2, c)]
            da = dot_nt(d2b[r], w_outer) * slope[r].astype(F32)
            d_bi[r] = jnp.sum(da, 0, keepdims=True)
            dab[r] = da.astype(BF)
            send = dot_nt(dab[r][half:], w_in)
            arrived = [f"q{i}" for i in range(2, 2 * reach)] if r == rows - 1 else []
            stage_sum(f"c{r}", dot_nt(dab[r][:half], w_in), send, f"c{r - 1}" if r else f"b{rows - 1}", *arrived)

        def over_rows(terms):
            return functools.reduce(lambda p, q: p + q, terms)

        def shard_send(name, send):
            box[name] = exchange(send, "shard", 2, 1) if n_shard == 2 else send

        def shard_total(name, own, axis):
            if n_shard == 2:
                return own + box[name].astype(F32)
            whole = unrolled(jnp.concatenate([own, box[name].astype(F32)], axis), axis)
            return lax.psum_scatter(whole, "shard", scatter_dimension=axis, tiled=True)

        def advance(name, *names):
            value, step = box[name], at_step.get(name, 0)
            if ctx_whole and step < ctx_count:
                box[name] = ctx_step(value, step, lambda got: hold(got, *names) if names else got)
            elif not step:
                box[name] = lax.psum(value, "ctx")
            at_step[name] = step + 1

        def finish(name):
            while at_step.get(name, 0) < ctx_count:
                advance(name)
            return box[name].astype(F32)

        at_step = {}

        dh1, d1b, d_vec1, dos, deltas = ([None] * rows for _ in range(5))

        def stage4(r, *names):
            total = hold(chip_total(f"c{r}"), *names)
            dy1 = dh2[r] + total
            dh1[r] = norm_back(dy1, g1, hat1[r], scale1[r])
            d1b[r] = both_halves(dh1[r].astype(BF))
            d_vec1[r] = [jnp.sum(v, 0, keepdims=True) for v in (dh1[r], dy1 * hat1[r], dy1)]
            box[f"do{r}"], deltas[r] = mix_back(ranges[r], d1b[r], w_out, o[r])

        gate = [f"c{rows - 1}"]
        for r in every:
            stage4(r, *gate)
            if r:
                box[f"do{r}"] = hold(box[f"do{r}"], *[f"do{r - 1}_{i}" for i in range(2, 2 * reach)])
            send_blocks(f"do{r}", 1)
            gate = [f"do{r}"]
            if not r:
                lefts = [hold(u[0], "do0")] + u[1:]
                own_first, send_first = weight_grads(
                    [(lefts, d2b), (dab, y1b)], part, [(0, units), (0, units)]
                )
                box["send_first"] = send_first
                names = ["do0_0", "do0_1"] + ([f"yc{rows - 1}"] if len(bits) == 2 else [])
                own_first, box["send_first"] = hold_all([own_first, send_first], *names)
                shard_send("x_first", box["send_first"])
                gate = ["send_first"]
            elif r < rows - 1:
                box[f"do{r}"] = hold(box[f"do{r}"], f"do{r}_0", f"do{r}_1")
            if r < rows - 1:
                for d in range(2, reach + 1):
                    send_blocks(f"do{r}", d)

        dqs, biases, dkvs, d_bv = ([None] * rows for _ in range(4))
        for r in every:
            query = hold(aug[r], f"dq{r - 1}" if r else f"do{rows - 1}")
            dq, biases[r] = query_back(
                ranges[r], query, q_seg3[r], key_col[r], box[f"do{r}"], lse[r], deltas[r], kv_all[r]
            )
            if not r:
                names = [f"do{rows - 1}_0", f"do{rows - 1}_1", "x_first"]
            else:
                names = [f"do{rows - 1}_{j}" for j in range(2, 2 * reach)] + ["first"] if r == rows - 1 else []
            box[f"dq{r}"] = hold(dq, *names)
            if not r:
                for d in range(2, reach + 1):
                    send_blocks(f"do{rows - 1}", d)
                box["first"] = shard_total("x_first", own_first, 1)
                advance("first")
        dqs = [box[f"dq{r}"] for r in every]
        own_mix, box["send_mix"] = weight_grads(
            [(o, d1b), (dqs, x_roll)], part, [(pad, wide), (0, cols)]
        )
        shard_send("x_mix", box["send_mix"])
        advance("first")
        for r in every:
            own = hold(box[f"kv{r}"], *(["send_mix"] if not r else [f"dkv{r - 1}"]))
            blocks = [box[f"do{r}"]] + [box[f"do{r}_{i}"] for i in range(2 * reach)]
            q_blocks = q_halo[:1] + [box[f"q{i}"] for i in range(2 * reach)]
            dkv, d_bv[r] = key_back(ranges[r], own, q_seg3[r], key_col[r], *q_blocks, *blocks)
            box[f"dkv{r}"] = hold(dkv, *(["x_mix"] if not r else ["mix"] if r == 1 else []))
            if not r:
                box["mix"] = shard_total("x_mix", own_mix, 1)
                advance("mix")
        dkvs = [box[f"dkv{r}"] for r in every]
        for r in every:
            own, send = input_back(ranges[r], dqs[r], dkvs[r], w_q, w_kv)
            if r == rows - 1:
                own, send = hold_all([own, send], "first")
            box[f"h{r}"] = core_sum(own, send)
            chip_send(f"h{r}")

        def finish_outputs():
            mine = hold(jnp.stack([unrolled(result[r], 1) for r in every]), "h0")
            theirs = exchange(mine, "tp", n_tp, 1)
            outputs = jnp.where(
                core == 0, jnp.concatenate([mine, theirs], 1), jnp.concatenate([theirs, mine], 1)
            )
            box["outputs"] = outputs

        def finish_first():
            total = finish("first")
            return total[units:].T, total[:units]

        def finish_hidden():
            hidden_grads = []
            for r in every:
                total = chip_total(f"h{r}")
                grad = (unrolled(dh1[r], 1) + total).astype(BF)
                hidden_grads.append(in_order(both_halves(grad)))
            box["hidden"] = jnp.stack(hidden_grads)

        d_vec = jnp.concatenate(
            [over_rows(v) for v in zip(*d_vec1)]
            + [over_rows(v) for v in zip(*d_vec2)]
            + [jnp.zeros((2, width), F32)],
            0,
        )
        d_vec = d_vec + exchange(d_vec, "tp", n_tp, 1)
        if n_shard == 2 and ctx_whole and part == packed and units % packed == 0:
            lines = 8 + units // packed + 1
            lines += (-(packed + lines)) % (16 * n_ctx)
            own_last, send_last = last_grads(dkvs, x_roll, d_vec, d_bi, biases, d_bv, part, lines)
            shard_send("x_last", send_last)
            box["last"] = shard_total("x_last", own_last, 1)
            advance("last")
            advance("mix", "last")
            box["first"] = hold(box["first"], "last")
            finish_outputs()
            advance("last", "outputs")
            finish_hidden()
            box["grad_in"], box["grad_outer"] = finish_first()
            advance("last", "hidden", "grad_in", "grad_outer")
            g_last = finish("last")
            vec = g_last[packed : packed + 6]
            d_units = g_last[packed + 8 : packed + 8 + units // packed].reshape(units)
            d_qv = g_last[packed + 8 + units // packed].reshape(2, cols)
        else:
            own_last, send_last = weight_grads([(dkvs, x_roll)], part, [(0, packed)])
            d_qv = jnp.concatenate([over_rows(biases)[:, :cols], over_rows(d_bv)[:, cols:]], 1)
            vec = lax.psum_scatter(unrolled(d_vec, 1), "shard", scatter_dimension=1, tiled=True)
            vec = lax.psum(vec, "ctx")
            d_units = lax.psum(over_rows(d_bi)[0], ("shard", "ctx"))
            d_qv = lax.psum(d_qv[0], ("shard", "ctx")).reshape(2, cols)
            shard_send("x_last", send_last)
            box["last"] = shard_total("x_last", own_last, 1)
            g_last = finish("last")
            finish_outputs()
            finish_hidden()
            box["grad_in"], box["grad_outer"] = finish_first()
        g_mix = finish("mix")
        grad_qkv = jnp.concatenate([g_mix[cols:], g_last[:packed]], 0).T.reshape(part, 3, cols)

        return (
            box["outputs"],
            box["hidden"],
            grad_qkv,
            d_qv,
            g_mix[:cols],
            vec[0],
            vec[1],
            vec[2],
            box["grad_in"],
            d_units,
            box["grad_outer"],
            vec[3],
            vec[4],
            vec[5],
        )

    return body


def solution(mesh):
    body = make_body(mesh.shape["shard"], mesh.shape["ctx"], mesh.shape["tp"])
    in_specs = (
        P("shard", "ctx", None),
        P("shard", None),
        P("shard", None, "tp"),
        P(None, "tp"),
        P("tp", "shard"),
        P("shard"),
        P("shard"),
        P("shard"),
        P("shard", "tp"),
        P("tp"),
        P("tp", "shard"),
        P("shard"),
        P("shard"),
        P("shard"),
        P("shard", "ctx", None),
    )
    out_specs = (
        P("shard", "ctx", None),
        P("shard", "ctx", None),
        P("shard", None, "tp"),
        P(None, "tp"),
        P("tp", "shard"),
        P("shard"),
        P("shard"),
        P("shard"),
        P("shard", "tp"),
        P("tp"),
        P("tp", "shard"),
        P("shard"),
        P("shard"),
        P("shard"),
    )
    return jax.shard_map(body, mesh=mesh, in_specs=in_specs, out_specs=out_specs, check_vma=False)
```

```python
import functools

import jax
import jax.numpy as jnp
from jax import lax
from jax.experimental import pallas as pl
from jax.experimental.pallas import tpu as pltpu
from jax.sharding import PartitionSpec as P

HEAD_DIM = 64
LONGEST = 1024
EPSILON = 1e-12
NEGATIVE = -1e30
HBM_SPACE = pl.ANY
FWD, BWD = 14, 10
BF = jnp.bfloat16
F32 = jnp.float32


def dot(a, b):
    return jnp.dot(a, b, preferred_element_type=F32)


def dot_tn(a, b):
    return lax.dot_general(a, b, (((0,), (0,)), ((), ())), preferred_element_type=F32)


def dot_nt(a, b):
    return lax.dot_general(a, b, (((1,), (1,)), ((), ())), preferred_element_type=F32)


def head_stack(tile, first, heads):
    row = lax.broadcasted_iota(jnp.int32, tile.shape, 0)
    parts = []
    for h in range(heads):
        start = first + h * HEAD_DIM
        parts.append(jnp.where((row >= start) & (row < start + HEAD_DIM), tile, jnp.zeros_like(tile)))
    return jnp.concatenate(parts, 1)


def load_blocks(kv_refs, kvb, sem, tok, slot_of):
    copies = [
        pltpu.make_async_copy(ref, kvb.at[pl.ds(pl.multiple_of(slot_of(i) * tok, tok), tok)], sem.at[i])
        for i, ref in enumerate(kv_refs)
    ]
    for copy in copies:
        copy.start()
    for copy in copies:
        copy.wait()


def forward_kernel(slots, heads, tq, tk, rng, q_ref, qseg_ref, kseg_ref, *rest):
    kv_refs = rest[:slots]
    o_ref, lse_ref, aug_ref, all_ref, kvb, st, acc, sem, out_sem = rest[slots:]
    tok = q_ref.shape[0]
    wide = q_ref.shape[1]
    table = 3 * (tok // tq)
    load_blocks(kv_refs, kvb, sem, tok, lambda i: rng[table + i])
    keep = pltpu.make_async_copy(kvb, all_ref, out_sem)
    keep.start()
    vfirst = 2 * heads * HEAD_DIM - wide
    voff = wide - heads * HEAD_DIM

    def one_tile(t, carry):
        lo, hi = rng[3 * t], rng[3 * t + 1]
        qs = pl.multiple_of(rng[3 * t + 2], tq)
        qt = q_ref[pl.ds(qs, tq), :].T
        q3t = head_stack(qt, 0, heads)
        qseg = qseg_ref[t]

        def scan_scores(j, top):
            at = pl.multiple_of(j * tk, tk)
            scores = dot(kvb[pl.ds(at, tk), :wide], q3t)
            scores = jnp.where(kseg_ref[pl.ds(at, tk), :] == qseg, scores, NEGATIVE)
            st[pl.ds(at, tk), :] = scores
            return jnp.maximum(top, jnp.max(scores.reshape(tk // 8, 8, heads * tq), 0))

        top8 = lax.fori_loop(lo, hi, scan_scores, jnp.full((8, heads * tq), NEGATIVE, F32))
        top = jnp.max(top8, 0, keepdims=True)
        acc[...] = jnp.zeros_like(acc)

        def scan_values(j, total):
            at = pl.multiple_of(j * tk, tk)
            weights = jnp.exp(st[pl.ds(at, tk), :] - top)
            acc[...] += dot_tn(kvb[pl.ds(at, tk), vfirst:], weights.astype(BF))
            return total + jnp.sum(weights.reshape(tk // 8, 8, heads * tq), 0)

        total8 = lax.fori_loop(lo, hi, scan_values, jnp.zeros((8, heads * tq), F32))
        total = jnp.sum(total8, 0, keepdims=True)
        lse = top + jnp.log(total)
        lse_ref[t] = lse
        full = jnp.concatenate([qt[: wide - voff].astype(F32), spread(-lse, voff, heads, tq)], 0)
        aug_ref[pl.ds(qs, tq), :] = full.T.astype(BF)
        inv = 1.0 / total
        pieces = [jnp.zeros((voff, tq), F32)]
        for h in range(heads):
            rows = slice(voff + h * HEAD_DIM, voff + (h + 1) * HEAD_DIM)
            cols = slice(h * tq, (h + 1) * tq)
            pieces.append(acc[rows, cols] * inv[:, cols])
        o_ref[pl.ds(pl.multiple_of(t * tq, tq), tq), :] = jnp.concatenate(pieces, 0).T.astype(BF)
        return carry

    lax.fori_loop(0, tok // tq, one_tile, 0)
    keep.wait()


def thirds(value):
    high = value.astype(BF).astype(F32)
    rest = value - high
    middle = rest.astype(BF).astype(F32)
    return [high, middle, rest - middle]


def spread(rows, count, heads, tq):
    at = lax.broadcasted_iota(jnp.int32, (count, tq), 0)
    out = jnp.zeros((count, tq), F32)
    for h in range(heads):
        for i, piece in enumerate(thirds(rows[:, h * tq : (h + 1) * tq])):
            out = jnp.where(at == 3 * h + i, piece, out)
    return out


def mix_kernel(heads, tq, rng, d1_ref, w_ref, o_ref, do_ref, delta_ref):
    wide = o_ref.shape[1]
    voff = wide - heads * HEAD_DIM

    def one_tile(t, carry):
        qs = pl.multiple_of(rng[3 * t + 2], tq)
        at = pl.ds(pl.multiple_of(t * tq, tq), tq)
        grad = dot_nt(w_ref[...], d1_ref[at, :]).astype(BF).astype(F32)
        prod = grad * o_ref[at, :].T.astype(F32)
        delta = jnp.concatenate(
            [
                jnp.sum(prod[voff + h * HEAD_DIM : voff + (h + 1) * HEAD_DIM], 0, keepdims=True)
                for h in range(heads)
            ],
            1,
        )
        delta_ref[t] = delta
        full = jnp.concatenate([spread(-delta, voff, heads, tq), grad[voff:]], 0)
        do_ref[pl.ds(qs, tq), :] = full.T.astype(BF)
        return carry

    lax.fori_loop(0, o_ref.shape[0] // tq, one_tile, 0)


def query_kernel(heads, tq, tk, rng, q_ref, qseg_ref, kseg_ref, do_ref, lse_ref, delta_ref, *rest):
    kv_ref, dq_ref, bias_ref, kvb, dqt, sem = rest
    tok = q_ref.shape[0]
    wide = q_ref.shape[1]
    load = pltpu.make_async_copy(kv_ref, kvb, sem)
    load.start()
    load.wait()
    vfirst = 2 * heads * HEAD_DIM - wide
    voff = wide - heads * HEAD_DIM

    def one_tile(t, bias):
        lo, hi = rng[3 * t], rng[3 * t + 1]
        qs = pl.multiple_of(rng[3 * t + 2], tq)
        q3t = head_stack(q_ref[pl.ds(qs, tq), :].T, 0, heads)
        do3t = head_stack(do_ref[pl.ds(qs, tq), :].T, voff, heads)
        delta = delta_ref[t]
        qseg = qseg_ref[t]
        lse = lse_ref[t]
        dqt[...] = jnp.zeros_like(dqt)

        def scan_keys(j, carry):
            at = pl.multiple_of(j * tk, tk)
            k = kvb[pl.ds(at, tk), :wide]
            same = kseg_ref[pl.ds(at, tk), :] == qseg
            probs = jnp.where(same, jnp.exp(dot(k, q3t) - lse), 0.0)
            grad = (probs * (dot(kvb[pl.ds(at, tk), vfirst:], do3t) - delta)).astype(BF)
            dqt[...] += dot_tn(k, grad)
            return carry

        lax.fori_loop(lo, hi, scan_keys, 0)
        pieces = []
        for h in range(heads):
            pieces.append(dqt[h * HEAD_DIM : (h + 1) * HEAD_DIM, h * tq : (h + 1) * tq])
        pieces.append(jnp.zeros((wide - heads * HEAD_DIM, tq), F32))
        dq = jnp.concatenate(pieces, 0).T * HEAD_DIM**-0.5
        added = jnp.sum(dq, 0, keepdims=True)
        dq_ref[pl.ds(qs, tq), :] = dq.astype(BF)
        return bias + added

    bias_ref[...] = lax.fori_loop(0, tok // tq, one_tile, jnp.zeros((1, wide), F32))


def key_kernel(slots, heads, tq, tk, rng, kv_ref, kseg_ref, qseg_ref, *rest):
    q_refs, do_refs = rest[:slots], rest[slots : 2 * slots]
    dkv_ref, bias_ref, qb, dob, dkt, dvt, qsem, dosem = rest[2 * slots :]
    tok, packed = kv_ref.shape
    wide = qb.shape[1]
    table = 3 * (tok // tq)
    copies = []
    for i in range(slots):
        place = pl.ds(pl.multiple_of(rng[table + i] * tok, tok), tok)
        q_part = q_refs[i].at[pl.ds(pl.multiple_of(rng[table + slots] * tok, tok), tok)]
        copies.append(pltpu.make_async_copy(q_part, qb.at[place], qsem.at[i]))
        copies.append(pltpu.make_async_copy(do_refs[i], dob.at[place], dosem.at[i]))
    for copy in copies:
        copy.start()
    for copy in copies:
        copy.wait()
    cols = heads * HEAD_DIM
    vfirst = packed - wide
    voff = wide - cols
    at_row = lax.broadcasted_iota(jnp.int32, (wide, tq), 0)

    def one_tile(t, bias):
        lo, hi = rng[3 * t], rng[3 * t + 1]
        qs = pl.multiple_of(rng[3 * t + 2], tq)

        def stack(tile, first, ones):
            parts = []
            for h in range(heads):
                head = (at_row >= first + h * HEAD_DIM) & (at_row < first + (h + 1) * HEAD_DIM)
                one = (at_row >= ones + 3 * h) & (at_row < ones + 3 * h + 3)
                kept = jnp.where(head, tile, jnp.zeros_like(tile))
                parts.append(jnp.where(one, jnp.ones_like(tile), kept))
            return jnp.concatenate(parts, 1)

        k3t = stack(kv_ref[pl.ds(qs, tq), :wide].T, 0, cols)
        v3t = stack(kv_ref[pl.ds(qs, tq), vfirst:].T, voff, 0)
        kseg = kseg_ref[t]
        dkt[...] = jnp.zeros_like(dkt)
        dvt[...] = jnp.zeros_like(dvt)

        def scan_queries(j, carry):
            at = pl.multiple_of(j * tk, tk)
            q = qb[pl.ds(at, tk), :]
            do = dob[pl.ds(at, tk), :]
            same = qseg_ref[pl.ds(at, tk), :] == kseg
            probs = jnp.where(same, jnp.exp(dot(q, k3t)), 0.0)
            grad = (probs * dot(do, v3t)).astype(BF)
            dkt[...] += dot_tn(q, grad)
            dvt[...] += dot_tn(do, probs.astype(BF))
            return carry

        lax.fori_loop(lo, hi, scan_queries, 0)
        pieces = []
        for ref, first in ((dkt, 0), (dvt, voff)):
            for h in range(heads):
                start = first + h * HEAD_DIM
                pieces.append(ref[start : start + HEAD_DIM, h * tq : (h + 1) * tq])
        grads = jnp.concatenate(pieces, 0).T
        added = jnp.sum(grads, 0, keepdims=True)
        dkv_ref[pl.ds(qs, tq), :] = grads.astype(BF)
        return bias + added

    bias_ref[...] = lax.fori_loop(0, tok // tq, one_tile, jnp.zeros((1, packed), F32))


def input_kernel(rng, dq_ref, dkv_ref, wq_ref, wkv_ref, own_ref, send_ref):
    half = own_ref.shape[0]
    for t, ref in enumerate((own_ref, send_ref)):
        at = pl.ds(pl.multiple_of(rng[3 * t + 2], half), half)
        total = dot_nt(dq_ref[at, :], wq_ref[...]) + dot_nt(dkv_ref[at, :], wkv_ref[...])
        ref[...] = total.astype(ref.dtype)


def add_products(lefts, rights, cut, span, dtype):
    total = None
    for a, b in zip(lefts, rights):
        term = dot_tn(a[:, cut], b[:, span])
        total = term if total is None else total + term
    return total.astype(dtype)


def weight_kernel(part, rows, keep, *refs):
    own_ref, send_ref = refs[-2:]
    spans = ((own_ref, slice(0, part)), (send_ref, slice(part, None)))
    at = 0
    for first, last in keep:
        lefts, rights = refs[:rows], refs[rows : 2 * rows]
        refs = refs[2 * rows :]
        if first or last % 256:
            for ref, span in spans:
                total = add_products(lefts, rights, slice(None), span, ref.dtype)
                ref[at : at + last - first, :] = total[first:last]
        else:

            def one_tile(i, carry, lefts=lefts, rights=rights, at=at):
                cut = pl.ds(pl.multiple_of(i * 256, 256), 256)
                for ref, span in spans:
                    total = add_products(lefts, rights, cut, span, ref.dtype)
                    ref[pl.ds(pl.multiple_of(at + i * 256, 64), 256), :] = total
                return carry

            lax.fori_loop(0, last // 256, one_tile, 0)
        at += last - first


def weight_grads(pairs, part, keep):
    width = pairs[0][1][0].shape[1]
    if part % 128 or (width - part) % 128:
        total = jnp.concatenate(
            [
                functools.reduce(lambda p, q: p + q, [dot_tn(a, b) for a, b in zip(*pair)])[slice(*span)]
                for pair, span in zip(pairs, keep)
            ],
            0,
        )
        return total[:, :part], total[:, part:].astype(BF)
    kept = sum(last - first for first, last in keep)
    operands = [x for lefts, rights in pairs for x in list(lefts) + list(rights)]
    work = sum(2 * a.shape[0] * a.shape[1] * b.shape[1] for lefts, rights in pairs for a, b in zip(lefts, rights))
    vmem = pl.BlockSpec(memory_space=pltpu.VMEM)
    return pl.pallas_call(
        functools.partial(weight_kernel, part, len(pairs[0][0]), keep),
        out_shape=(
            jax.ShapeDtypeStruct((kept, part), F32),
            jax.ShapeDtypeStruct((kept, width - part), BF),
        ),
        in_specs=[vmem] * len(operands),
        out_specs=(vmem, vmem),
        cost_estimate=pl.CostEstimate(
            flops=work, transcendentals=0, bytes_accessed=sum(x.size * 2 for x in operands)
        ),
        compiler_params=pltpu.CompilerParams(vmem_limit_bytes=10 << 20),
        name="weight_grads",
    )(*operands)


def last_kernel(rows, part, units, refs_in, own_ref, send_ref):
    dkv_refs, x_refs = refs_in[:rows], refs_in[rows : 2 * rows]
    vec_ref = refs_in[2 * rows]
    unit_refs, q_refs, v_refs = (refs_in[2 * rows + 1 + i * rows :][:rows] for i in range(3))
    packed = dkv_refs[0].shape[1]
    cols = packed // 2
    shape = (own_ref.shape[0] - packed, part)
    at = lax.broadcasted_iota(jnp.int32, shape, 0)
    lane = lax.broadcasted_iota(jnp.int32, (1, part), 1)

    def over(refs):
        return functools.reduce(lambda a, b: a + b, [ref[...] for ref in refs])

    unit_row = over(unit_refs)
    q_row = jnp.concatenate([over(q_refs), jnp.zeros((1, packed - q_refs[0].shape[1]), F32)], 1)
    pieces = [unit_row[:, i : i + packed] for i in range(0, units, packed)]
    pieces.append(jnp.where(lane < cols, q_row, over(v_refs)))
    for ref, span in ((own_ref, slice(0, part)), (send_ref, slice(part, None))):

        def one_tile(i, carry, ref=ref, span=span):
            cut = pl.ds(pl.multiple_of(i * 128, 128), 128)
            ref[cut, :] = add_products(dkv_refs, x_refs, cut, span, ref.dtype)
            return carry

        lax.fori_loop(0, packed // 128, one_tile, 0)
        block = jnp.concatenate([vec_ref[:, span], jnp.zeros((shape[0] - 8, part), F32)], 0)
        for i, piece in enumerate(pieces):
            block = jnp.where(at == 8 + i, piece, block)
        ref[packed:, :] = block.astype(ref.dtype)


def last_grads(dkvs, xs, d_vec, d_units, d_q, d_v, part, lines):
    rows = len(dkvs)
    packed = dkvs[0].shape[1]
    units = d_units[0].shape[1]
    operands = list(dkvs) + list(xs) + [d_vec] + list(d_units) + list(d_q) + list(d_v)
    vmem = pl.BlockSpec(memory_space=pltpu.VMEM)
    shape = (packed + lines, part)

    def kernel(*refs):
        last_kernel(rows, part, units, refs[:-2], *refs[-2:])

    return pl.pallas_call(
        kernel,
        out_shape=(jax.ShapeDtypeStruct(shape, F32), jax.ShapeDtypeStruct(shape, BF)),
        in_specs=[vmem] * len(operands),
        out_specs=(vmem, vmem),
        cost_estimate=pl.CostEstimate(
            flops=4 * rows * packed * part * xs[0].shape[0],
            transcendentals=0,
            bytes_accessed=sum(x.size * 2 for x in operands),
        ),
        compiler_params=pltpu.CompilerParams(vmem_limit_bytes=10 << 20),
        name="last_grads",
    )(*operands)


def make_attention(slots, heads, tok, wide, packed, width):
    tq = tok // 2
    tk = tq
    vmem = pl.BlockSpec(memory_space=pltpu.VMEM)
    smem = pl.BlockSpec(memory_space=pltpu.SMEM)
    hbm = pl.BlockSpec(memory_space=HBM_SPACE)
    pairs = 2 * heads * tok * 1024 * wide
    def grant(size):
        return pltpu.CompilerParams(vmem_limit_bytes=size << 20)

    params = grant(BWD)
    rowed = jax.ShapeDtypeStruct((2, 1, heads * tq), F32)
    tokens = jax.ShapeDtypeStruct((tok, wide), BF)

    def cost(products, exps):
        return pl.CostEstimate(
            flops=products * pairs,
            transcendentals=exps * heads * tok * 1024,
            bytes_accessed=slots * tok * packed * 2,
        )

    forward = pl.pallas_call(
        functools.partial(forward_kernel, slots, heads, tq, tk),
        out_shape=(tokens, rowed, tokens, jax.ShapeDtypeStruct((slots * tok, packed), BF)),
        in_specs=[smem, vmem, vmem, vmem] + [hbm] * slots,
        out_specs=(vmem, vmem, vmem, pl.BlockSpec(memory_space=pltpu.HBM)),
        scratch_shapes=[
            pltpu.VMEM((slots * tok, packed), BF),
            pltpu.VMEM((slots * tok, heads * tq), F32),
            pltpu.VMEM((wide, heads * tq), F32),
            pltpu.SemaphoreType.DMA((slots,)),
            pltpu.SemaphoreType.DMA,
        ],
        cost_estimate=cost(2, 1),
        compiler_params=grant(FWD),
        name="attend_forward",
    )
    mix_back = pl.pallas_call(
        functools.partial(mix_kernel, heads, tq),
        out_shape=(tokens, rowed),
        in_specs=[smem, vmem, vmem, vmem],
        out_specs=(vmem, vmem),
        cost_estimate=pl.CostEstimate(
            flops=2 * tok * wide * width, transcendentals=0, bytes_accessed=tok * (2 * wide + width) * 2
        ),
        compiler_params=params,
        name="mix_back",
    )
    query_back = pl.pallas_call(
        functools.partial(query_kernel, heads, tq, tk),
        out_shape=(tokens, jax.ShapeDtypeStruct((1, wide), F32)),
        in_specs=[smem] + [vmem] * 6 + [pl.BlockSpec(memory_space=pltpu.HBM)],
        out_specs=(vmem, vmem),
        scratch_shapes=[
            pltpu.VMEM((slots * tok, packed), BF),
            pltpu.VMEM((wide, heads * tq), F32),
            pltpu.SemaphoreType.DMA,
        ],
        cost_estimate=cost(3, 1),
        compiler_params=params,
        name="query_back",
    )
    key_back = pl.pallas_call(
        functools.partial(key_kernel, slots, heads, tq, tk),
        out_shape=(
            jax.ShapeDtypeStruct((tok, packed), BF),
            jax.ShapeDtypeStruct((1, packed), F32),
        ),
        in_specs=[smem] + [vmem] * 3 + [hbm] * (2 * slots),
        out_specs=(vmem, vmem),
        scratch_shapes=[
            pltpu.VMEM((slots * tok, wide), BF),
            pltpu.VMEM((slots * tok, wide), BF),
            pltpu.VMEM((wide, heads * tq), F32),
            pltpu.VMEM((wide, heads * tq), F32),
            pltpu.SemaphoreType.DMA((slots,)),
            pltpu.SemaphoreType.DMA((slots,)),
        ],
        cost_estimate=cost(4, 1),
        compiler_params=params,
        name="key_back",
    )
    input_back = pl.pallas_call(
        input_kernel,
        out_shape=(
            jax.ShapeDtypeStruct((tq, width), F32),
            jax.ShapeDtypeStruct((tq, width), BF),
        ),
        in_specs=[smem] + [vmem] * 4,
        out_specs=(vmem, vmem),
        cost_estimate=pl.CostEstimate(
            flops=2 * tok * (wide + packed) * width,
            transcendentals=0,
            bytes_accessed=tok * (wide + packed + width) * 4,
        ),
        compiler_params=params,
        name="input_back",
    )
    return forward, mix_back, query_back, key_back, input_back


def after(value, *others):
    return lax.optimization_barrier((value,) + others)[0]


def make_body(n_shard, n_ctx, n_tp):
    bits = [1 << i for i in range(n_tp.bit_length() - 1)]
    ctx_steps = [1 << i for i in range(n_ctx.bit_length() - 1)]
    ctx_whole = not n_ctx & (n_ctx - 1)

    def exchange(value, axis, size, bit):
        return lax.ppermute(value, axis, [(i, i ^ bit) for i in range(size) if i ^ bit < size])

    def even_swap(value):
        return exchange(value, "ctx", n_ctx, 1)

    def odd_swap(value):
        pairs = []
        for i in range(1, n_ctx - 1, 2):
            pairs += [(i, i + 1), (i + 1, i)]
        return lax.ppermute(value, "ctx", pairs)

    def swap(value, kind):
        return odd_swap(value) if kind else even_swap(value)

    ctx_count = max(2 * len(ctx_steps) - 1, 1)

    def ctx_step(cur, step, late):
        ci = lax.axis_index("ctx")
        count = len(ctx_steps)
        bit = ctx_steps[step] if step < count else ctx_steps[2 * count - 2 - step]
        up = (ci // bit) % 2
        if step == count - 1:
            cur = cur.astype(BF)
            return (cur.astype(F32) + late(exchange(cur, "ctx", n_ctx, bit)).astype(F32)).astype(BF)
        if step < count:
            half = cur.shape[0] // 2
            send = lax.dynamic_slice_in_dim(cur, (1 - up) * half, half, 0).astype(BF)
            keep = lax.dynamic_slice_in_dim(cur, up * half, half, 0)
            return keep + late(exchange(send, "ctx", n_ctx, bit)).astype(F32)
        other = late(exchange(cur, "ctx", n_ctx, bit))
        return jnp.where(up == 0, jnp.concatenate([cur, other], 0), jnp.concatenate([other, cur], 0))

    def body(
        hidden_in,
        segment_ids,
        qkv_weight,
        qv_bias,
        out_weight,
        out_bias,
        first_gain,
        first_shift,
        inner_weight,
        inner_bias,
        outer_weight,
        outer_bias,
        second_gain,
        second_shift,
        cotangent,
    ):
        rows, tok, width = hidden_in.shape
        part = width // n_shard
        cols = qkv_weight.shape[2]
        heads = cols // HEAD_DIM
        units = inner_weight.shape[1]
        wide = -(-cols // 128) * 128
        pad = wide - cols
        packed = 2 * cols
        half = tok // 2
        every = list(range(rows))
        si = lax.axis_index("shard")
        ci = lax.axis_index("ctx")
        core = lax.axis_index("tp") % 2
        reach = min(n_ctx - 1, 1 + (LONGEST - 2) // tok)
        slots = 2 * reach + 1
        attend_fwd, mix_back, query_back, key_back, input_back = make_attention(
            slots, heads, tok, wide, packed, width
        )

        def rolled(value, axis):
            if n_shard == 2:
                first = lax.slice_in_dim(value, 0, part, axis=axis)
                second = lax.slice_in_dim(value, part, width, axis=axis)
                return jnp.where(si == 0, value, jnp.concatenate([second, first], axis))
            return jnp.roll(value, -si * part, axis)

        def unrolled(value, axis):
            if n_shard == 2:
                return rolled(value, axis)
            return jnp.roll(value, si * part, axis)

        def others(own, axis):
            if n_shard == 2:
                return exchange(own, "shard", 2, 1)
            whole = rolled(lax.all_gather(own, "shard", axis=axis, tiled=True), axis)
            return lax.slice_in_dim(whole, part, width, axis=axis)

        def gathered(own, axis):
            if n_shard == 2:
                return jnp.concatenate([own, exchange(own, "shard", 2, 1)], axis)
            return rolled(lax.all_gather(own, "shard", axis=axis, tiled=True), axis)

        def gathered_in_order(own):
            if n_shard == 2:
                other = exchange(own, "shard", 2, 1)
                return jnp.where(
                    si == 0, jnp.concatenate([own, other], 0), jnp.concatenate([other, own], 0)
                )
            return lax.all_gather(own, "shard", axis=0, tiled=True)

        def own_half(value):
            return lax.dynamic_slice_in_dim(value, core * half, half, 0)

        def core_sum(own, send):
            total = own + exchange(send.astype(BF), "tp", n_tp, 1).astype(F32)
            return total.astype(BF) if len(bits) > 1 else total

        def chip_send(name):
            if len(bits) == 2:
                box["y" + name] = exchange(box[name], "tp", n_tp, bits[1])

        def chip_total(name):
            total = box[name].astype(F32)
            if len(bits) == 2:
                return total + box["y" + name].astype(F32)
            for bit in bits[1:]:
                total = total.astype(BF)
                total = total.astype(F32) + exchange(total, "tp", n_tp, bit).astype(F32)
            return total

        def stage_sum(name, own, send, beside, *names):
            if beside and len(bits) == 2:
                names += ("y" + beside,)
            if names:
                own, send = hold_all([own, send], *names)
            box[name] = core_sum(own, send)
            chip_send(name)

        def both_halves(own):
            return jnp.concatenate([own, exchange(own, "tp", n_tp, 1)], 0)

        def in_order(pair):
            first, second = pair[:half], pair[half:]
            return jnp.where(core == 0, pair, jnp.concatenate([second, first], 0))

        box = {}

        def hold_all(values, *names):
            kept = lax.optimization_barrier(tuple(values) + tuple(box[n] for n in names))
            box.update(zip(names, kept[len(values) :]))
            return kept[: len(values)]

        def hold(value, *names):
            return hold_all([value], *names)[0]

        box["kv_own"] = qkv_weight[:, 1:].astype(BF).reshape(part, packed)
        box["w_kv"] = gathered_in_order(box["kv_own"])
        q_own = jnp.pad(qkv_weight[:, 0].astype(BF), ((0, 0), (0, pad)))
        q_own = hold(q_own, "w_kv")
        w_kv = box["w_kv"]
        w_q = gathered_in_order(q_own)

        before = jnp.full((rows, reach * tok), -1, jnp.int32)
        behind = jnp.full((rows, reach * tok), 1 << 20, jnp.int32)
        padded = jnp.concatenate([before, segment_ids, behind], 1)
        key_seg = lax.dynamic_slice_in_dim(padded, ci * tok, slots * tok, 1)
        q_seg = lax.dynamic_slice_in_dim(segment_ids, ci * tok, tok, 1)
        q_seg = q_seg.reshape(rows, 2, half)
        q_seg = jnp.where(core == 0, q_seg, q_seg[:, ::-1])
        low = jnp.sum(key_seg[:, None, :] < q_seg[:, :, :1], -1) // half
        high = (jnp.sum(key_seg[:, None, :] <= q_seg[:, :, -1:], -1) + half - 1) // half
        begin = jnp.broadcast_to(jnp.stack([core * half, (1 - core) * half])[None], (rows, 2))
        ranges = jnp.stack([low, high, begin], -1).reshape(rows, 6).astype(jnp.int32)
        side = 1 - 2 * (ci % 2)
        places = [jnp.int32(reach) + 0 * side]
        for d in range(1, reach + 1):
            places += [reach + d * side, reach - d * side]
        places = jnp.broadcast_to(jnp.stack(places)[None], (rows, slots))
        numbers = jnp.arange(rows, dtype=jnp.int32)[:, None]
        ranges = jnp.concatenate([ranges, places.astype(jnp.int32), numbers], 1)
        q_seg3 = jnp.tile(q_seg[:, :, None, :], (1, 1, 1, heads))
        key_col = key_seg[:, :, None]

        v_bias = jnp.concatenate([jnp.zeros((cols,), F32), qv_bias[1]])
        q_bias = jnp.pad(qv_bias[0], (0, pad))

        def halo(own):
            found = [own]
            last = [own, own]
            for d in range(1, reach + 1):
                even, odd = even_swap(last[1]), odd_swap(last[0])
                found += [even, odd]
                last = [even, odd]
            return found

        def send_blocks(name, d):
            last = [box[name]] * 2 if d == 1 else [box[f"{name}_{2 * d - 4}"], box[f"{name}_{2 * d - 3}"]]
            box[f"{name}_{2 * d - 2}"] = even_swap(last[1])
            box[f"{name}_{2 * d - 1}"] = odd_swap(last[0])

        def send_kv(r, first):
            for d in range(first, reach + 1):
                send_blocks(f"kv{r}", d)

        for r in every:
            box[f"kv{r}"] = (dot(hidden_in[r], w_kv) + v_bias).astype(BF)
            if r:
                box[f"kv{r}"] = hold(box[f"kv{r}"], f"kv{r - 1}_0", f"kv{r - 1}_1")
            else:
                send_kv(0, 1)
                continue
            send_blocks(f"kv{r}", 1)
        q = [
            ((dot(hidden_in[r], w_q) + q_bias).astype(BF) * jnp.asarray(HEAD_DIM**-0.5, BF))
            for r in every
        ]

        vec_own = [out_bias, first_gain, first_shift, outer_bias, second_gain, second_shift]
        vec_own = jnp.concatenate([v[None] for v in vec_own] + [jnp.zeros((10, part), F32)], 0)
        wo_own = hold(jnp.concatenate([out_weight, vec_own], 0).astype(BF), "kv0")
        wo_vec = gathered(wo_own, 1)
        w_out = jnp.concatenate([jnp.zeros((pad, width), BF), wo_vec[:cols]], 0)
        vectors = wo_vec[cols : cols + 6].astype(F32)
        in_own = hold(inner_weight, "kv0").astype(BF)
        box["w_in"] = others(in_own, 0)
        outer_own = hold(outer_weight, "w_in").astype(BF)
        box["w_outer"] = others(outer_own, 1)
        bo, g1, s1, bd, g2, s2 = [vectors[i] for i in range(6)]

        def normed(summed):
            average = jnp.mean(summed, -1, keepdims=True)
            centered = summed - average
            variance = jnp.mean(centered * centered, -1, keepdims=True)
            scale = lax.rsqrt(variance + EPSILON)
            return centered * scale, scale

        def norm_back(grad, gain, hat, scale):
            inner = grad * gain
            return scale * (
                inner
                - jnp.mean(inner, -1, keepdims=True)
                - hat * jnp.mean(inner * hat, -1, keepdims=True)
            )

        x_roll = [rolled(hidden_in[r], 1) for r in every]
        x_res = [own_half(x_roll[r]).astype(F32) for r in every]
        cots = [rolled(own_half(cotangent[r]), 1).astype(F32) for r in every]

        ready = {0: ["w_in"], rows - 1: ["w_outer"]}

        def before(r, this, last):
            return [f"{this}{r - 1}"] if r else ([f"{last}{rows - 1}"] if last else [])

        o, lse, aug, kv_all = ([None] * rows for _ in range(4))
        for r in every:
            query = hold(q[r], *before(r, "a", None), *ready.get(r, []))
            blocks = [box[f"kv{r}"]] + [box[f"kv{r}_{i}"] for i in range(2 * reach)]
            out = attend_fwd(ranges[r], query, q_seg3[r], key_col[r], *blocks)
            if r < rows - 1:
                out = hold_all(out, f"kv{r + 1}_0", f"kv{r + 1}_1")
                send_kv(r + 1, 2)
            o[r], lse[r], aug[r], kv_all[r] = out
            send = dot(o[r][half:], w_out)
            stage_sum(f"a{r}", dot(o[r][:half], w_out), send, f"a{r - 1}" if r else None)
        q_halo = halo(jnp.concatenate(aug, 0))
        for i, block in enumerate(q_halo[1:]):
            box[f"q{i}"] = block

        hat1, scale1, y1, y1b = [None] * rows, [None] * rows, [None] * rows, [None] * rows
        u, slope = [None] * rows, [None] * rows
        for r in every:
            total = hold(chip_total(f"a{r}"), *before(r, "b", "a"))
            hat1[r], scale1[r] = normed(x_res[r] + total + bo)
            y1[r] = hat1[r] * g1 + s1
            y1b[r] = both_halves(y1[r].astype(BF))
            if not r:
                w_in = jnp.concatenate([in_own, box["w_in"]], 0)
                w_outer = jnp.concatenate([outer_own, box["w_outer"]], 1)
            a = dot(y1b[r], w_in) + inner_bias
            cdf = 0.5 * (1.0 + lax.erf(a * (0.5**0.5)))
            u[r] = (a * cdf).astype(BF)
            slope[r] = (cdf + a * jnp.exp(-0.5 * a * a) * 0.3989422804014327).astype(BF)
            send = dot(u[r][half:], w_outer)
            arrived = ["q0", "q1"] if r == rows - 1 else []
            stage_sum(f"b{r}", dot(u[r][:half], w_outer), send, f"b{r - 1}" if r else f"a{rows - 1}", *arrived)

        result, dh2, d2b, dab = ([None] * rows for _ in range(4))
        d_vec2, d_bi = [None] * rows, [None] * rows
        for r in every:
            total = hold(chip_total(f"b{r}"), *before(r, "c", "b"))
            hat2, scale2 = normed(y1[r] + total + bd)
            c = cots[r]
            result[r] = (hat2 * g2 + s2).astype(BF)
            dh2[r] = norm_back(c, g2, hat2, scale2)
            d2b[r] = both_halves(dh2[r].astype(BF))
            d_vec2[r] = [jnp.sum(v, 0, keepdims=True) for v in (dh2[r], c * hat2, c)]
            da = dot_nt(d2b[r], w_outer) * slope[r].astype(F32)
            d_bi[r] = jnp.sum(da, 0, keepdims=True)
            dab[r] = da.astype(BF)
            send = dot_nt(dab[r][half:], w_in)
            arrived = [f"q{i}" for i in range(2, 2 * reach)] if r == rows - 1 else []
            stage_sum(f"c{r}", dot_nt(dab[r][:half], w_in), send, f"c{r - 1}" if r else f"b{rows - 1}", *arrived)

        def over_rows(terms):
            return functools.reduce(lambda p, q: p + q, terms)

        def shard_send(name, send):
            box[name] = exchange(send, "shard", 2, 1) if n_shard == 2 else send

        def shard_total(name, own, axis):
            if n_shard == 2:
                return own + box[name].astype(F32)
            whole = unrolled(jnp.concatenate([own, box[name].astype(F32)], axis), axis)
            return lax.psum_scatter(whole, "shard", scatter_dimension=axis, tiled=True)

        def advance(name, *names):
            value, step = box[name], at_step.get(name, 0)
            if ctx_whole and step < ctx_count:
                box[name] = ctx_step(value, step, lambda got: hold(got, *names) if names else got)
            elif not step:
                box[name] = lax.psum(value, "ctx")
            at_step[name] = step + 1

        def finish(name):
            while at_step.get(name, 0) < ctx_count:
                advance(name)
            return box[name].astype(F32)

        at_step = {}

        dh1, d1b, d_vec1, dos, deltas = ([None] * rows for _ in range(5))

        def stage4(r, *names):
            total = hold(chip_total(f"c{r}"), *names)
            dy1 = dh2[r] + total
            dh1[r] = norm_back(dy1, g1, hat1[r], scale1[r])
            d1b[r] = both_halves(dh1[r].astype(BF))
            d_vec1[r] = [jnp.sum(v, 0, keepdims=True) for v in (dh1[r], dy1 * hat1[r], dy1)]
            box[f"do{r}"], deltas[r] = mix_back(ranges[r], d1b[r], w_out, o[r])

        gate = [f"c{rows - 1}"]
        for r in every:
            stage4(r, *gate)
            if r:
                box[f"do{r}"] = hold(box[f"do{r}"], *[f"do{r - 1}_{i}" for i in range(2, 2 * reach)])
            send_blocks(f"do{r}", 1)
            gate = [f"do{r}"]
            if not r:
                lefts = [hold(u[0], "do0")] + u[1:]
                own_first, send_first = weight_grads(
                    [(lefts, d2b), (dab, y1b)], part, [(0, units), (0, units)]
                )
                box["send_first"] = send_first
                names = ["do0_0", "do0_1"] + ([f"yc{rows - 1}"] if len(bits) == 2 else [])
                own_first, box["send_first"] = hold_all([own_first, send_first], *names)
                shard_send("x_first", box["send_first"])
                gate = ["send_first"]
            elif r < rows - 1:
                box[f"do{r}"] = hold(box[f"do{r}"], f"do{r}_0", f"do{r}_1")
            if r < rows - 1:
                for d in range(2, reach + 1):
                    send_blocks(f"do{r}", d)

        dqs, biases, dkvs, d_bv = ([None] * rows for _ in range(4))
        for r in every:
            query = hold(aug[r], f"dq{r - 1}" if r else f"do{rows - 1}")
            dq, biases[r] = query_back(
                ranges[r], query, q_seg3[r], key_col[r], box[f"do{r}"], lse[r], deltas[r], kv_all[r]
            )
            if not r:
                names = [f"do{rows - 1}_0", f"do{rows - 1}_1", "x_first"]
            else:
                names = [f"do{rows - 1}_{j}" for j in range(2, 2 * reach)] + ["first"] if r == rows - 1 else []
            box[f"dq{r}"] = hold(dq, *names)
            if not r:
                for d in range(2, reach + 1):
                    send_blocks(f"do{rows - 1}", d)
                box["first"] = shard_total("x_first", own_first, 1)
                advance("first")
        dqs = [box[f"dq{r}"] for r in every]
        own_mix, box["send_mix"] = weight_grads(
            [(o, d1b), (dqs, x_roll)], part, [(pad, wide), (0, cols)]
        )
        shard_send("x_mix", box["send_mix"])
        advance("first")
        for r in every:
            own = hold(box[f"kv{r}"], *(["send_mix"] if not r else [f"dkv{r - 1}"]))
            blocks = [box[f"do{r}"]] + [box[f"do{r}_{i}"] for i in range(2 * reach)]
            q_blocks = q_halo[:1] + [box[f"q{i}"] for i in range(2 * reach)]
            dkv, d_bv[r] = key_back(ranges[r], own, q_seg3[r], key_col[r], *q_blocks, *blocks)
            box[f"dkv{r}"] = hold(dkv, *(["x_mix"] if not r else ["mix"] if r == 1 else []))
            if not r:
                box["mix"] = shard_total("x_mix", own_mix, 1)
                advance("mix")
        dkvs = [box[f"dkv{r}"] for r in every]
        for r in every:
            own, send = input_back(ranges[r], dqs[r], dkvs[r], w_q, w_kv)
            if r == rows - 1:
                own, send = hold_all([own, send], "first")
            box[f"h{r}"] = core_sum(own, send)
            chip_send(f"h{r}")

        def finish_outputs():
            mine = hold(jnp.stack([unrolled(result[r], 1) for r in every]), "h0")
            theirs = exchange(mine, "tp", n_tp, 1)
            outputs = jnp.where(
                core == 0, jnp.concatenate([mine, theirs], 1), jnp.concatenate([theirs, mine], 1)
            )
            box["outputs"] = outputs

        def finish_first():
            total = finish("first")
            return total[units:].T, total[:units]

        def finish_hidden():
            hidden_grads = []
            for r in every:
                total = chip_total(f"h{r}")
                grad = (unrolled(dh1[r], 1) + total).astype(BF)
                hidden_grads.append(in_order(both_halves(grad)))
            box["hidden"] = jnp.stack(hidden_grads)

        d_vec = jnp.concatenate(
            [over_rows(v) for v in zip(*d_vec1)]
            + [over_rows(v) for v in zip(*d_vec2)]
            + [jnp.zeros((2, width), F32)],
            0,
        )
        d_vec = d_vec + exchange(d_vec, "tp", n_tp, 1)
        if n_shard == 2 and ctx_whole and part == packed and units % packed == 0:
            lines = 8 + units // packed + 1
            lines += (-(packed + lines)) % (16 * n_ctx)
            own_last, send_last = last_grads(dkvs, x_roll, d_vec, d_bi, biases, d_bv, part, lines)
            shard_send("x_last", send_last)
            box["last"] = shard_total("x_last", own_last, 1)
            advance("last")
            advance("mix", "last")
            box["first"] = hold(box["first"], "last")
            finish_outputs()
            advance("last", "outputs")
            finish_hidden()
            box["grad_in"], box["grad_outer"] = finish_first()
            advance("last", "hidden", "grad_in", "grad_outer")
            g_last = finish("last")
            vec = g_last[packed : packed + 6]
            d_units = g_last[packed + 8 : packed + 8 + units // packed].reshape(units)
            d_qv = g_last[packed + 8 + units // packed].reshape(2, cols)
        else:
            own_last, send_last = weight_grads([(dkvs, x_roll)], part, [(0, packed)])
            d_qv = jnp.concatenate([over_rows(biases)[:, :cols], over_rows(d_bv)[:, cols:]], 1)
            vec = lax.psum_scatter(unrolled(d_vec, 1), "shard", scatter_dimension=1, tiled=True)
            vec = lax.psum(vec, "ctx")
            d_units = lax.psum(over_rows(d_bi)[0], ("shard", "ctx"))
            d_qv = lax.psum(d_qv[0], ("shard", "ctx")).reshape(2, cols)
            shard_send("x_last", send_last)
            box["last"] = shard_total("x_last", own_last, 1)
            g_last = finish("last")
            finish_outputs()
            finish_hidden()
            box["grad_in"], box["grad_outer"] = finish_first()
        g_mix = finish("mix")
        grad_qkv = jnp.concatenate([g_mix[cols:], g_last[:packed]], 0).T.reshape(part, 3, cols)

        return (
            box["outputs"],
            box["hidden"],
            grad_qkv,
            d_qv,
            g_mix[:cols],
            vec[0],
            vec[1],
            vec[2],
            box["grad_in"],
            d_units,
            box["grad_outer"],
            vec[3],
            vec[4],
            vec[5],
        )

    return body


def solution(mesh):
    body = make_body(mesh.shape["shard"], mesh.shape["ctx"], mesh.shape["tp"])
    in_specs = (
        P("shard", "ctx", None),
        P("shard", None),
        P("shard", None, "tp"),
        P(None, "tp"),
        P("tp", "shard"),
        P("shard"),
        P("shard"),
        P("shard"),
        P("shard", "tp"),
        P("tp"),
        P("tp", "shard"),
        P("shard"),
        P("shard"),
        P("shard"),
        P("shard", "ctx", None),
    )
    out_specs = (
        P("shard", "ctx", None),
        P("shard", "ctx", None),
        P("shard", None, "tp"),
        P(None, "tp"),
        P("tp", "shard"),
        P("shard"),
        P("shard"),
        P("shard"),
        P("shard", "tp"),
        P("tp"),
        P("tp", "shard"),
        P("shard"),
        P("shard"),
        P("shard"),
    )
    return jax.shard_map(body, mesh=mesh, in_specs=in_specs, out_specs=out_specs, check_vma=False)
```
